32 devices in a mesh: group: 2 (over x), tile: 4 (over y, core), orient: 4 (over z).
Axes of the slice: x: 2, y: 2, z: 4, core: 2. Of those that a mesh axis runs over, the one named last changes fastest.
Arguments:
- micrograph: float32 [768, 1024], P('group', 'tile'), parts along dimension 0, may hold values from -30 to 30
- templates: float32 [4, 4, 128, 128], P('orient', 'tile'), may hold values from 0 to 0.0107421875
- orient_ids: int32 [4, 4], P('orient', 'tile'), may hold values from 0 to 15, as said below
- log_weight: float32 [16], replicated, may hold values from -2 to 2
- ice_mask: int32 [32, 64], P('group', 'tile'), parts along dimension 0, may hold values 0 or 1
Outputs:
- score_map: float32 [512, 1024], P(('group', 'orient'), 'tile'), parts along dimension 0
The draws below stay inside these ranges and needn't reach their ends.
There are 2 independent parts, one for each index of `group`. The reference program is written for one: setup_inputs(seed, part) draws one part's arguments, and reference() takes and returns one part's arrays. A program takes and returns all parts, laid end to end along the dimension named above; an argument that names none is the same for every part. Nothing has to cross between parts.
Inputs may be any that keep to these rules, and one draw needn't show every extreme that they name: `orient_ids`: every slot holds a different orientation.
All inputs are finite; a program needn't handle non-finite values. No bound on the sum of `ice_mask` on one device may be relied on, other than what follows from the above.
Results may differ from the reference program's by a relative error of at most 0.00024.
Values sent between devices are 32-bit elements; how exact they have to be, the bound alone decides.
A program may use at most 64 MiB of HBM per device.

```python
import jax
import jax.numpy as jnp
from jax import lax

TILE = 256
GUARD = 64
TPL = 128
MBLK = 16
EXT = 384
ORI_CYCLE = 4
ORI_BLOCKS = 4
ORIENTS = 16
WIDTH = 1024
N_TILE = 4


def bright_patches(third_key, fourth_key):
    row_starts = jax.random.randint(third_key, (3,), 0, min(TILE, EXT - TPL + 1))
    col_starts = jax.random.randint(fourth_key, (3,), 0, WIDTH - TPL + 1)
    row_grid = jnp.arange(EXT, dtype=jnp.int32)[:, None]
    col_grid = jnp.arange(WIDTH, dtype=jnp.int32)[None, :]
    strengths = jnp.array([120.0, 200.0, 300.0], jnp.float32) / (0.75 * TPL)
    bright = jnp.zeros((EXT, WIDTH), jnp.float32)
    for which in range(3):
        inside = (row_grid >= row_starts[which]) & (row_grid < row_starts[which] + TPL)
        inside = inside & (col_grid >= col_starts[which]) & (col_grid < col_starts[which] + TPL)
        bright = bright + jnp.where(inside, strengths[which], 0.0)
    return bright


def draw_micrograph(key, part):
    first_key, second_key, third_key, fourth_key = jax.random.split(key, 4)
    columns = jnp.arange(WIDTH, dtype=jnp.float32)
    ramp = 1.0 + 2.0 * columns[None, :] / max(WIDTH - 1, 1)
    rough = jax.random.uniform(second_key, (EXT, WIDTH), jnp.float32, 0.6, 1.6)
    bright = bright_patches(third_key, fourth_key)
    base = jnp.clip(jax.random.normal(first_key, (EXT, WIDTH), jnp.float32), -4.0, 4.0)
    field = base * ramp * rough + bright
    return jnp.clip(field, -30.0, 30.0)


def draw_templates(key, part):
    first_key, second_key = jax.random.split(key)
    scales = jax.random.uniform(first_key, (ORI_BLOCKS, ORI_CYCLE, 1, 1), jnp.float32, 0.9, 1.1)
    values = jax.random.uniform(second_key, (ORI_BLOCKS, ORI_CYCLE, TPL, TPL), jnp.float32, 0.0, 1.0)
    return scales * (0.25 + values) / TPL


def draw_orient_ids(key, part):
    order = jax.random.permutation(key, jnp.arange(ORIENTS, dtype=jnp.int32))
    return order.reshape(ORI_BLOCKS, ORI_CYCLE).astype(jnp.int32)


def set_ends(result, rng, least, top_value):
    place = [jax.random.randint(jax.random.fold_in(rng, axis), (), 0, length) for axis, length in enumerate(result.shape)]
    widest = result.shape.index(max(result.shape))
    neighbour = place[:widest] + [(place[widest] + 1) % result.shape[widest]] + place[widest + 1:]
    return result.at[tuple(place)].set(least).at[tuple(neighbour)].set(top_value)


def setup_inputs(seed: int = 0, part: int = 0) -> dict:
    seeds = jax.random.split(jax.random.key(seed), 6)
    part_keys = jax.random.split(jax.random.fold_in(seeds[5], part), 6)
    micrograph = draw_micrograph(jax.random.fold_in(jax.random.fold_in(seeds[5], part), 71), part)
    templates = draw_templates(jax.random.fold_in(seeds[5], 71), part)
    orient_ids = draw_orient_ids(jax.random.fold_in(seeds[5], 71), part)
    log_weight = jnp.clip(jax.random.uniform(seeds[3], (ORIENTS,), jnp.float32, -2.0, 2.0), -2.0, 2.0)
    ice_mask = set_ends((jax.random.randint(part_keys[4], (TILE // MBLK, WIDTH // MBLK), 0, 4) < 1).astype(jnp.int32), jax.random.fold_in(part_keys[4], 1), 0, 1)
    return dict(micrograph=micrograph, templates=templates, orient_ids=orient_ids, log_weight=log_weight, ice_mask=ice_mask)


def reference(micrograph, templates, orient_ids, log_weight, ice_mask):
    padded = jnp.pad(micrograph, ((0, 0), (GUARD, GUARD)))
    flat_templates = templates.reshape(ORIENTS, TPL, TPL)
    template_spec = jnp.fft.rfft2(flat_templates, s=(EXT, EXT))
    weights = log_weight[orient_ids.reshape(-1)]

    def one_tile(tile_index):
        window = lax.dynamic_slice_in_dim(padded, tile_index * TILE, EXT, 1)
        window_spec = jnp.fft.rfft2(window)
        correlation = jnp.fft.irfft2(window_spec[None] * jnp.conj(template_spec), s=(EXT, EXT))[:, :TILE, :TILE]
        scores = correlation + weights[:, None, None]
        return jax.scipy.special.logsumexp(scores, axis=0)
    per_tile = lax.map(one_tile, jnp.arange(N_TILE, dtype=jnp.int32))
    log_total = jnp.transpose(per_tile, (1, 0, 2)).reshape(TILE, WIDTH)
    blocks = jnp.repeat(jnp.repeat(ice_mask, MBLK, axis=0), MBLK, axis=1)
    unmasked = 1.0 - blocks.astype(jnp.float32)
    live_count = jnp.sum(unmasked)
    average = jnp.sum(unmasked * log_total) / live_count
    variance = jnp.sum(unmasked * (log_total - average) ** 2) / live_count
    return unmasked * (log_total - average) / jnp.sqrt(variance + 1e-05)
```

```python
import functools
import math

import jax
import jax.numpy as jnp
import numpy as np
from jax import lax
from jax.experimental import pallas as pl
from jax.experimental.pallas import tpu as pltpu
from jax.sharding import PartitionSpec as P

MBLK = 16
F32 = jnp.float32
BF16 = jnp.bfloat16
MESH = pl.DeviceIdType.MESH


def halves(table, axis=0):
    table = table.astype(np.float32)
    high = table.astype(jnp.bfloat16)
    low = (table - high.astype(np.float32)).astype(jnp.bfloat16)
    return np.concatenate([high, low], axis=axis)


def tables(patch):
    length = 2 * patch
    n = np.arange(length)[:, None]
    k = np.arange(patch)[None, :]
    theta = 2 * math.pi * ((n * (2 * k + 1)) % (2 * length)) / (2 * length)
    tx = np.concatenate([np.cos(theta), -np.sin(theta)], axis=1)
    back = theta[:patch].T
    ix = np.concatenate([np.cos(back), -np.sin(back)], axis=0) * (2.0 / length)
    m = np.arange(length)
    phi = 2 * math.pi * ((m[:, None] * m[None, :]) % length) / length
    c, s = np.cos(phi), np.sin(phi)
    ty = np.block([[c, s], [-s, c]])
    cp, sp = c[:, :patch], s[:, :patch]
    tt = np.block([[cp, sp], [-sp, cp]])
    ci, si = c[:patch], s[:patch]
    iy = np.block([[ci, -si], [si, ci]]) / length
    return halves(tx), halves(ix, 1), halves(ty), halves(tt), halves(iy)


def split(value):
    high = value.astype(BF16)
    low = (value - high.astype(F32)).astype(BF16)
    return high, low


def dot(a, b):
    return jnp.dot(a, b, preferred_element_type=F32)


def left_table(table, high, low):
    rows = table.shape[0] // 2
    both = dot(table[...], high)
    return both[:rows] + both[rows:] + dot(table[:rows, :], low)


def right_table(value, table):
    depth = table.shape[0] // 2
    high, low = split(value)
    return dot(jnp.concatenate([high, high], axis=1), table[...]) + dot(low, table[:depth, :])


def right_wide(value, table):
    width = table.shape[1] // 2
    high, low = split(value)
    both = dot(high, table[...])
    return both[:, :width] + both[:, width:] + dot(low, table[:, :width])


def kernel(
    tiles, orients, guard,
    mic_any, tpl_any, ids_any, logw_any, mask_any, tx_any, ix_any, ty_any, tt_any, iy_any,
    out,
    mic, ids, logw, mask, tx, ix, ty, tt, iy, pack, halo,
    stack, ext, img, spec, scores, lse_out, lse_in, stats,
    load_sem,
    halo_send, halo_recv, tpl_send, tpl_recv, lse_send, lse_recv, st_send, st_recv,
):
    t = lax.axis_index("tile")
    o = lax.axis_index("orient")
    everyone = tiles * orients
    extent, side = mic.shape
    patch = tpl_any.shape[2]
    length = 2 * patch
    blocks = side // patch
    share = out.shape[0]
    unrolled = everyone <= 16

    def partner(k):
        if tiles & (tiles - 1):
            return lax.rem(t + k, tiles)
        bit, peer = 1, 0
        while bit < tiles:
            peer = peer + lax.rem(t // bit + k // bit, 2) * bit
            bit *= 2
        return peer

    def seat_of(k):
        return {"tile": partner(k // orients), "orient": lax.rem(o + k % orients, orients)}

    def each_peer(body):
        if unrolled:
            for k in range(everyone - 1, 0, -1):
                body(k)
        else:
            def step(k, carry):
                body(k)
                return carry

            lax.fori_loop(1, everyone, step, 0)

    barrier = pltpu.get_barrier_semaphore()

    def greet(k):
        pl.semaphore_signal(barrier, inc=1, device_id=seat_of(k), device_id_type=MESH)

    each_peer(greet)

    sources = (
        ("tpl", tpl_any.at[0, 0], stack.at[0, pl.ds(0, patch)]),
        ("mic", mic_any, mic),
        ("ids", ids_any, ids),
        ("logw", logw_any, logw),
        ("tx", tx_any, tx),
        ("tt", tt_any, tt),
        ("ty", ty_any, ty),
        ("iy", iy_any, iy),
        ("ix", ix_any, ix),
        ("mask", mask_any, mask),
    )
    loads = {}
    for index, (name, source, target) in enumerate(sources):
        loads[name] = pltpu.make_async_copy(source, target, load_sem.at[index])
        loads[name].start()

    loads["ids"].wait()
    loads["logw"].wait()
    known = lax.broadcasted_iota(jnp.int32, (1, logw.shape[1]), 1) == ids[...]
    weight_here = jnp.sum(jnp.where(known, logw[...], 0.0), axis=1, keepdims=True)
    stack[0, patch:, :] = jnp.broadcast_to(weight_here, (stack.shape[1] - patch, patch))

    loads["mic"].wait()
    middle = extent // 2
    lane_half = lax.broadcasted_iota(jnp.int32, (middle, patch), 1) < guard
    outer, inner = mic[:, side - patch:], mic[:, :patch]
    pack[1] = jnp.where(lane_half, pltpu.roll(outer[:middle], guard, 1), outer[middle:])
    pack[0] = jnp.where(lane_half, inner[:middle], pltpu.roll(inner[middle:], guard, 1))
    loads["tpl"].wait()

    pl.semaphore_wait(barrier, everyone - 1)

    def halo_copy(place, peer):
        return pltpu.make_async_remote_copy(
            src_ref=pack.at[place], dst_ref=halo.at[1 - place], send_sem=halo_send.at[place],
            recv_sem=halo_recv.at[1 - place], device_id={"tile": peer}, device_id_type=MESH,
        )

    to_left = halo_copy(0, lax.rem(t + tiles - 1, tiles))
    to_right = halo_copy(1, lax.rem(t + 1, tiles))

    def tpl_copy(k):
        return pltpu.make_async_remote_copy(
            src_ref=stack.at[0], dst_ref=stack.at[k], send_sem=tpl_send.at[k],
            recv_sem=tpl_recv.at[k], device_id={"tile": partner(k)}, device_id_type=MESH,
        )

    @pl.when(t > 0)
    def _():
        to_left.start()

    @pl.when(t < tiles - 1)
    def _():
        to_right.start()

    for k in range(1, tiles):
        tpl_copy(k).start()

    loads["tx"].wait()
    loads["tt"].wait()

    def spectra(first, many):
        value = stack[pl.ds(first, many), :patch, :].reshape(many * patch, patch)
        high, low = split(value)
        top = tx[:patch, :]
        half = dot(jnp.concatenate([high, low], axis=1), jnp.concatenate([top, top], axis=0))
        half = half + dot(high, tx[length:length + patch, :])
        high, low = split(half)

        def stacked(part):
            return jnp.concatenate(
                [
                    jnp.concatenate(
                        [part[j * patch:(j + 1) * patch, :patch], part[j * patch:(j + 1) * patch, patch:]],
                        axis=0,
                    )
                    for j in range(many)
                ],
                axis=1,
            )

        whole = left_table(tt, stacked(high), stacked(low))
        for j in range(many):
            spec[first + j] = whole[:, j * patch:(j + 1) * patch]

    spectra(0, 1)

    rolled = [pltpu.roll(mic[:, b * patch:(b + 1) * patch], guard, 1) for b in range(blocks)]
    lane = lax.broadcasted_iota(jnp.int32, (extent, patch), 1)
    ext[0] = rolled[0]
    for b in range(1, blocks):
        ext[b] = jnp.where(lane < guard, rolled[b - 1], rolled[b])
    ext[blocks] = rolled[blocks - 1]

    loads["mask"].wait()
    mask_rows, mask_cols = mask.shape
    row_id = lax.broadcasted_iota(jnp.int32, (share, mask_rows), 0) + o * share
    pick = lax.broadcasted_iota(jnp.int32, (share, mask_rows), 1)
    low_edge = pick * MBLK
    rows_of = jnp.where((row_id >= low_edge) & (row_id < low_edge + MBLK), 1.0, 0.0).astype(F32)
    col_id = lax.broadcasted_iota(jnp.int32, (mask_cols, side), 1)
    col_edge = lax.broadcasted_iota(jnp.int32, (mask_cols, side), 0) * MBLK
    cols_of = jnp.where((col_id >= col_edge) & (col_id < col_edge + MBLK), 1.0, 0.0).astype(F32)
    unmasked = 1.0 - dot(dot(rows_of, mask[...].astype(F32)), cols_of)

    def whole_sum(value):
        return jnp.sum(jnp.sum(value, axis=0, keepdims=True), axis=1, keepdims=True)

    count = whole_sum(unmasked)

    def receive(place):
        present = (t > 0) if place == 0 else (t < tiles - 1)

        @pl.when(present)
        def _():
            halo_copy(1 - place, t).wait_recv()

        @pl.when(jnp.logical_not(present))
        def _():
            halo[place] = jnp.zeros(halo.shape[1:], F32)

        got = halo[place]
        turned = pltpu.roll(got, guard, 1)
        near = lax.broadcasted_iota(jnp.int32, (middle, patch), 1) < guard
        edge = 0 if place == 0 else blocks
        if place == 0:
            ext[edge, :middle] = jnp.where(near, got, ext[edge, :middle])
            ext[edge, middle:] = jnp.where(near, turned, ext[edge, middle:])
        else:
            ext[edge, :middle] = jnp.where(near, ext[edge, :middle], turned)
            ext[edge, middle:] = jnp.where(near, ext[edge, middle:], got)

    odd = lax.rem(t, 2) == 1
    early = 1 - lax.rem(t, 2)

    @pl.when(odd)
    def _():
        receive(0)

    @pl.when(jnp.logical_not(odd))
    def _():
        receive(1)

    def image(b):
        half = right_table(jnp.concatenate([ext[b], ext[b + 1]], axis=1), tx)
        high, low = split(half)

        def stacked(part):
            return jnp.concatenate(
                [
                    jnp.concatenate(
                        [part[a * patch:a * patch + length, :patch], part[a * patch:a * patch + length, patch:]],
                        axis=0,
                    )
                    for a in range(blocks)
                ],
                axis=1,
            )

        whole = left_table(ty, stacked(high), stacked(low))
        for a in range(blocks):
            img[b, a] = whole[:, a * patch:(a + 1) * patch]

    loads["ty"].wait()
    image(early)

    tpl_copy(1).wait_recv()
    spectra(1, 1)

    loads["ix"].wait()
    loads["iy"].wait()

    def correlate(items):
        highs, lows = [], []
        for k, a, b in items:
            sr, si = spec[k, :length], spec[k, length:]
            ir, ii = img[b, a, :length], img[b, a, length:]
            cross = jnp.concatenate([ir * sr + ii * si, ii * sr - ir * si], axis=0)
            high, low = split(cross)
            highs.append(high)
            lows.append(low)
        mid = left_table(iy, jnp.concatenate(highs, axis=1), jnp.concatenate(lows, axis=1))
        pieces = jnp.concatenate(
            [
                jnp.concatenate(
                    [mid[:patch, i * patch:(i + 1) * patch], mid[patch:, i * patch:(i + 1) * patch]],
                    axis=1,
                )
                for i in range(len(items))
            ],
            axis=0,
        )
        final = right_wide(pieces, ix)
        for i, (k, a, b) in enumerate(items):
            scores[k, a, b] = final[i * patch:(i + 1) * patch] + stack[k, patch:, :][:1, :1]

    correlate([(k, a, early) for k in range(2) for a in range(blocks)])

    @pl.when(odd)
    def _():
        receive(1)

    @pl.when(jnp.logical_not(odd))
    def _():
        receive(0)

    image(1 - early)
    correlate([(k, a, 1 - early) for k in range(2) for a in range(blocks)])

    for k in range(2, tiles):
        tpl_copy(k).wait_recv()

    def pairs(body):
        if tiles == 4:
            body(2)
        elif tiles > 4:
            def step(p, carry):
                body(2 * p)
                return carry

            lax.fori_loop(1, tiles // 2, step, 0)

    pairs(lambda k: spectra(k, 2))

    def own_lse(a, place):
        rows = pl.ds(pl.multiple_of(place * share, share), share)
        parts = []
        for b in range(blocks):
            top = scores[0, a, b, rows, :]
            for k in range(1, tiles):
                top = jnp.maximum(top, scores[k, a, b, rows, :])
            total = jnp.exp(scores[0, a, b, rows, :] - top)
            for k in range(1, tiles):
                total = total + jnp.exp(scores[k, a, b, rows, :] - top)
            parts.append(top + jnp.log(total))
        return jnp.concatenate(parts, axis=1)

    def lse_copy(k):
        return pltpu.make_async_remote_copy(
            src_ref=lse_out.at[k], dst_ref=lse_in.at[k], send_sem=lse_send.at[k],
            recv_sem=lse_recv.at[k], device_id={"orient": lax.rem(o + k, orients)},
            device_id_type=MESH,
        )

    owners = patch // share
    home, seat = o // owners, lax.rem(o, owners)

    def send_rows(a, place):
        ahead = lax.rem(a * owners + place - o + orients, orients)
        lse_out[ahead] = own_lse(a, place)
        lse_copy(ahead).start()

    for s in range(blocks):
        a = lax.rem(home + 1 + s, blocks)
        pairs(lambda k: correlate([(k + j, a, b) for j in range(2) for b in range(blocks)]))
        if s < blocks - 1:
            for place in range(owners):
                send_rows(a, place)
        else:
            for gap in range(1, owners):
                send_rows(a, lax.rem(seat + gap, owners))
    mine = own_lse(home, seat)
    for k in range(1, orients):
        lse_copy(k).wait_recv()
    top = mine
    for k in range(1, orients):
        top = jnp.maximum(top, lse_in[k])
    total = jnp.exp(mine - top)
    for k in range(1, orients):
        total = total + jnp.exp(lse_in[k] - top)
    lse = top + jnp.log(total)

    sum_here = whole_sum(unmasked * lse)
    mean_here = sum_here / jnp.maximum(count, 1.0)
    deviation = lse - mean_here
    squares = whole_sum(unmasked * deviation * deviation)
    slot = lax.broadcasted_iota(jnp.int32, stats.shape[1:], 1)
    stats[0] = jnp.where(
        slot == 0, count, jnp.where(slot == 1, sum_here, jnp.where(slot == 2, squares, 0.0))
    )

    def st_copy(k):
        return pltpu.make_async_remote_copy(
            src_ref=stats.at[0], dst_ref=stats.at[k], send_sem=st_send.at[k],
            recv_sem=st_recv.at[k], device_id=seat_of(k), device_id_type=MESH,
        )

    each_peer(lambda k: st_copy(k).start())

    @pl.when(t > 0)
    def _():
        to_left.wait_send()

    @pl.when(t < tiles - 1)
    def _():
        to_right.wait_send()

    for k in range(1, tiles):
        tpl_copy(k).wait_send()
    for k in range(1, orients):
        lse_copy(k).wait_send()
    each_peer(lambda k: st_copy(k).wait())
    table = stats[:, 0, :]
    counts, sums, sqs = table[:, 0:1], table[:, 1:2], table[:, 2:3]
    live = jnp.sum(counts, axis=0, keepdims=True)
    average = jnp.sum(sums, axis=0, keepdims=True) / live
    gap = sums / jnp.maximum(counts, 1.0) - average
    variance = jnp.sum(sqs + counts * gap * gap, axis=0, keepdims=True) / live
    out[...] = unmasked * (lse - average) / jnp.sqrt(variance + 1e-05)


def body(tiles, orients, micrograph, templates, orient_ids, log_weight, ice_mask):
    extent, side = micrograph.shape
    patch = templates.shape[2]
    share = side // orients
    blocks = side // patch
    everyone = tiles * orients
    anywhere = pl.BlockSpec(memory_space=pl.ANY)
    vmem = pltpu.VMEM
    dma = pltpu.SemaphoreType.DMA
    consts = [jnp.asarray(table) for table in tables(patch)]
    return pl.pallas_call(
        functools.partial(kernel, tiles, orients, patch // 2),
        out_shape=jax.ShapeDtypeStruct((share, side), F32),
        in_specs=[anywhere] * (5 + len(consts)),
        out_specs=pl.BlockSpec(memory_space=pltpu.VMEM),
        scratch_shapes=[
            vmem((extent, side), F32),
            vmem(orient_ids.shape, jnp.int32),
            vmem((1, log_weight.shape[0]), F32),
            vmem(ice_mask.shape, jnp.int32),
            *[vmem(table.shape, BF16) for table in consts],
            vmem((2, extent // 2, patch), F32),
            vmem((2, extent // 2, patch), F32),
            vmem((tiles, patch + 8, patch), F32),
            vmem((blocks + 1, extent, patch), F32),
            vmem((blocks, blocks, 4 * patch, patch), F32),
            vmem((tiles, 4 * patch, patch), F32),
            vmem((tiles, blocks, blocks, patch, patch), F32),
            vmem((orients, share, side), F32),
            vmem((orients, share, side), F32),
            vmem((everyone, 1, 128), F32),
            dma((5 + len(consts),)),
            dma((2,)), dma((2,)),
            dma((tiles,)), dma((tiles,)),
            dma((orients,)), dma((orients,)),
            dma((everyone,)), dma((everyone,)),
        ],
        compiler_params=pltpu.CompilerParams(
            collective_id=0, has_side_effects=True, vmem_limit_bytes=56 * 1024 * 1024
        ),
    )(micrograph, templates, orient_ids, log_weight.reshape(1, -1), ice_mask, *consts)


def solution(mesh):
    return jax.shard_map(
        functools.partial(body, mesh.shape["tile"], mesh.shape["orient"]),
        mesh=mesh,
        in_specs=(
            P("group", "tile"),
            P("orient", "tile", None, None),
            P("orient", "tile"),
            P(),
            P("group", "tile"),
        ),
        out_specs=P(("group", "orient"), "tile"),
        check_vma=False,
    )
```

```python
import functools
import math

import jax
import jax.numpy as jnp
import numpy as np
from jax import lax
from jax.experimental import pallas as pl
from jax.experimental.pallas import tpu as pltpu
from jax.sharding import PartitionSpec as P

MBLK = 16
F32 = jnp.float32
BF16 = jnp.bfloat16
MESH = pl.DeviceIdType.MESH


def halves(table, axis=0):
    table = table.astype(np.float32)
    high = table.astype(jnp.bfloat16)
    low = (table - high.astype(np.float32)).astype(jnp.bfloat16)
    return np.concatenate([high, low], axis=axis)


def tables(patch):
    length = 2 * patch
    n = np.arange(length)[:, None]
    k = np.arange(patch)[None, :]
    theta = 2 * math.pi * ((n * (2 * k + 1)) % (2 * length)) / (2 * length)
    tx = np.concatenate([np.cos(theta), -np.sin(theta)], axis=1)
    back = theta[:patch].T
    ix = np.concatenate([np.cos(back), -np.sin(back)], axis=0) * (2.0 / length)
    m = np.arange(length)
    phi = 2 * math.pi * ((m[:, None] * m[None, :]) % length) / length
    c, s = np.cos(phi), np.sin(phi)
    ty = np.block([[c, s], [-s, c]])
    cp, sp = c[:, :patch], s[:, :patch]
    tt = np.block([[cp, sp], [-sp, cp]])
    ci, si = c[:patch], s[:patch]
    iy = np.block([[ci, -si], [si, ci]]) / length
    return halves(tx), halves(ix, 1), halves(ty), halves(tt), halves(iy)


def split(value):
    high = value.astype(BF16)
    low = (value - high.astype(F32)).astype(BF16)
    return high, low


def dot(a, b):
    return jnp.dot(a, b, preferred_element_type=F32)


def left_table(table, high, low):
    rows = table.shape[0] // 2
    both = dot(table[...], high)
    return both[:rows] + both[rows:] + dot(table[:rows, :], low)


def right_table(value, table):
    depth = table.shape[0] // 2
    high, low = split(value)
    return dot(jnp.concatenate([high, high], axis=1), table[...]) + dot(low, table[:depth, :])


def right_wide(value, table):
    width = table.shape[1] // 2
    high, low = split(value)
    both = dot(high, table[...])
    return both[:, :width] + both[:, width:] + dot(low, table[:, :width])


def kernel(
    tiles, orients, guard,
    mic_any, tpl_any, ids_any, logw_any, mask_any, tx_any, ix_any, ty_any, tt_any, iy_any,
    out,
    mic, ids, logw, mask, tx, ix, ty, tt, iy, pack, halo,
    stack, ext, img, spec, scores, lse_out, lse_in, stats,
    load_sem, ready,
    halo_send, halo_recv, tpl_send, tpl_recv, lse_send, lse_recv, st_send, st_recv,
):
    t = lax.axis_index("tile")
    o = lax.axis_index("orient")
    everyone = tiles * orients
    extent, side = mic.shape
    patch = tpl_any.shape[2]
    length = 2 * patch
    blocks = side // patch
    share = out.shape[0]
    unrolled = everyone <= 16

    def partner(k):
        if tiles & (tiles - 1):
            return lax.rem(t + k, tiles)
        bit, peer = 1, 0
        while bit < tiles:
            peer = peer + lax.rem(t // bit + k // bit, 2) * bit
            bit *= 2
        return peer

    def seat_of(k):
        return {"tile": partner(k // orients), "orient": lax.rem(o + k % orients, orients)}

    def each_peer(body):
        if unrolled:
            for k in range(everyone - 1, 0, -1):
                body(k)
        else:
            def step(k, carry):
                body(k)
                return carry

            lax.fori_loop(1, everyone, step, 0)

    barrier = pltpu.get_barrier_semaphore()

    def announce(semaphore, first, last):
        def step(place, carry):
            for k in range(tiles):
                pl.semaphore_signal(
                    semaphore, inc=1, device_id={"tile": partner(k), "orient": place},
                    device_id_type=MESH,
                )
            return carry

        lax.fori_loop(first, last, step, 0)

    for k in range(1, tiles):
        pl.semaphore_signal(barrier, inc=1, device_id={"tile": partner(k)}, device_id_type=MESH)
    announce(barrier, o + 1, orients)

    sources = (
        ("tpl", tpl_any.at[0, 0], stack.at[0, pl.ds(0, patch)]),
        ("mic", mic_any, mic),
        ("ids", ids_any, ids),
        ("logw", logw_any, logw),
        ("tx", tx_any, tx),
        ("tt", tt_any, tt),
        ("ty", ty_any, ty),
        ("iy", iy_any, iy),
        ("ix", ix_any, ix),
        ("mask", mask_any, mask),
    )
    loads = {}
    for index, (name, source, target) in enumerate(sources):
        loads[name] = pltpu.make_async_copy(source, target, load_sem.at[index])
        loads[name].start()

    loads["ids"].wait()
    loads["logw"].wait()
    known = lax.broadcasted_iota(jnp.int32, (1, logw.shape[1]), 1) == ids[...]
    weight_here = jnp.sum(jnp.where(known, logw[...], 0.0), axis=1, keepdims=True)
    stack[0, patch:, :] = jnp.broadcast_to(weight_here, (stack.shape[1] - patch, patch))

    loads["mic"].wait()
    middle = extent // 2
    lane_half = lax.broadcasted_iota(jnp.int32, (middle, patch), 1) < guard
    outer, inner = mic[:, side - patch:], mic[:, :patch]
    pack[1] = jnp.where(lane_half, pltpu.roll(outer[:middle], guard, 1), outer[middle:])
    pack[0] = jnp.where(lane_half, inner[:middle], pltpu.roll(inner[middle:], guard, 1))
    loads["tpl"].wait()

    pl.semaphore_wait(barrier, tiles - 1 + tiles * o)

    def halo_copy(place, peer):
        return pltpu.make_async_remote_copy(
            src_ref=pack.at[place], dst_ref=halo.at[1 - place], send_sem=halo_send.at[place],
            recv_sem=halo_recv.at[1 - place], device_id={"tile": peer}, device_id_type=MESH,
        )

    to_left = halo_copy(0, lax.rem(t + tiles - 1, tiles))
    to_right = halo_copy(1, lax.rem(t + 1, tiles))

    def tpl_copy(k):
        return pltpu.make_async_remote_copy(
            src_ref=stack.at[0], dst_ref=stack.at[k], send_sem=tpl_send.at[k],
            recv_sem=tpl_recv.at[k], device_id={"tile": partner(k)}, device_id_type=MESH,
        )

    @pl.when(t > 0)
    def _():
        to_left.start()

    @pl.when(t < tiles - 1)
    def _():
        to_right.start()

    for k in range(1, tiles):
        tpl_copy(k).start()

    announce(ready, 0, o)

    loads["tx"].wait()
    loads["tt"].wait()

    def spectra(first, many):
        value = stack[pl.ds(first, many), :patch, :].reshape(many * patch, patch)
        high, low = split(value)
        top = tx[:patch, :]
        half = dot(jnp.concatenate([high, low], axis=1), jnp.concatenate([top, top], axis=0))
        half = half + dot(high, tx[length:length + patch, :])
        high, low = split(half)

        def stacked(part):
            return jnp.concatenate(
                [
                    jnp.concatenate(
                        [part[j * patch:(j + 1) * patch, :patch], part[j * patch:(j + 1) * patch, patch:]],
                        axis=0,
                    )
                    for j in range(many)
                ],
                axis=1,
            )

        whole = left_table(tt, stacked(high), stacked(low))
        for j in range(many):
            spec[first + j] = whole[:, j * patch:(j + 1) * patch]

    spectra(0, 1)

    rolled = [pltpu.roll(mic[:, b * patch:(b + 1) * patch], guard, 1) for b in range(blocks)]
    lane = lax.broadcasted_iota(jnp.int32, (extent, patch), 1)
    ext[0] = rolled[0]
    for b in range(1, blocks):
        ext[b] = jnp.where(lane < guard, rolled[b - 1], rolled[b])
    ext[blocks] = rolled[blocks - 1]

    loads["mask"].wait()
    mask_rows, mask_cols = mask.shape
    row_id = lax.broadcasted_iota(jnp.int32, (share, mask_rows), 0) + o * share
    pick = lax.broadcasted_iota(jnp.int32, (share, mask_rows), 1)
    low_edge = pick * MBLK
    rows_of = jnp.where((row_id >= low_edge) & (row_id < low_edge + MBLK), 1.0, 0.0).astype(F32)
    col_id = lax.broadcasted_iota(jnp.int32, (mask_cols, side), 1)
    col_edge = lax.broadcasted_iota(jnp.int32, (mask_cols, side), 0) * MBLK
    cols_of = jnp.where((col_id >= col_edge) & (col_id < col_edge + MBLK), 1.0, 0.0).astype(F32)
    unmasked = 1.0 - dot(dot(rows_of, mask[...].astype(F32)), cols_of)

    def whole_sum(value):
        return jnp.sum(jnp.sum(value, axis=0, keepdims=True), axis=1, keepdims=True)

    count = whole_sum(unmasked)

    def receive(place):
        present = (t > 0) if place == 0 else (t < tiles - 1)

        @pl.when(present)
        def _():
            halo_copy(1 - place, t).wait_recv()

        @pl.when(jnp.logical_not(present))
        def _():
            halo[place] = jnp.zeros(halo.shape[1:], F32)

        got = halo[place]
        turned = pltpu.roll(got, guard, 1)
        near = lax.broadcasted_iota(jnp.int32, (middle, patch), 1) < guard
        edge = 0 if place == 0 else blocks
        if place == 0:
            ext[edge, :middle] = jnp.where(near, got, ext[edge, :middle])
            ext[edge, middle:] = jnp.where(near, turned, ext[edge, middle:])
        else:
            ext[edge, :middle] = jnp.where(near, ext[edge, :middle], turned)
            ext[edge, middle:] = jnp.where(near, ext[edge, middle:], got)

    odd = lax.rem(t, 2) == 1
    early = 1 - lax.rem(t, 2)

    @pl.when(odd)
    def _():
        receive(0)

    @pl.when(jnp.logical_not(odd))
    def _():
        receive(1)

    def image(b):
        half = right_table(jnp.concatenate([ext[b], ext[b + 1]], axis=1), tx)
        high, low = split(half)

        def stacked(part):
            return jnp.concatenate(
                [
                    jnp.concatenate(
                        [part[a * patch:a * patch + length, :patch], part[a * patch:a * patch + length, patch:]],
                        axis=0,
                    )
                    for a in range(blocks)
                ],
                axis=1,
            )

        whole = left_table(ty, stacked(high), stacked(low))
        for a in range(blocks):
            img[b, a] = whole[:, a * patch:(a + 1) * patch]

    loads["ty"].wait()
    image(early)

    tpl_copy(1).wait_recv()
    spectra(1, 1)

    loads["ix"].wait()
    loads["iy"].wait()

    def correlate(items):
        highs, lows = [], []
        for k, a, b in items:
            sr, si = spec[k, :length], spec[k, length:]
            ir, ii = img[b, a, :length], img[b, a, length:]
            cross = jnp.concatenate([ir * sr + ii * si, ii * sr - ir * si], axis=0)
            high, low = split(cross)
            highs.append(high)
            lows.append(low)
        mid = left_table(iy, jnp.concatenate(highs, axis=1), jnp.concatenate(lows, axis=1))
        pieces = jnp.concatenate(
            [
                jnp.concatenate(
                    [mid[:patch, i * patch:(i + 1) * patch], mid[patch:, i * patch:(i + 1) * patch]],
                    axis=1,
                )
                for i in range(len(items))
            ],
            axis=0,
        )
        final = right_wide(pieces, ix)
        for i, (k, a, b) in enumerate(items):
            scores[k, a, b] = final[i * patch:(i + 1) * patch] + stack[k, patch:, :][:1, :1]

    correlate([(k, a, early) for k in range(2) for a in range(blocks)])

    @pl.when(odd)
    def _():
        receive(1)

    @pl.when(jnp.logical_not(odd))
    def _():
        receive(0)

    image(1 - early)
    correlate([(k, a, 1 - early) for k in range(2) for a in range(blocks)])

    for k in range(2, tiles):
        tpl_copy(k).wait_recv()

    def pairs(body):
        if tiles == 4:
            body(2)
        elif tiles > 4:
            def step(p, carry):
                body(2 * p)
                return carry

            lax.fori_loop(1, tiles // 2, step, 0)

    pairs(lambda k: spectra(k, 2))

    def own_lse(a, place):
        rows = pl.ds(pl.multiple_of(place * share, share), share)
        parts = []
        for b in range(blocks):
            top = scores[0, a, b, rows, :]
            for k in range(1, tiles):
                top = jnp.maximum(top, scores[k, a, b, rows, :])
            total = jnp.exp(scores[0, a, b, rows, :] - top)
            for k in range(1, tiles):
                total = total + jnp.exp(scores[k, a, b, rows, :] - top)
            parts.append(top + jnp.log(total))
        return jnp.concatenate(parts, axis=1)

    def lse_copy(k):
        return pltpu.make_async_remote_copy(
            src_ref=lse_out.at[k], dst_ref=lse_in.at[k], send_sem=lse_send.at[k],
            recv_sem=lse_recv.at[k], device_id={"orient": lax.rem(o + k, orients)},
            device_id_type=MESH,
        )

    owners = patch // share
    home, seat = o // owners, lax.rem(o, owners)

    def send_rows(a, place):
        ahead = lax.rem(a * owners + place - o + orients, orients)
        lse_out[ahead] = own_lse(a, place)
        lse_copy(ahead).start()

    @pl.when(o < orients - 1)
    def _():
        pl.semaphore_wait(ready, tiles * (orients - 1 - o))

    for s in range(blocks):
        a = lax.rem(home + 1 + s, blocks)
        pairs(lambda k: correlate([(k + j, a, b) for j in range(2) for b in range(blocks)]))
        if s < blocks - 1:
            for place in range(owners):
                send_rows(a, place)
        else:
            for gap in range(1, owners):
                send_rows(a, lax.rem(seat + gap, owners))
    mine = own_lse(home, seat)
    for k in range(1, orients):
        lse_copy(k).wait_recv()
    top = mine
    for k in range(1, orients):
        top = jnp.maximum(top, lse_in[k])
    total = jnp.exp(mine - top)
    for k in range(1, orients):
        total = total + jnp.exp(lse_in[k] - top)
    lse = top + jnp.log(total)

    sum_here = whole_sum(unmasked * lse)
    mean_here = sum_here / jnp.maximum(count, 1.0)
    deviation = lse - mean_here
    squares = whole_sum(unmasked * deviation * deviation)
    slot = lax.broadcasted_iota(jnp.int32, stats.shape[1:], 1)
    stats[0] = jnp.where(
        slot == 0, count, jnp.where(slot == 1, sum_here, jnp.where(slot == 2, squares, 0.0))
    )

    def st_copy(k):
        return pltpu.make_async_remote_copy(
            src_ref=stats.at[0], dst_ref=stats.at[k], send_sem=st_send.at[k],
            recv_sem=st_recv.at[k], device_id=seat_of(k), device_id_type=MESH,
        )

    each_peer(lambda k: st_copy(k).start())

    @pl.when(t > 0)
    def _():
        to_left.wait_send()

    @pl.when(t < tiles - 1)
    def _():
        to_right.wait_send()

    for k in range(1, tiles):
        tpl_copy(k).wait_send()
    for k in range(1, orients):
        lse_copy(k).wait_send()
    each_peer(lambda k: st_copy(k).wait())
    table = stats[:, 0, :]
    counts, sums, sqs = table[:, 0:1], table[:, 1:2], table[:, 2:3]
    live = jnp.sum(counts, axis=0, keepdims=True)
    average = jnp.sum(sums, axis=0, keepdims=True) / live
    gap = sums / jnp.maximum(counts, 1.0) - average
    variance = jnp.sum(sqs + counts * gap * gap, axis=0, keepdims=True) / live
    out[...] = unmasked * (lse - average) / jnp.sqrt(variance + 1e-05)


def body(tiles, orients, micrograph, templates, orient_ids, log_weight, ice_mask):
    extent, side = micrograph.shape
    patch = templates.shape[2]
    share = side // orients
    blocks = side // patch
    everyone = tiles * orients
    anywhere = pl.BlockSpec(memory_space=pl.ANY)
    vmem = pltpu.VMEM
    dma = pltpu.SemaphoreType.DMA
    consts = [jnp.asarray(table) for table in tables(patch)]
    return pl.pallas_call(
        functools.partial(kernel, tiles, orients, patch // 2),
        out_shape=jax.ShapeDtypeStruct((share, side), F32),
        in_specs=[anywhere] * (5 + len(consts)),
        out_specs=pl.BlockSpec(memory_space=pltpu.VMEM),
        scratch_shapes=[
            vmem((extent, side), F32),
            vmem(orient_ids.shape, jnp.int32),
            vmem((1, log_weight.shape[0]), F32),
            vmem(ice_mask.shape, jnp.int32),
            *[vmem(table.shape, BF16) for table in consts],
            vmem((2, extent // 2, patch), F32),
            vmem((2, extent // 2, patch), F32),
            vmem((tiles, patch + 8, patch), F32),
            vmem((blocks + 1, extent, patch), F32),
            vmem((blocks, blocks, 4 * patch, patch), F32),
            vmem((tiles, 4 * patch, patch), F32),
            vmem((tiles, blocks, blocks, patch, patch), F32),
            vmem((orients, share, side), F32),
            vmem((orients, share, side), F32),
            vmem((everyone, 1, 128), F32),
            dma((5 + len(consts),)),
            pltpu.SemaphoreType.REGULAR,
            dma((2,)), dma((2,)),
            dma((tiles,)), dma((tiles,)),
            dma((orients,)), dma((orients,)),
            dma((everyone,)), dma((everyone,)),
        ],
        compiler_params=pltpu.CompilerParams(
            collective_id=0, has_side_effects=True, vmem_limit_bytes=56 * 1024 * 1024
        ),
    )(micrograph, templates, orient_ids, log_weight.reshape(1, -1), ice_mask, *consts)


def solution(mesh):
    return jax.shard_map(
        functools.partial(body, mesh.shape["tile"], mesh.shape["orient"]),
        mesh=mesh,
        in_specs=(
            P("group", "tile"),
            P("orient", "tile", None, None),
            P("orient", "tile"),
            P(),
            P("group", "tile"),
        ),
        out_specs=P(("group", "orient"), "tile"),
        check_vma=False,
    )
```

```python
import functools
import math

import jax
import jax.numpy as jnp
import numpy as np
from jax import lax
from jax.experimental import pallas as pl
from jax.experimental.pallas import tpu as pltpu
from jax.sharding import PartitionSpec as P

MBLK = 16
F32 = jnp.float32
BF16 = jnp.bfloat16
MESH = pl.DeviceIdType.MESH


def halves(table, axis=0):
    table = table.astype(np.float32)
    high = table.astype(jnp.bfloat16)
    low = (table - high.astype(np.float32)).astype(jnp.bfloat16)
    return np.concatenate([high, low], axis=axis)


def tables(patch):
    length = 2 * patch
    n = np.arange(length)[:, None]
    k = np.arange(patch)[None, :]
    theta = 2 * math.pi * ((n * (2 * k + 1)) % (2 * length)) / (2 * length)
    tx = np.concatenate([np.cos(theta), -np.sin(theta)], axis=1)
    back = theta[:patch].T
    ix = np.concatenate([np.cos(back), -np.sin(back)], axis=0) * (2.0 / length)
    m = np.arange(length)
    phi = 2 * math.pi * ((m[:, None] * m[None, :]) % length) / length
    c, s = np.cos(phi), np.sin(phi)
    ty = np.block([[c, s], [-s, c]])
    cp, sp = c[:, :patch], s[:, :patch]
    tt = np.block([[cp, sp], [-sp, cp]])
    ci, si = c[:patch], s[:patch]
    iy = np.block([[ci, -si], [si, ci]]) / length
    return halves(tx), halves(ix, 1), halves(ty), halves(tt), halves(iy)


def split(value):
    high = value.astype(BF16)
    low = (value - high.astype(F32)).astype(BF16)
    return high, low


def dot(a, b):
    return jnp.dot(a, b, preferred_element_type=F32)


def left_table(table, high, low):
    rows = table.shape[0] // 2
    both = dot(table[...], high)
    return both[:rows] + both[rows:] + dot(table[:rows, :], low)


def right_table(value, table):
    depth = table.shape[0] // 2
    high, low = split(value)
    return dot(jnp.concatenate([high, high], axis=1), table[...]) + dot(low, table[:depth, :])


def right_wide(value, table):
    width = table.shape[1] // 2
    high, low = split(value)
    both = dot(high, table[...])
    return both[:, :width] + both[:, width:] + dot(low, table[:, :width])


def kernel(
    tiles, orients, guard,
    mic_any, tpl_any, ids_any, logw_any, mask_any, tx_any, ix_any, ty_any, tt_any, iy_any,
    out,
    mic, ids, logw, mask, tx, ix, ty, tt, iy, pack, halo,
    stack, ext, img, spec, scores, lse_out, lse_in, stats,
    load_sem, ready,
    halo_send, halo_recv, tpl_send, tpl_recv, lse_send, lse_recv, st_send, st_recv,
):
    t = lax.axis_index("tile")
    o = lax.axis_index("orient")
    everyone = tiles * orients
    extent, side = mic.shape
    patch = tpl_any.shape[2]
    length = 2 * patch
    blocks = side // patch
    share = out.shape[0]
    unrolled = everyone <= 16

    def partner(k):
        if tiles & (tiles - 1):
            return lax.rem(t + k, tiles)
        bit, peer = 1, 0
        while bit < tiles:
            peer = peer + lax.rem(t // bit + k // bit, 2) * bit
            bit *= 2
        return peer

    def seat_of(k):
        return {"tile": partner(k // orients), "orient": lax.rem(o + k % orients, orients)}

    def each_peer(body):
        if unrolled:
            for k in range(everyone - 1, 0, -1):
                body(k)
        else:
            def step(k, carry):
                body(k)
                return carry

            lax.fori_loop(1, everyone, step, 0)

    barrier = pltpu.get_barrier_semaphore()

    def announce(semaphore, first, last):
        def step(place, carry):
            for k in range(tiles):
                pl.semaphore_signal(
                    semaphore, inc=1, device_id={"tile": partner(k), "orient": place},
                    device_id_type=MESH,
                )
            return carry

        lax.fori_loop(first, last, step, 0)

    for k in range(1, tiles):
        pl.semaphore_signal(barrier, inc=1, device_id={"tile": partner(k)}, device_id_type=MESH)
    announce(barrier, o + 1, orients)

    sources = (
        ("tpl", tpl_any.at[0, 0], stack.at[0, pl.ds(0, patch)]),
        ("mic", mic_any, mic),
        ("ids", ids_any, ids),
        ("logw", logw_any, logw),
        ("tx", tx_any, tx),
        ("tt", tt_any, tt),
        ("ty", ty_any, ty),
        ("iy", iy_any, iy),
        ("ix", ix_any, ix),
        ("mask", mask_any, mask),
    )
    loads = {}
    for index, (name, source, target) in enumerate(sources):
        loads[name] = pltpu.make_async_copy(source, target, load_sem.at[index])
        loads[name].start()

    loads["ids"].wait()
    loads["logw"].wait()
    known = lax.broadcasted_iota(jnp.int32, (1, logw.shape[1]), 1) == ids[...]
    weight_here = jnp.sum(jnp.where(known, logw[...], 0.0), axis=1, keepdims=True)
    stack[0, patch:, :] = jnp.broadcast_to(weight_here, (stack.shape[1] - patch, patch))

    loads["mic"].wait()
    middle = extent // 2
    lane_half = lax.broadcasted_iota(jnp.int32, (middle, patch), 1) < guard
    outer, inner = mic[:, side - patch:], mic[:, :patch]
    pack[1] = jnp.where(lane_half, pltpu.roll(outer[:middle], guard, 1), outer[middle:])
    pack[0] = jnp.where(lane_half, inner[:middle], pltpu.roll(inner[middle:], guard, 1))
    loads["tpl"].wait()

    pl.semaphore_wait(barrier, tiles - 1 + tiles * o)

    def halo_copy(place, peer):
        return pltpu.make_async_remote_copy(
            src_ref=pack.at[place], dst_ref=halo.at[1 - place], send_sem=halo_send.at[place],
            recv_sem=halo_recv.at[1 - place], device_id={"tile": peer}, device_id_type=MESH,
        )

    to_left = halo_copy(0, lax.rem(t + tiles - 1, tiles))
    to_right = halo_copy(1, lax.rem(t + 1, tiles))

    def tpl_copy(k):
        return pltpu.make_async_remote_copy(
            src_ref=stack.at[0], dst_ref=stack.at[k], send_sem=tpl_send.at[k],
            recv_sem=tpl_recv.at[k], device_id={"tile": partner(k)}, device_id_type=MESH,
        )

    @pl.when(t > 0)
    def _():
        to_left.start()

    @pl.when(t < tiles - 1)
    def _():
        to_right.start()

    for k in range(1, tiles):
        tpl_copy(k).start()

    announce(ready, 0, o)

    loads["tx"].wait()
    loads["tt"].wait()

    def spectra(first, many):
        value = stack[pl.ds(first, many), :patch, :].reshape(many * patch, patch)
        high, low = split(value)
        top = tx[:patch, :]
        half = dot(jnp.concatenate([high, low], axis=1), jnp.concatenate([top, top], axis=0))
        half = half + dot(high, tx[length:length + patch, :])
        high, low = split(half)

        def stacked(part):
            return jnp.concatenate(
                [
                    jnp.concatenate(
                        [part[j * patch:(j + 1) * patch, :patch], part[j * patch:(j + 1) * patch, patch:]],
                        axis=0,
                    )
                    for j in range(many)
                ],
                axis=1,
            )

        whole = left_table(tt, stacked(high), stacked(low))
        for j in range(many):
            spec[first + j] = whole[:, j * patch:(j + 1) * patch]

    spectra(0, 1)

    rolled = [pltpu.roll(mic[:, b * patch:(b + 1) * patch], guard, 1) for b in range(blocks)]
    lane = lax.broadcasted_iota(jnp.int32, (extent, patch), 1)
    ext[0] = rolled[0]
    for b in range(1, blocks):
        ext[b] = jnp.where(lane < guard, rolled[b - 1], rolled[b])
    ext[blocks] = rolled[blocks - 1]

    loads["mask"].wait()
    mask_rows, mask_cols = mask.shape
    row_id = lax.broadcasted_iota(jnp.int32, (share, mask_rows), 0) + o * share
    pick = lax.broadcasted_iota(jnp.int32, (share, mask_rows), 1)
    low_edge = pick * MBLK
    rows_of = jnp.where((row_id >= low_edge) & (row_id < low_edge + MBLK), 1.0, 0.0).astype(F32)
    col_id = lax.broadcasted_iota(jnp.int32, (mask_cols, side), 1)
    col_edge = lax.broadcasted_iota(jnp.int32, (mask_cols, side), 0) * MBLK
    cols_of = jnp.where((col_id >= col_edge) & (col_id < col_edge + MBLK), 1.0, 0.0).astype(F32)
    unmasked = 1.0 - dot(dot(rows_of, mask[...].astype(F32)), cols_of)

    def whole_sum(value):
        return jnp.sum(jnp.sum(value, axis=0, keepdims=True), axis=1, keepdims=True)

    count = whole_sum(unmasked)

    def receive(place):
        present = (t > 0) if place == 0 else (t < tiles - 1)

        @pl.when(present)
        def _():
            halo_copy(1 - place, t).wait_recv()

        @pl.when(jnp.logical_not(present))
        def _():
            halo[place] = jnp.zeros(halo.shape[1:], F32)

        got = halo[place]
        turned = pltpu.roll(got, guard, 1)
        near = lax.broadcasted_iota(jnp.int32, (middle, patch), 1) < guard
        edge = 0 if place == 0 else blocks
        if place == 0:
            ext[edge, :middle] = jnp.where(near, got, ext[edge, :middle])
            ext[edge, middle:] = jnp.where(near, turned, ext[edge, middle:])
        else:
            ext[edge, :middle] = jnp.where(near, ext[edge, :middle], turned)
            ext[edge, middle:] = jnp.where(near, ext[edge, middle:], got)

    def image(b):
        half = right_table(jnp.concatenate([ext[b], ext[b + 1]], axis=1), tx)
        high, low = split(half)

        def stacked(part):
            return jnp.concatenate(
                [
                    jnp.concatenate(
                        [part[a * patch:a * patch + length, :patch], part[a * patch:a * patch + length, patch:]],
                        axis=0,
                    )
                    for a in range(blocks)
                ],
                axis=1,
            )

        whole = left_table(ty, stacked(high), stacked(low))
        for a in range(blocks):
            img[b, a] = whole[:, a * patch:(a + 1) * patch]

    def correlate(items):
        highs, lows = [], []
        for k, a, b in items:
            sr, si = spec[k, :length], spec[k, length:]
            ir, ii = img[b, a, :length], img[b, a, length:]
            cross = jnp.concatenate([ir * sr + ii * si, ii * sr - ir * si], axis=0)
            high, low = split(cross)
            highs.append(high)
            lows.append(low)
        mid = left_table(iy, jnp.concatenate(highs, axis=1), jnp.concatenate(lows, axis=1))
        pieces = jnp.concatenate(
            [
                jnp.concatenate(
                    [mid[:patch, i * patch:(i + 1) * patch], mid[patch:, i * patch:(i + 1) * patch]],
                    axis=1,
                )
                for i in range(len(items))
            ],
            axis=0,
        )
        final = right_wide(pieces, ix)
        for i, (k, a, b) in enumerate(items):
            scores[k, a, b] = final[i * patch:(i + 1) * patch] + stack[k, patch:, :][:1, :1]

    tpl_copy(1).wait_recv()
    spectra(1, 1)
    loads["ty"].wait()
    loads["ix"].wait()
    loads["iy"].wait()
    odd = lax.rem(t, 2)

    def column(i, carry):
        place = lax.rem(i + 1 + odd, 2)

        @pl.when(place == 0)
        def _():
            receive(0)

        @pl.when(place == 1)
        def _():
            receive(1)

        image(place)
        correlate([(k, a, place) for k in range(2) for a in range(blocks)])
        return carry

    lax.fori_loop(0, 2, column, 0)

    for k in range(2, tiles):
        tpl_copy(k).wait_recv()

    def pairs(body):
        if tiles == 4:
            body(2)
        elif tiles > 4:
            def step(p, carry):
                body(2 * p)
                return carry

            lax.fori_loop(1, tiles // 2, step, 0)

    pairs(lambda k: spectra(k, 2))

    def own_lse(a, place):
        rows = pl.ds(pl.multiple_of(place * share, share), share)
        parts = []
        for b in range(blocks):
            top = scores[0, a, b, rows, :]
            for k in range(1, tiles):
                top = jnp.maximum(top, scores[k, a, b, rows, :])
            total = jnp.exp(scores[0, a, b, rows, :] - top)
            for k in range(1, tiles):
                total = total + jnp.exp(scores[k, a, b, rows, :] - top)
            parts.append(top + jnp.log(total))
        return jnp.concatenate(parts, axis=1)

    def lse_copy(k):
        return pltpu.make_async_remote_copy(
            src_ref=lse_out.at[k], dst_ref=lse_in.at[k], send_sem=lse_send.at[k],
            recv_sem=lse_recv.at[k], device_id={"orient": lax.rem(o + k, orients)},
            device_id_type=MESH,
        )

    owners = patch // share
    home, seat = o // owners, lax.rem(o, owners)

    @pl.when(o < orients - 1)
    def _():
        pl.semaphore_wait(ready, tiles * (orients - 1 - o))

    def row(s, carry):
        a = lax.rem(home + 1 + s, blocks)
        pairs(lambda k: correlate([(k + j, a, b) for j in range(2) for b in range(blocks)]))
        for gap in range(1, owners + 1):
            place = lax.rem(seat + gap, owners)
            ahead = lax.rem(a * owners + place - o + orients, orients)
            lse_out[ahead] = own_lse(a, place)

            @pl.when(ahead > 0)
            def _():
                lse_copy(ahead).start()
        return carry

    lax.fori_loop(0, blocks, row, 0)
    mine = lse_out[0]
    for k in range(1, orients):
        lse_copy(k).wait_recv()
    top = mine
    for k in range(1, orients):
        top = jnp.maximum(top, lse_in[k])
    total = jnp.exp(mine - top)
    for k in range(1, orients):
        total = total + jnp.exp(lse_in[k] - top)
    lse = top + jnp.log(total)

    sum_here = whole_sum(unmasked * lse)
    mean_here = sum_here / jnp.maximum(count, 1.0)
    deviation = lse - mean_here
    squares = whole_sum(unmasked * deviation * deviation)
    slot = lax.broadcasted_iota(jnp.int32, stats.shape[1:], 1)
    stats[0] = jnp.where(
        slot == 0, count, jnp.where(slot == 1, sum_here, jnp.where(slot == 2, squares, 0.0))
    )

    def st_copy(k):
        return pltpu.make_async_remote_copy(
            src_ref=stats.at[0], dst_ref=stats.at[k], send_sem=st_send.at[k],
            recv_sem=st_recv.at[k], device_id=seat_of(k), device_id_type=MESH,
        )

    each_peer(lambda k: st_copy(k).start())

    @pl.when(t > 0)
    def _():
        to_left.wait_send()

    @pl.when(t < tiles - 1)
    def _():
        to_right.wait_send()

    for k in range(1, tiles):
        tpl_copy(k).wait_send()
    for k in range(1, orients):
        lse_copy(k).wait_send()
    each_peer(lambda k: st_copy(k).wait())
    table = stats[:, 0, :]
    counts, sums, sqs = table[:, 0:1], table[:, 1:2], table[:, 2:3]
    live = jnp.sum(counts, axis=0, keepdims=True)
    average = jnp.sum(sums, axis=0, keepdims=True) / live
    gap = sums / jnp.maximum(counts, 1.0) - average
    variance = jnp.sum(sqs + counts * gap * gap, axis=0, keepdims=True) / live
    out[...] = unmasked * (lse - average) / jnp.sqrt(variance + 1e-05)


def body(tiles, orients, micrograph, templates, orient_ids, log_weight, ice_mask):
    extent, side = micrograph.shape
    patch = templates.shape[2]
    share = side // orients
    blocks = side // patch
    everyone = tiles * orients
    anywhere = pl.BlockSpec(memory_space=pl.ANY)
    vmem = pltpu.VMEM
    dma = pltpu.SemaphoreType.DMA
    consts = [jnp.asarray(table) for table in tables(patch)]
    return pl.pallas_call(
        functools.partial(kernel, tiles, orients, patch // 2),
        out_shape=jax.ShapeDtypeStruct((share, side), F32),
        in_specs=[anywhere] * (5 + len(consts)),
        out_specs=pl.BlockSpec(memory_space=pltpu.VMEM),
        scratch_shapes=[
            vmem((extent, side), F32),
            vmem(orient_ids.shape, jnp.int32),
            vmem((1, log_weight.shape[0]), F32),
            vmem(ice_mask.shape, jnp.int32),
            *[vmem(table.shape, BF16) for table in consts],
            vmem((2, extent // 2, patch), F32),
            vmem((2, extent // 2, patch), F32),
            vmem((tiles, patch + 8, patch), F32),
            vmem((blocks + 1, extent, patch), F32),
            vmem((blocks, blocks, 4 * patch, patch), F32),
            vmem((tiles, 4 * patch, patch), F32),
            vmem((tiles, blocks, blocks, patch, patch), F32),
            vmem((orients, share, side), F32),
            vmem((orients, share, side), F32),
            vmem((everyone, 1, 128), F32),
            dma((5 + len(consts),)),
            pltpu.SemaphoreType.REGULAR,
            dma((2,)), dma((2,)),
            dma((tiles,)), dma((tiles,)),
            dma((orients,)), dma((orients,)),
            dma((everyone,)), dma((everyone,)),
        ],
        compiler_params=pltpu.CompilerParams(
            collective_id=0, has_side_effects=True, vmem_limit_bytes=56 * 1024 * 1024
        ),
    )(micrograph, templates, orient_ids, log_weight.reshape(1, -1), ice_mask, *consts)


def solution(mesh):
    return jax.shard_map(
        functools.partial(body, mesh.shape["tile"], mesh.shape["orient"]),
        mesh=mesh,
        in_specs=(
            P("group", "tile"),
            P("orient", "tile", None, None),
            P("orient", "tile"),
            P(),
            P("group", "tile"),
        ),
        out_specs=P(("group", "orient"), "tile"),
        check_vma=False,
    )
```

```python
import functools
import math

import jax
import jax.numpy as jnp
import numpy as np
from jax import lax
from jax.experimental import pallas as pl
from jax.experimental.pallas import tpu as pltpu
from jax.sharding import PartitionSpec as P

MBLK = 16
F32 = jnp.float32
BF16 = jnp.bfloat16
MESH = pl.DeviceIdType.MESH


def halves(table, axis=0):
    table = table.astype(np.float32)
    high = table.astype(jnp.bfloat16)
    low = (table - high.astype(np.float32)).astype(jnp.bfloat16)
    return np.concatenate([high, low], axis=axis)


def tables(patch):
    length = 2 * patch
    n = np.arange(length)[:, None]
    k = np.arange(patch)[None, :]
    theta = 2 * math.pi * ((n * (2 * k + 1)) % (2 * length)) / (2 * length)
    tx = np.concatenate([np.cos(theta), -np.sin(theta)], axis=1)
    back = theta[:patch].T
    ix = np.concatenate([np.cos(back), -np.sin(back)], axis=0) * (2.0 / length)
    m = np.arange(length)
    phi = 2 * math.pi * ((m[:, None] * m[None, :]) % length) / length
    c, s = np.cos(phi), np.sin(phi)
    ty = np.block([[c, s], [-s, c]])
    cp, sp = c[:, :patch], s[:, :patch]
    tt = np.block([[cp, sp], [-sp, cp]])
    ci, si = c[:patch], s[:patch]
    iy = np.block([[ci, -si], [si, ci]]) / length
    return halves(tx), halves(ix, 1), halves(ty), halves(tt), halves(iy)


def split(value):
    high = value.astype(BF16)
    low = (value - high.astype(F32)).astype(BF16)
    return high, low


def dot(a, b):
    return jnp.dot(a, b, preferred_element_type=F32)


def left_table(table, high, low):
    rows = table.shape[0] // 2
    both = dot(table[...], high)
    return both[:rows] + both[rows:] + dot(table[:rows, :], low)


def right_table(value, table):
    depth = table.shape[0] // 2
    high, low = split(value)
    return dot(jnp.concatenate([high, high], axis=1), table[...]) + dot(low, table[:depth, :])


def right_wide(value, table):
    width = table.shape[1] // 2
    high, low = split(value)
    both = dot(high, table[...])
    return both[:, :width] + both[:, width:] + dot(low, table[:, :width])


def kernel(
    tiles, orients, guard,
    mic_any, tpl_any, ids_any, logw_any, mask_any, tx_any, ix_any, ty_any, tt_any, iy_any,
    lse_any, um_any, st_any,
    mic, ids, logw, mask, tx, ix, ty, tt, iy, pack, halo,
    stack, ext, img, spec, scores, lse_out, lse_in, stats, um,
    load_sem, ready, keep_sem,
    halo_send, halo_recv, tpl_send, tpl_recv, lse_send, lse_recv, st_send, st_recv,
):
    t = lax.axis_index("tile")
    o = lax.axis_index("orient")
    everyone = tiles * orients
    extent, side = mic.shape
    patch = tpl_any.shape[2]
    length = 2 * patch
    blocks = side // patch
    share = lse_any.shape[0]
    unrolled = everyone <= 16

    def partner(k):
        if tiles & (tiles - 1):
            return lax.rem(t + k, tiles)
        bit, peer = 1, 0
        while bit < tiles:
            peer = peer + lax.rem(t // bit + k // bit, 2) * bit
            bit *= 2
        return peer

    def seat_of(k):
        return {"tile": partner(k // orients), "orient": lax.rem(o + k % orients, orients)}

    def each_peer(body):
        if unrolled:
            for k in range(everyone - 1, 0, -1):
                body(k)
        else:
            def step(k, carry):
                body(k)
                return carry

            lax.fori_loop(1, everyone, step, 0)

    barrier = pltpu.get_barrier_semaphore()

    def announce(semaphore, first, last):
        def step(place, carry):
            for k in range(tiles):
                pl.semaphore_signal(
                    semaphore, inc=1, device_id={"tile": partner(k), "orient": place},
                    device_id_type=MESH,
                )
            return carry

        lax.fori_loop(first, last, step, 0)

    for k in range(1, tiles):
        pl.semaphore_signal(barrier, inc=1, device_id={"tile": partner(k)}, device_id_type=MESH)
    announce(barrier, o + 1, orients)

    sources = (
        ("tpl", tpl_any.at[0, 0], stack.at[0, pl.ds(0, patch)]),
        ("mic", mic_any, mic),
        ("ids", ids_any, ids),
        ("logw", logw_any, logw),
        ("tx", tx_any, tx),
        ("tt", tt_any, tt),
        ("ty", ty_any, ty),
        ("iy", iy_any, iy),
        ("ix", ix_any, ix),
        ("mask", mask_any, mask),
    )
    loads = {}
    for index, (name, source, target) in enumerate(sources):
        loads[name] = pltpu.make_async_copy(source, target, load_sem.at[index])
        loads[name].start()

    loads["ids"].wait()
    loads["logw"].wait()
    known = lax.broadcasted_iota(jnp.int32, (1, logw.shape[1]), 1) == ids[...]
    weight_here = jnp.sum(jnp.where(known, logw[...], 0.0), axis=1, keepdims=True)
    stack[0, patch:, :] = jnp.broadcast_to(weight_here, (stack.shape[1] - patch, patch))

    loads["mic"].wait()
    middle = extent // 2
    lane_half = lax.broadcasted_iota(jnp.int32, (middle, patch), 1) < guard
    outer, inner = mic[:, side - patch:], mic[:, :patch]
    pack[1] = jnp.where(lane_half, pltpu.roll(outer[:middle], guard, 1), outer[middle:])
    pack[0] = jnp.where(lane_half, inner[:middle], pltpu.roll(inner[middle:], guard, 1))
    loads["tpl"].wait()

    pl.semaphore_wait(barrier, tiles - 1 + tiles * o)

    def halo_copy(place, peer):
        return pltpu.make_async_remote_copy(
            src_ref=pack.at[place], dst_ref=halo.at[1 - place], send_sem=halo_send.at[place],
            recv_sem=halo_recv.at[1 - place], device_id={"tile": peer}, device_id_type=MESH,
        )

    to_left = halo_copy(0, lax.rem(t + tiles - 1, tiles))
    to_right = halo_copy(1, lax.rem(t + 1, tiles))

    def tpl_copy(k):
        return pltpu.make_async_remote_copy(
            src_ref=stack.at[0], dst_ref=stack.at[k], send_sem=tpl_send.at[k],
            recv_sem=tpl_recv.at[k], device_id={"tile": partner(k)}, device_id_type=MESH,
        )

    @pl.when(t > 0)
    def _():
        to_left.start()

    @pl.when(t < tiles - 1)
    def _():
        to_right.start()

    for k in range(1, tiles):
        tpl_copy(k).start()

    announce(ready, 0, o)

    loads["tx"].wait()
    loads["tt"].wait()

    def spectra(first, many):
        value = stack[pl.ds(first, many), :patch, :].reshape(many * patch, patch)
        high, low = split(value)
        top = tx[:patch, :]
        half = dot(jnp.concatenate([high, low], axis=1), jnp.concatenate([top, top], axis=0))
        half = half + dot(high, tx[length:length + patch, :])
        high, low = split(half)

        def stacked(part):
            return jnp.concatenate(
                [
                    jnp.concatenate(
                        [part[j * patch:(j + 1) * patch, :patch], part[j * patch:(j + 1) * patch, patch:]],
                        axis=0,
                    )
                    for j in range(many)
                ],
                axis=1,
            )

        whole = left_table(tt, stacked(high), stacked(low))
        for j in range(many):
            spec[first + j] = whole[:, j * patch:(j + 1) * patch]

    spectra(0, 1)

    rolled = [pltpu.roll(mic[:, b * patch:(b + 1) * patch], guard, 1) for b in range(blocks)]
    lane = lax.broadcasted_iota(jnp.int32, (extent, patch), 1)
    ext[0] = rolled[0]
    for b in range(1, blocks):
        ext[b] = jnp.where(lane < guard, rolled[b - 1], rolled[b])
    ext[blocks] = rolled[blocks - 1]

    loads["mask"].wait()
    mask_rows, mask_cols = mask.shape
    row_id = lax.broadcasted_iota(jnp.int32, (share, mask_rows), 0) + o * share
    pick = lax.broadcasted_iota(jnp.int32, (share, mask_rows), 1)
    low_edge = pick * MBLK
    rows_of = jnp.where((row_id >= low_edge) & (row_id < low_edge + MBLK), 1.0, 0.0).astype(F32)
    col_id = lax.broadcasted_iota(jnp.int32, (mask_cols, side), 1)
    col_edge = lax.broadcasted_iota(jnp.int32, (mask_cols, side), 0) * MBLK
    cols_of = jnp.where((col_id >= col_edge) & (col_id < col_edge + MBLK), 1.0, 0.0).astype(F32)
    unmasked = 1.0 - dot(dot(rows_of, mask[...].astype(F32)), cols_of)

    def whole_sum(value):
        return jnp.sum(jnp.sum(value, axis=0, keepdims=True), axis=1, keepdims=True)

    count = whole_sum(unmasked)
    um[...] = unmasked
    keep_um = pltpu.make_async_copy(um, um_any, keep_sem.at[0])
    keep_um.start()

    def receive(place):
        present = (t > 0) if place == 0 else (t < tiles - 1)

        @pl.when(present)
        def _():
            halo_copy(1 - place, t).wait_recv()

        @pl.when(jnp.logical_not(present))
        def _():
            halo[place] = jnp.zeros(halo.shape[1:], F32)

        got = halo[place]
        turned = pltpu.roll(got, guard, 1)
        near = lax.broadcasted_iota(jnp.int32, (middle, patch), 1) < guard
        edge = 0 if place == 0 else blocks
        if place == 0:
            ext[edge, :middle] = jnp.where(near, got, ext[edge, :middle])
            ext[edge, middle:] = jnp.where(near, turned, ext[edge, middle:])
        else:
            ext[edge, :middle] = jnp.where(near, ext[edge, :middle], turned)
            ext[edge, middle:] = jnp.where(near, ext[edge, middle:], got)

    def image(b):
        half = right_table(jnp.concatenate([ext[b], ext[b + 1]], axis=1), tx)
        high, low = split(half)

        def stacked(part):
            return jnp.concatenate(
                [
                    jnp.concatenate(
                        [part[a * patch:a * patch + length, :patch], part[a * patch:a * patch + length, patch:]],
                        axis=0,
                    )
                    for a in range(blocks)
                ],
                axis=1,
            )

        whole = left_table(ty, stacked(high), stacked(low))
        for a in range(blocks):
            img[b, a] = whole[:, a * patch:(a + 1) * patch]

    def correlate(items):
        highs, lows = [], []
        for k, a, b in items:
            sr, si = spec[k, :length], spec[k, length:]
            ir, ii = img[b, a, :length], img[b, a, length:]
            cross = jnp.concatenate([ir * sr + ii * si, ii * sr - ir * si], axis=0)
            high, low = split(cross)
            highs.append(high)
            lows.append(low)
        mid = left_table(iy, jnp.concatenate(highs, axis=1), jnp.concatenate(lows, axis=1))
        pieces = jnp.concatenate(
            [
                jnp.concatenate(
                    [mid[:patch, i * patch:(i + 1) * patch], mid[patch:, i * patch:(i + 1) * patch]],
                    axis=1,
                )
                for i in range(len(items))
            ],
            axis=0,
        )
        final = right_wide(pieces, ix)
        for i, (k, a, b) in enumerate(items):
            scores[k, a, b] = final[i * patch:(i + 1) * patch] + stack[k, patch:, :][:1, :1]

    tpl_copy(1).wait_recv()
    spectra(1, 1)
    loads["ty"].wait()
    loads["ix"].wait()
    loads["iy"].wait()
    odd = lax.rem(t, 2)

    def column(i, carry):
        place = lax.rem(i + 1 + odd, 2)

        @pl.when(place == 0)
        def _():
            receive(0)

        @pl.when(place == 1)
        def _():
            receive(1)

        image(place)
        return carry

    lax.fori_loop(0, 2, column, 0)

    def pairs(body):
        if tiles == 4:
            body(2)
        elif tiles > 4:
            def step(p, carry):
                body(2 * p)
                return carry

            lax.fori_loop(1, tiles // 2, step, 0)

    def own_lse(a, place):
        rows = pl.ds(pl.multiple_of(place * share, share), share)
        parts = []
        for b in range(blocks):
            top = scores[0, a, b, rows, :]
            for k in range(1, tiles):
                top = jnp.maximum(top, scores[k, a, b, rows, :])
            total = jnp.exp(scores[0, a, b, rows, :] - top)
            for k in range(1, tiles):
                total = total + jnp.exp(scores[k, a, b, rows, :] - top)
            parts.append(top + jnp.log(total))
        return jnp.concatenate(parts, axis=1)

    def lse_copy(k):
        return pltpu.make_async_remote_copy(
            src_ref=lse_out.at[k], dst_ref=lse_in.at[k], send_sem=lse_send.at[k],
            recv_sem=lse_recv.at[k], device_id={"orient": lax.rem(o + k, orients)},
            device_id_type=MESH,
        )

    owners = patch // share
    home, seat = o // owners, lax.rem(o, owners)

    def far_spectra():
        for k in range(2, tiles):
            tpl_copy(k).wait_recv()
        pairs(lambda k: spectra(k, 2))

        @pl.when(o < orients - 1)
        def _():
            pl.semaphore_wait(ready, tiles * (orients - 1 - o))

    def cell(j, carry):
        first = j // blocks * 2
        a = lax.rem(home + 1 + lax.rem(j, blocks), blocks)

        @pl.when(j == blocks)
        def _():
            far_spectra()

        correlate([(first + q, a, b) for q in range(2) for b in range(blocks)])

        @pl.when(first == tiles - 2)
        def _():
            def send(gap, inner):
                place = lax.rem(seat + gap, owners)
                ahead = lax.rem(a * owners + place - o + orients, orients)
                lse_out[ahead] = own_lse(a, place)

                @pl.when(ahead > 0)
                def _():
                    lse_copy(ahead).start()

                return inner

            lax.fori_loop(1, owners + 1, send, 0)

        return carry

    lax.fori_loop(0, blocks * (tiles // 2), cell, 0)
    mine = lse_out[0]
    for k in range(1, orients):
        lse_copy(k).wait_recv()
    top = mine
    for k in range(1, orients):
        top = jnp.maximum(top, lse_in[k])
    total = jnp.exp(mine - top)
    for k in range(1, orients):
        total = total + jnp.exp(lse_in[k] - top)
    lse = top + jnp.log(total)

    sum_here = whole_sum(unmasked * lse)
    mean_here = sum_here / jnp.maximum(count, 1.0)
    deviation = lse - mean_here
    squares = whole_sum(unmasked * deviation * deviation)
    slot = lax.broadcasted_iota(jnp.int32, stats.shape, 1)
    stats[...] = jnp.where(
        slot == 0, count, jnp.where(slot == 1, sum_here, jnp.where(slot == 2, squares, 0.0))
    )

    def st_copy(k):
        return pltpu.make_async_remote_copy(
            src_ref=stats, dst_ref=st_any.at[k], send_sem=st_send.at[k],
            recv_sem=st_recv.at[k], device_id=seat_of(k), device_id_type=MESH,
        )

    each_peer(lambda k: st_copy(k).start())
    lse_in[0] = lse
    keep_lse = pltpu.make_async_copy(lse_in.at[0], lse_any, keep_sem.at[1])
    keep_lse.start()
    keep_st = pltpu.make_async_copy(stats, st_any.at[0], keep_sem.at[2])
    keep_st.start()

    @pl.when(t > 0)
    def _():
        to_left.wait_send()

    @pl.when(t < tiles - 1)
    def _():
        to_right.wait_send()

    for k in range(1, tiles):
        tpl_copy(k).wait_send()
    for k in range(1, orients):
        lse_copy(k).wait_send()
    each_peer(lambda k: st_copy(k).wait())
    keep_um.wait()
    keep_lse.wait()
    keep_st.wait()


def finish(lse, unmasked, stats, out):
    table = stats[:, 0, :]
    counts, sums, sqs = table[:, 0:1], table[:, 1:2], table[:, 2:3]
    live = jnp.sum(counts, axis=0, keepdims=True)
    average = jnp.sum(sums, axis=0, keepdims=True) / live
    gap = sums / jnp.maximum(counts, 1.0) - average
    variance = jnp.sum(sqs + counts * gap * gap, axis=0, keepdims=True) / live
    out[...] = unmasked[...] * (lse[...] - average) / jnp.sqrt(variance + 1e-05)


def body(tiles, orients, micrograph, templates, orient_ids, log_weight, ice_mask):
    extent, side = micrograph.shape
    patch = templates.shape[2]
    share = side // orients
    blocks = side // patch
    everyone = tiles * orients
    anywhere = pl.BlockSpec(memory_space=pl.ANY)
    vmem = pltpu.VMEM
    dma = pltpu.SemaphoreType.DMA
    consts = [jnp.asarray(table) for table in tables(patch)]
    lse, unmasked, stats = pl.pallas_call(
        functools.partial(kernel, tiles, orients, patch // 2),
        out_shape=[
            jax.ShapeDtypeStruct((share, side), F32),
            jax.ShapeDtypeStruct((share, side), F32),
            jax.ShapeDtypeStruct((everyone, 1, 128), F32),
        ],
        in_specs=[anywhere] * (5 + len(consts)),
        out_specs=[anywhere] * 3,
        scratch_shapes=[
            vmem((extent, side), F32),
            vmem(orient_ids.shape, jnp.int32),
            vmem((1, log_weight.shape[0]), F32),
            vmem(ice_mask.shape, jnp.int32),
            *[vmem(table.shape, BF16) for table in consts],
            vmem((2, extent // 2, patch), F32),
            vmem((2, extent // 2, patch), F32),
            vmem((tiles, patch + 8, patch), F32),
            vmem((blocks + 1, extent, patch), F32),
            vmem((blocks, blocks, 4 * patch, patch), F32),
            vmem((tiles, 4 * patch, patch), F32),
            vmem((tiles, blocks, blocks, patch, patch), F32),
            vmem((orients, share, side), F32),
            vmem((orients, share, side), F32),
            vmem((1, 128), F32),
            vmem((share, side), F32),
            dma((5 + len(consts),)),
            pltpu.SemaphoreType.REGULAR,
            dma((3,)),
            dma((2,)), dma((2,)),
            dma((tiles,)), dma((tiles,)),
            dma((orients,)), dma((orients,)),
            dma((everyone,)), dma((everyone,)),
        ],
        compiler_params=pltpu.CompilerParams(
            collective_id=0, has_side_effects=True, vmem_limit_bytes=56 * 1024 * 1024
        ),
    )(micrograph, templates, orient_ids, log_weight.reshape(1, -1), ice_mask, *consts)
    here = pl.BlockSpec(memory_space=pltpu.VMEM)
    return pl.pallas_call(
        finish,
        out_shape=jax.ShapeDtypeStruct((share, side), F32),
        in_specs=[here] * 3,
        out_specs=here,
        cost_estimate=pl.CostEstimate(flops=4 * share * side, bytes_accessed=12 * share * side, transcendentals=0),
    )(lse, unmasked, stats)


def solution(mesh):
    return jax.shard_map(
        functools.partial(body, mesh.shape["tile"], mesh.shape["orient"]),
        mesh=mesh,
        in_specs=(
            P("group", "tile"),
            P("orient", "tile", None, None),
            P("orient", "tile"),
            P(),
            P("group", "tile"),
        ),
        out_specs=P(("group", "orient"), "tile"),
        check_vma=False,
    )
```

```python
import functools
import math

import jax
import jax.numpy as jnp
import numpy as np
from jax import lax
from jax.experimental import pallas as pl
from jax.experimental.pallas import tpu as pltpu
from jax.sharding import PartitionSpec as P

MBLK = 16
F32 = jnp.float32
BF16 = jnp.bfloat16
MESH = pl.DeviceIdType.MESH


def halves(table, axis=0):
    table = table.astype(np.float32)
    high = table.astype(jnp.bfloat16)
    low = (table - high.astype(np.float32)).astype(jnp.bfloat16)
    return np.concatenate([high, low], axis=axis)


def tables(patch):
    length = 2 * patch
    n = np.arange(length)[:, None]
    k = np.arange(patch)[None, :]
    theta = 2 * math.pi * ((n * (2 * k + 1)) % (2 * length)) / (2 * length)
    tx = np.concatenate([np.cos(theta), -np.sin(theta)], axis=1)
    back = theta[:patch].T
    ix = np.concatenate([np.cos(back), -np.sin(back)], axis=0) * (2.0 / length)
    m = np.arange(length)
    phi = 2 * math.pi * ((m[:, None] * m[None, :]) % length) / length
    c, s = np.cos(phi), np.sin(phi)
    ty = np.block([[c, s], [-s, c]])
    cp, sp = c[:, :patch], s[:, :patch]
    tt = np.block([[cp, sp], [-sp, cp]])
    ci, si = c[:patch], s[:patch]
    iy = np.block([[ci, -si], [si, ci]]) / length
    return halves(tx), halves(ix, 1), halves(ty), halves(tt), halves(iy)


def split(value):
    high = value.astype(BF16)
    low = (value - high.astype(F32)).astype(BF16)
    return high, low


def dot(a, b):
    return jnp.dot(a, b, preferred_element_type=F32)


def left_table(table, high, low):
    rows = table.shape[0] // 2
    both = dot(table[...], high)
    return both[:rows] + both[rows:] + dot(table[:rows, :], low)


def right_table(value, table):
    depth = table.shape[0] // 2
    high, low = split(value)
    return dot(jnp.concatenate([high, high], axis=1), table[...]) + dot(low, table[:depth, :])


def right_wide(value, table):
    width = table.shape[1] // 2
    high, low = split(value)
    both = dot(high, table[...])
    return both[:, :width] + both[:, width:] + dot(low, table[:, :width])


def kernel(
    tiles, orients, guard,
    mic_any, tpl_any, ids_any, logw_any, mask_any, tx_any, ix_any, ty_any, tt_any, iy_any,
    lse_any, um_any, st_any,
    mic, ids, logw, mask, tx, ix, ty, tt, iy, pack, halo,
    stack, ext, img, spec, scores, lse_out, lse_in, stats, um,
    load_sem, ready, keep_sem,
    halo_send, halo_recv, tpl_send, tpl_recv, lse_send, lse_recv, st_send, st_recv,
):
    t = lax.axis_index("tile")
    o = lax.axis_index("orient")
    everyone = tiles * orients
    extent, side = mic.shape
    patch = tpl_any.shape[2]
    length = 2 * patch
    blocks = side // patch
    share = lse_any.shape[0]
    unrolled = everyone <= 16

    def partner(k):
        if tiles & (tiles - 1):
            return lax.rem(t + k, tiles)
        bit, peer = 1, 0
        while bit < tiles:
            peer = peer + lax.rem(t // bit + k // bit, 2) * bit
            bit *= 2
        return peer

    def seat_of(k):
        return {"tile": partner(k // orients), "orient": lax.rem(o + k % orients, orients)}

    def each_peer(body):
        if unrolled:
            for k in range(everyone - 1, 0, -1):
                body(k)
        else:
            def step(k, carry):
                body(k)
                return carry

            lax.fori_loop(1, everyone, step, 0)

    barrier = pltpu.get_barrier_semaphore()

    def announce(semaphore, first, last):
        def step(place, carry):
            for k in range(tiles):
                pl.semaphore_signal(
                    semaphore, inc=1, device_id={"tile": partner(k), "orient": place},
                    device_id_type=MESH,
                )
            return carry

        lax.fori_loop(first, last, step, 0)

    for k in range(1, tiles):
        pl.semaphore_signal(barrier, inc=1, device_id={"tile": partner(k)}, device_id_type=MESH)
    announce(barrier, o + 1, orients)

    sources = (
        ("tpl", tpl_any.at[0, 0], stack.at[0, pl.ds(0, patch)]),
        ("mic", mic_any, mic),
        ("ids", ids_any, ids),
        ("logw", logw_any, logw),
        ("tx", tx_any, tx),
        ("tt", tt_any, tt),
        ("ty", ty_any, ty),
        ("iy", iy_any, iy),
        ("ix", ix_any, ix),
        ("mask", mask_any, mask),
    )
    loads = {}
    for index, (name, source, target) in enumerate(sources):
        loads[name] = pltpu.make_async_copy(source, target, load_sem.at[index])
        loads[name].start()

    loads["ids"].wait()
    loads["logw"].wait()
    known = lax.broadcasted_iota(jnp.int32, (1, logw.shape[1]), 1) == ids[...]
    weight_here = jnp.sum(jnp.where(known, logw[...], 0.0), axis=1, keepdims=True)
    stack[0, patch:, :] = jnp.broadcast_to(weight_here, (stack.shape[1] - patch, patch))

    loads["mic"].wait()
    middle = extent // 2
    lane_half = lax.broadcasted_iota(jnp.int32, (middle, patch), 1) < guard
    outer, inner = mic[:, side - patch:], mic[:, :patch]
    pack[1] = jnp.where(lane_half, pltpu.roll(outer[:middle], guard, 1), outer[middle:])
    pack[0] = jnp.where(lane_half, inner[:middle], pltpu.roll(inner[middle:], guard, 1))
    loads["tpl"].wait()

    pl.semaphore_wait(barrier, tiles - 1 + tiles * o)

    def halo_copy(place, peer):
        return pltpu.make_async_remote_copy(
            src_ref=pack.at[place], dst_ref=halo.at[1 - place], send_sem=halo_send.at[place],
            recv_sem=halo_recv.at[1 - place], device_id={"tile": peer}, device_id_type=MESH,
        )

    to_left = halo_copy(0, lax.rem(t + tiles - 1, tiles))
    to_right = halo_copy(1, lax.rem(t + 1, tiles))

    def tpl_copy(k):
        return pltpu.make_async_remote_copy(
            src_ref=stack.at[0], dst_ref=stack.at[k], send_sem=tpl_send.at[k],
            recv_sem=tpl_recv.at[k], device_id={"tile": partner(k)}, device_id_type=MESH,
        )

    @pl.when(t > 0)
    def _():
        to_left.start()

    @pl.when(t < tiles - 1)
    def _():
        to_right.start()

    for k in range(1, tiles):
        tpl_copy(k).start()

    announce(ready, 0, o)

    loads["tx"].wait()
    loads["tt"].wait()

    def spectra(first, many):
        value = stack[pl.ds(first, many), :patch, :].reshape(many * patch, patch)
        high, low = split(value)
        top = tx[:patch, :]
        half = dot(jnp.concatenate([high, low], axis=1), jnp.concatenate([top, top], axis=0))
        half = half + dot(high, tx[length:length + patch, :])
        high, low = split(half)

        def stacked(part):
            return jnp.concatenate(
                [
                    jnp.concatenate(
                        [part[j * patch:(j + 1) * patch, :patch], part[j * patch:(j + 1) * patch, patch:]],
                        axis=0,
                    )
                    for j in range(many)
                ],
                axis=1,
            )

        whole = left_table(tt, stacked(high), stacked(low))
        for j in range(many):
            spec[first + j] = whole[:, j * patch:(j + 1) * patch]

    spectra(0, 1)

    rolled = [pltpu.roll(mic[:, b * patch:(b + 1) * patch], guard, 1) for b in range(blocks)]
    lane = lax.broadcasted_iota(jnp.int32, (extent, patch), 1)
    ext[0] = rolled[0]
    for b in range(1, blocks):
        ext[b] = jnp.where(lane < guard, rolled[b - 1], rolled[b])
    ext[blocks] = rolled[blocks - 1]

    def receive(place):
        present = (t > 0) if place == 0 else (t < tiles - 1)

        @pl.when(present)
        def _():
            halo_copy(1 - place, t).wait_recv()

        @pl.when(jnp.logical_not(present))
        def _():
            halo[place] = jnp.zeros(halo.shape[1:], F32)

        got = halo[place]
        turned = pltpu.roll(got, guard, 1)
        near = lax.broadcasted_iota(jnp.int32, (middle, patch), 1) < guard
        edge = 0 if place == 0 else blocks
        if place == 0:
            ext[edge, :middle] = jnp.where(near, got, ext[edge, :middle])
            ext[edge, middle:] = jnp.where(near, turned, ext[edge, middle:])
        else:
            ext[edge, :middle] = jnp.where(near, ext[edge, :middle], turned)
            ext[edge, middle:] = jnp.where(near, ext[edge, middle:], got)

    def image(b):
        half = right_table(jnp.concatenate([ext[b], ext[b + 1]], axis=1), tx)
        high, low = split(half)

        def stacked(part):
            return jnp.concatenate(
                [
                    jnp.concatenate(
                        [part[a * patch:a * patch + length, :patch], part[a * patch:a * patch + length, patch:]],
                        axis=0,
                    )
                    for a in range(blocks)
                ],
                axis=1,
            )

        whole = left_table(ty, stacked(high), stacked(low))
        for a in range(blocks):
            img[b, a] = whole[:, a * patch:(a + 1) * patch]

    def correlate(items):
        highs, lows = [], []
        for k, a, b in items:
            sr, si = spec[k, :length], spec[k, length:]
            ir, ii = img[b, a, :length], img[b, a, length:]
            cross = jnp.concatenate([ir * sr + ii * si, ii * sr - ir * si], axis=0)
            high, low = split(cross)
            highs.append(high)
            lows.append(low)
        mid = left_table(iy, jnp.concatenate(highs, axis=1), jnp.concatenate(lows, axis=1))
        pieces = jnp.concatenate(
            [
                jnp.concatenate(
                    [mid[:patch, i * patch:(i + 1) * patch], mid[patch:, i * patch:(i + 1) * patch]],
                    axis=1,
                )
                for i in range(len(items))
            ],
            axis=0,
        )
        final = right_wide(pieces, ix)
        for i, (k, a, b) in enumerate(items):
            scores[k, a, b] = final[i * patch:(i + 1) * patch] + stack[k, patch:, :][:1, :1]

    tpl_copy(1).wait_recv()
    spectra(1, 1)
    loads["ty"].wait()
    loads["ix"].wait()
    loads["iy"].wait()
    odd = lax.rem(t, 2)

    def column(i, carry):
        place = lax.rem(i + 1 + odd, 2)

        @pl.when(place == 0)
        def _():
            receive(0)

        @pl.when(place == 1)
        def _():
            receive(1)

        image(place)
        return carry

    lax.fori_loop(0, 2, column, 0)

    def pairs(body):
        if tiles == 4:
            body(2)
        elif tiles > 4:
            def step(p, carry):
                body(2 * p)
                return carry

            lax.fori_loop(1, tiles // 2, step, 0)

    def own_lse(a, place):
        rows = pl.ds(pl.multiple_of(place * share, share), share)
        parts = []
        for b in range(blocks):
            top = scores[0, a, b, rows, :]
            for k in range(1, tiles):
                top = jnp.maximum(top, scores[k, a, b, rows, :])
            total = jnp.exp(scores[0, a, b, rows, :] - top)
            for k in range(1, tiles):
                total = total + jnp.exp(scores[k, a, b, rows, :] - top)
            parts.append(top + jnp.log(total))
        return jnp.concatenate(parts, axis=1)

    def lse_copy(k):
        return pltpu.make_async_remote_copy(
            src_ref=lse_out.at[k], dst_ref=lse_in.at[k], send_sem=lse_send.at[k],
            recv_sem=lse_recv.at[k], device_id={"orient": lax.rem(o + k, orients)},
            device_id_type=MESH,
        )

    owners = patch // share
    home, seat = o // owners, lax.rem(o, owners)

    def far_spectra():
        for k in range(2, tiles):
            tpl_copy(k).wait_recv()
        pairs(lambda k: spectra(k, 2))

        @pl.when(o < orients - 1)
        def _():
            pl.semaphore_wait(ready, tiles * (orients - 1 - o))

    def cell(j, carry):
        first = lax.rem(j, tiles // 2) * 2
        a = lax.rem(home + 1 + j // (tiles // 2), blocks)

        @pl.when(j == 1)
        def _():
            far_spectra()

        correlate([(first + q, a, b) for q in range(2) for b in range(blocks)])

        @pl.when(first == tiles - 2)
        def _():
            def send(gap, inner):
                place = lax.rem(seat + gap, owners)
                ahead = lax.rem(a * owners + place - o + orients, orients)
                lse_out[ahead] = own_lse(a, place)

                @pl.when(ahead > 0)
                def _():
                    lse_copy(ahead).start()

                return inner

            lax.fori_loop(1, owners + 1, send, 0)

        return carry

    lax.fori_loop(0, blocks * (tiles // 2), cell, 0)
    loads["mask"].wait()
    mask_rows, mask_cols = mask.shape
    row_id = lax.broadcasted_iota(jnp.int32, (share, mask_rows), 0) + o * share
    pick = lax.broadcasted_iota(jnp.int32, (share, mask_rows), 1)
    low_edge = pick * MBLK
    rows_of = jnp.where((row_id >= low_edge) & (row_id < low_edge + MBLK), 1.0, 0.0).astype(F32)
    col_id = lax.broadcasted_iota(jnp.int32, (mask_cols, side), 1)
    col_edge = lax.broadcasted_iota(jnp.int32, (mask_cols, side), 0) * MBLK
    cols_of = jnp.where((col_id >= col_edge) & (col_id < col_edge + MBLK), 1.0, 0.0).astype(F32)
    unmasked = 1.0 - dot(dot(rows_of, mask[...].astype(F32)), cols_of)

    def whole_sum(value):
        return jnp.sum(jnp.sum(value, axis=0, keepdims=True), axis=1, keepdims=True)

    count = whole_sum(unmasked)
    um[...] = unmasked
    keep_um = pltpu.make_async_copy(um, um_any, keep_sem.at[0])
    keep_um.start()

    mine = lse_out[0]
    for k in range(1, orients):
        lse_copy(k).wait_recv()
    top = mine
    for k in range(1, orients):
        top = jnp.maximum(top, lse_in[k])
    total = jnp.exp(mine - top)
    for k in range(1, orients):
        total = total + jnp.exp(lse_in[k] - top)
    lse = top + jnp.log(total)

    sum_here = whole_sum(unmasked * lse)
    mean_here = sum_here / jnp.maximum(count, 1.0)
    deviation = lse - mean_here
    squares = whole_sum(unmasked * deviation * deviation)
    slot = lax.broadcasted_iota(jnp.int32, stats.shape, 1)
    stats[...] = jnp.where(
        slot == 0, count, jnp.where(slot == 1, sum_here, jnp.where(slot == 2, squares, 0.0))
    )

    def st_copy(k):
        return pltpu.make_async_remote_copy(
            src_ref=stats, dst_ref=st_any.at[k], send_sem=st_send.at[k],
            recv_sem=st_recv.at[k], device_id=seat_of(k), device_id_type=MESH,
        )

    each_peer(lambda k: st_copy(k).start())
    lse_in[0] = lse
    keep_lse = pltpu.make_async_copy(lse_in.at[0], lse_any, keep_sem.at[1])
    keep_lse.start()
    keep_st = pltpu.make_async_copy(stats, st_any.at[0], keep_sem.at[2])
    keep_st.start()

    @pl.when(t > 0)
    def _():
        to_left.wait_send()

    @pl.when(t < tiles - 1)
    def _():
        to_right.wait_send()

    for k in range(1, tiles):
        tpl_copy(k).wait_send()
    for k in range(1, orients):
        lse_copy(k).wait_send()
    each_peer(lambda k: st_copy(k).wait())
    keep_um.wait()
    keep_lse.wait()
    keep_st.wait()


def finish(lse, unmasked, stats, out):
    table = stats[:, 0, :]
    counts, sums, sqs = table[:, 0:1], table[:, 1:2], table[:, 2:3]
    live = jnp.sum(counts, axis=0, keepdims=True)
    average = jnp.sum(sums, axis=0, keepdims=True) / live
    gap = sums / jnp.maximum(counts, 1.0) - average
    variance = jnp.sum(sqs + counts * gap * gap, axis=0, keepdims=True) / live
    out[...] = unmasked[...] * (lse[...] - average) / jnp.sqrt(variance + 1e-05)


def body(tiles, orients, micrograph, templates, orient_ids, log_weight, ice_mask):
    extent, side = micrograph.shape
    patch = templates.shape[2]
    share = side // orients
    blocks = side // patch
    everyone = tiles * orients
    anywhere = pl.BlockSpec(memory_space=pl.ANY)
    vmem = pltpu.VMEM
    dma = pltpu.SemaphoreType.DMA
    consts = [jnp.asarray(table) for table in tables(patch)]
    lse, unmasked, stats = pl.pallas_call(
        functools.partial(kernel, tiles, orients, patch // 2),
        out_shape=[
            jax.ShapeDtypeStruct((share, side), F32),
            jax.ShapeDtypeStruct((share, side), F32),
            jax.ShapeDtypeStruct((everyone, 1, 128), F32),
        ],
        in_specs=[anywhere] * (5 + len(consts)),
        out_specs=[anywhere] * 3,
        scratch_shapes=[
            vmem((extent, side), F32),
            vmem(orient_ids.shape, jnp.int32),
            vmem((1, log_weight.shape[0]), F32),
            vmem(ice_mask.shape, jnp.int32),
            *[vmem(table.shape, BF16) for table in consts],
            vmem((2, extent // 2, patch), F32),
            vmem((2, extent // 2, patch), F32),
            vmem((tiles, patch + 8, patch), F32),
            vmem((blocks + 1, extent, patch), F32),
            vmem((blocks, blocks, 4 * patch, patch), F32),
            vmem((tiles, 4 * patch, patch), F32),
            vmem((tiles, blocks, blocks, patch, patch), F32),
            vmem((orients, share, side), F32),
            vmem((orients, share, side), F32),
            vmem((1, 128), F32),
            vmem((share, side), F32),
            dma((5 + len(consts),)),
            pltpu.SemaphoreType.REGULAR,
            dma((3,)),
            dma((2,)), dma((2,)),
            dma((tiles,)), dma((tiles,)),
            dma((orients,)), dma((orients,)),
            dma((everyone,)), dma((everyone,)),
        ],
        compiler_params=pltpu.CompilerParams(
            collective_id=0, has_side_effects=True, vmem_limit_bytes=56 * 1024 * 1024
        ),
    )(micrograph, templates, orient_ids, log_weight.reshape(1, -1), ice_mask, *consts)
    here = pl.BlockSpec(memory_space=pltpu.VMEM)
    return pl.pallas_call(
        finish,
        out_shape=jax.ShapeDtypeStruct((share, side), F32),
        in_specs=[here] * 3,
        out_specs=here,
        cost_estimate=pl.CostEstimate(flops=4 * share * side, bytes_accessed=12 * share * side, transcendentals=0),
    )(lse, unmasked, stats)


def solution(mesh):
    return jax.shard_map(
        functools.partial(body, mesh.shape["tile"], mesh.shape["orient"]),
        mesh=mesh,
        in_specs=(
            P("group", "tile"),
            P("orient", "tile", None, None),
            P("orient", "tile"),
            P(),
            P("group", "tile"),
        ),
        out_specs=P(("group", "orient"), "tile"),
        check_vma=False,
    )
```

```python
import functools
import math

import jax
import jax.numpy as jnp
import numpy as np
from jax import lax
from jax.experimental import pallas as pl
from jax.experimental.pallas import tpu as pltpu
from jax.sharding import PartitionSpec as P

MBLK = 16
F32 = jnp.float32
BF16 = jnp.bfloat16
MESH = pl.DeviceIdType.MESH


def halves(table, axis=0):
    table = table.astype(np.float32)
    high = table.astype(jnp.bfloat16)
    low = (table - high.astype(np.float32)).astype(jnp.bfloat16)
    return np.concatenate([high, low], axis=axis)


def tables(patch):
    length = 2 * patch
    n = np.arange(length)[:, None]
    k = np.arange(patch)[None, :]
    theta = 2 * math.pi * ((n * (2 * k + 1)) % (2 * length)) / (2 * length)
    tx = np.concatenate([np.cos(theta), -np.sin(theta)], axis=1)
    back = theta[:patch].T
    ix = np.concatenate([np.cos(back), -np.sin(back)], axis=0) * (2.0 / length)
    m = np.arange(length)
    phi = 2 * math.pi * ((m[:, None] * m[None, :]) % length) / length
    c, s = np.cos(phi), np.sin(phi)
    ty = np.block([[c, s], [-s, c]])
    cp, sp = c[:, :patch], s[:, :patch]
    tt = np.block([[cp, sp], [-sp, cp]])
    ci, si = c[:patch], s[:patch]
    iy = np.block([[ci, -si], [si, ci]]) / length
    return halves(tx), halves(ix, 1), halves(ty), halves(tt), halves(iy)


def split(value):
    high = value.astype(BF16)
    low = (value - high.astype(F32)).astype(BF16)
    return high, low


def dot(a, b):
    return jnp.dot(a, b, preferred_element_type=F32)


def left_table(table, high, low):
    rows = table.shape[0] // 2
    both = dot(table[...], high)
    return both[:rows] + both[rows:] + dot(table[:rows, :], low)


def right_table(value, table):
    depth = table.shape[0] // 2
    high, low = split(value)
    return dot(jnp.concatenate([high, high], axis=1), table[...]) + dot(low, table[:depth, :])


def right_wide(value, table):
    width = table.shape[1] // 2
    high, low = split(value)
    both = dot(high, table[...])
    return both[:, :width] + both[:, width:] + dot(low, table[:, :width])


def kernel(
    tiles, orients, guard,
    mic_any, tpl_any, ids_any, logw_any, mask_any, tx_any, ix_any, ty_any, tt_any, iy_any,
    lse_any, um_any, st_any,
    mic, ids, logw, mask, tx, ix, ty, tt, iy, pack, halo,
    stack, ext, img, spec, scores, lse_out, lse_in, relay_in, stats, um,
    load_sem, ready, keep_sem, relay_sem,
    halo_send, halo_recv, tpl_send, tpl_recv, lse_send, lse_recv, st_send, st_recv,
):
    t = lax.axis_index("tile")
    o = lax.axis_index("orient")
    everyone = tiles * orients
    extent, side = mic.shape
    patch = tpl_any.shape[2]
    length = 2 * patch
    blocks = side // patch
    share = lse_any.shape[0]
    unrolled = everyone <= 16

    def partner(k):
        if tiles & (tiles - 1):
            return lax.rem(t + k, tiles)
        bit, peer = 1, 0
        while bit < tiles:
            peer = peer + lax.rem(t // bit + k // bit, 2) * bit
            bit *= 2
        return peer

    def seat_of(k):
        return {"tile": partner(k // orients), "orient": lax.rem(o + k % orients, orients)}

    def each_peer(body):
        if unrolled:
            for k in range(everyone - 1, 0, -1):
                body(k)
        else:
            def step(k, carry):
                body(k)
                return carry

            lax.fori_loop(1, everyone, step, 0)

    barrier = pltpu.get_barrier_semaphore()

    def announce(semaphore, first, last):
        def step(place, carry):
            for k in range(tiles):
                pl.semaphore_signal(
                    semaphore, inc=1, device_id={"tile": partner(k), "orient": place},
                    device_id_type=MESH,
                )
            return carry

        lax.fori_loop(first, last, step, 0)

    for k in range(1, tiles):
        pl.semaphore_signal(barrier, inc=1, device_id={"tile": partner(k)}, device_id_type=MESH)
    announce(barrier, o + 1, orients)

    sources = (
        ("tpl", tpl_any.at[0, 0], stack.at[0, pl.ds(0, patch)]),
        ("mic", mic_any, mic),
        ("ids", ids_any, ids),
        ("logw", logw_any, logw),
        ("tx", tx_any, tx),
        ("tt", tt_any, tt),
        ("ty", ty_any, ty),
        ("iy", iy_any, iy),
        ("ix", ix_any, ix),
        ("mask", mask_any, mask),
    )
    loads = {
        name: pltpu.make_async_copy(source, target, load_sem.at[index])
        for index, (name, source, target) in enumerate(sources)
    }
    for name in ("tpl", "mic", "ids", "logw", "tx", "tt"):
        loads[name].start()

    loads["ids"].wait()
    loads["logw"].wait()
    known = lax.broadcasted_iota(jnp.int32, (1, logw.shape[1]), 1) == ids[...]
    weight_here = jnp.sum(jnp.where(known, logw[...], 0.0), axis=1, keepdims=True)
    stack[0, patch:, :] = jnp.broadcast_to(weight_here, (stack.shape[1] - patch, patch))

    loads["mic"].wait()
    middle = extent // 2
    lane_half = lax.broadcasted_iota(jnp.int32, (middle, patch), 1) < guard
    outer, inner = mic[:, side - patch:], mic[:, :patch]
    pack[1] = jnp.where(lane_half, pltpu.roll(outer[:middle], guard, 1), outer[middle:])
    pack[0] = jnp.where(lane_half, inner[:middle], pltpu.roll(inner[middle:], guard, 1))
    loads["tpl"].wait()

    pl.semaphore_wait(barrier, tiles - 1 + tiles * o)

    def halo_copy(place, peer):
        return pltpu.make_async_remote_copy(
            src_ref=pack.at[place], dst_ref=halo.at[1 - place], send_sem=halo_send.at[place],
            recv_sem=halo_recv.at[1 - place], device_id={"tile": peer}, device_id_type=MESH,
        )

    to_left = halo_copy(0, lax.rem(t + tiles - 1, tiles))
    to_right = halo_copy(1, lax.rem(t + 1, tiles))

    def tpl_copy(k):
        return pltpu.make_async_remote_copy(
            src_ref=stack.at[0], dst_ref=stack.at[k], send_sem=tpl_send.at[k],
            recv_sem=tpl_recv.at[k], device_id={"tile": partner(k)}, device_id_type=MESH,
        )

    @pl.when(t > 0)
    def _():
        to_left.start()

    @pl.when(t < tiles - 1)
    def _():
        to_right.start()

    for k in range(1, tiles):
        tpl_copy(k).start()

    for name in ("ty", "iy", "ix", "mask"):
        loads[name].start()

    loads["tx"].wait()
    loads["tt"].wait()

    def spectra(first, many):
        value = stack[pl.ds(first, many), :patch, :].reshape(many * patch, patch)
        high, low = split(value)
        top = tx[:patch, :]
        half = dot(jnp.concatenate([high, low], axis=1), jnp.concatenate([top, top], axis=0))
        half = half + dot(high, tx[length:length + patch, :])
        high, low = split(half)

        def stacked(part):
            return jnp.concatenate(
                [
                    jnp.concatenate(
                        [part[j * patch:(j + 1) * patch, :patch], part[j * patch:(j + 1) * patch, patch:]],
                        axis=0,
                    )
                    for j in range(many)
                ],
                axis=1,
            )

        whole = left_table(tt, stacked(high), stacked(low))
        for j in range(many):
            spec[first + j] = whole[:, j * patch:(j + 1) * patch]

    spectra(0, 1)

    rolled = [pltpu.roll(mic[:, b * patch:(b + 1) * patch], guard, 1) for b in range(blocks)]
    lane = lax.broadcasted_iota(jnp.int32, (extent, patch), 1)
    ext[0] = rolled[0]
    for b in range(1, blocks):
        ext[b] = jnp.where(lane < guard, rolled[b - 1], rolled[b])
    ext[blocks] = rolled[blocks - 1]

    def receive(place):
        present = (t > 0) if place == 0 else (t < tiles - 1)

        @pl.when(present)
        def _():
            halo_copy(1 - place, t).wait_recv()

        @pl.when(jnp.logical_not(present))
        def _():
            halo[place] = jnp.zeros(halo.shape[1:], F32)

        got = halo[place]
        turned = pltpu.roll(got, guard, 1)
        near = lax.broadcasted_iota(jnp.int32, (middle, patch), 1) < guard
        edge = 0 if place == 0 else blocks
        if place == 0:
            ext[edge, :middle] = jnp.where(near, got, ext[edge, :middle])
            ext[edge, middle:] = jnp.where(near, turned, ext[edge, middle:])
        else:
            ext[edge, :middle] = jnp.where(near, ext[edge, :middle], turned)
            ext[edge, middle:] = jnp.where(near, ext[edge, middle:], got)

    def image(b):
        half = right_table(jnp.concatenate([ext[b], ext[b + 1]], axis=1), tx)
        high, low = split(half)

        def stacked(part):
            return jnp.concatenate(
                [
                    jnp.concatenate(
                        [part[a * patch:a * patch + length, :patch], part[a * patch:a * patch + length, patch:]],
                        axis=0,
                    )
                    for a in range(blocks)
                ],
                axis=1,
            )

        whole = left_table(ty, stacked(high), stacked(low))
        for a in range(blocks):
            img[b, a] = whole[:, a * patch:(a + 1) * patch]

    def correlate(items):
        highs, lows = [], []
        for k, a, b in items:
            sr, si = spec[k, :length], spec[k, length:]
            ir, ii = img[b, a, :length], img[b, a, length:]
            cross = jnp.concatenate([ir * sr + ii * si, ii * sr - ir * si], axis=0)
            high, low = split(cross)
            highs.append(high)
            lows.append(low)
        mid = left_table(iy, jnp.concatenate(highs, axis=1), jnp.concatenate(lows, axis=1))
        pieces = jnp.concatenate(
            [
                jnp.concatenate(
                    [mid[:patch, i * patch:(i + 1) * patch], mid[patch:, i * patch:(i + 1) * patch]],
                    axis=1,
                )
                for i in range(len(items))
            ],
            axis=0,
        )
        final = right_wide(pieces, ix)
        for i, (k, a, b) in enumerate(items):
            scores[k, a, b] = final[i * patch:(i + 1) * patch] + stack[k, patch:, :][:1, :1]

    tpl_copy(1).wait_recv()
    spectra(1, 1)
    loads["ty"].wait()
    loads["ix"].wait()
    loads["iy"].wait()
    odd = lax.rem(t, 2)

    def column(i, carry):
        place = lax.rem(i + 1 + odd, 2)

        @pl.when(i == 1)
        def _():
            announce(ready, 0, o)

        @pl.when(place == 0)
        def _():
            receive(0)

        @pl.when(place == 1)
        def _():
            receive(1)

        image(place)
        return carry

    lax.fori_loop(0, 2, column, 0)

    def pairs(body):
        if tiles == 4:
            body(2)
        elif tiles > 4:
            def step(p, carry):
                body(2 * p)
                return carry

            lax.fori_loop(1, tiles // 2, step, 0)

    def own_lse(a, place):
        rows = pl.ds(pl.multiple_of(place * share, share), share)
        parts = []
        for b in range(blocks):
            top = scores[0, a, b, rows, :]
            for k in range(1, tiles):
                top = jnp.maximum(top, scores[k, a, b, rows, :])
            total = jnp.exp(scores[0, a, b, rows, :] - top)
            for k in range(1, tiles):
                total = total + jnp.exp(scores[k, a, b, rows, :] - top)
            parts.append(top + jnp.log(total))
        return jnp.concatenate(parts, axis=1)

    def lse_copy(k):
        return pltpu.make_async_remote_copy(
            src_ref=lse_out.at[k], dst_ref=lse_in.at[k], send_sem=lse_send.at[k],
            recv_sem=lse_recv.at[k], device_id={"orient": lax.rem(o + k, orients)},
            device_id_type=MESH,
        )

    relayed = orients == 4
    outer = lax.rem(o, 3) == 0
    held = 2 * o - 1
    relay = pltpu.make_async_remote_copy(
        src_ref=lse_out.at[2], dst_ref=relay_in, send_sem=relay_sem.at[0], recv_sem=relay_sem.at[1],
        device_id={"orient": o + 1 - 2 * lax.rem(o, 2)}, device_id_type=MESH,
    ) if relayed else None
    owners = patch // share
    home, seat = o // owners, lax.rem(o, owners)

    def far_spectra():
        for k in range(2, tiles):
            tpl_copy(k).wait_recv()
        pairs(lambda k: spectra(k, 2))

        @pl.when(o < orients - 1)
        def _():
            pl.semaphore_wait(ready, tiles * (orients - 1 - o))

    def cell(j, carry):
        first = lax.rem(j, tiles // 2) * 2
        a = lax.rem(home + 1 + j // (tiles // 2), blocks)

        @pl.when(j == 1)
        def _():
            far_spectra()

        correlate([(first + q, a, b) for q in range(2) for b in range(blocks)])

        @pl.when(first == tiles - 2)
        def _():
            far = jnp.where(a == home, 0, owners - 1)

            def send(gap, inner):
                place = lax.rem(seat + gap + far, owners)
                ahead = lax.rem(a * owners + place - o + orients, orients)
                lse_out[ahead] = own_lse(a, place)

                direct = ahead > 0
                if relayed:
                    direct = direct & jnp.where(outer, ahead != 2, ahead != held)

                    @pl.when(outer & (ahead == 2))
                    def _():
                        relay.start()

                @pl.when(direct)
                def _():
                    lse_copy(ahead).start()

                return inner

            lax.fori_loop(1, owners + 1, send, 0)

        return carry

    lax.fori_loop(0, blocks * (tiles // 2), cell, 0)

    if relayed:
        @pl.when(jnp.logical_not(outer))
        def _():
            relay.wait_recv()
            ours, theirs = lse_out[held], relay_in[...]
            most = jnp.maximum(ours, theirs)
            lse_out[held] = most + jnp.log(jnp.exp(ours - most) + jnp.exp(theirs - most))
            lse_copy(held).start()
            lse_in[2] = jnp.full(lse_in.shape[1:], -1e30, F32)

    loads["mask"].wait()
    mask_rows, mask_cols = mask.shape
    row_id = lax.broadcasted_iota(jnp.int32, (share, mask_rows), 0) + o * share
    pick = lax.broadcasted_iota(jnp.int32, (share, mask_rows), 1)
    low_edge = pick * MBLK
    rows_of = jnp.where((row_id >= low_edge) & (row_id < low_edge + MBLK), 1.0, 0.0).astype(F32)
    col_id = lax.broadcasted_iota(jnp.int32, (mask_cols, side), 1)
    col_edge = lax.broadcasted_iota(jnp.int32, (mask_cols, side), 0) * MBLK
    cols_of = jnp.where((col_id >= col_edge) & (col_id < col_edge + MBLK), 1.0, 0.0).astype(F32)
    unmasked = 1.0 - dot(dot(rows_of, mask[...].astype(F32)), cols_of)

    def whole_sum(value):
        return jnp.sum(jnp.sum(value, axis=0, keepdims=True), axis=1, keepdims=True)

    count = whole_sum(unmasked)
    um[...] = unmasked
    keep_um = pltpu.make_async_copy(um, um_any, keep_sem.at[0])
    keep_um.start()

    mine = lse_out[0]
    for k in range(1, orients):
        if relayed and k == 2:
            @pl.when(outer)
            def _():
                lse_copy(2).wait_recv()
        else:
            lse_copy(k).wait_recv()
    top = mine
    for k in range(1, orients):
        top = jnp.maximum(top, lse_in[k])
    total = jnp.exp(mine - top)
    for k in range(1, orients):
        total = total + jnp.exp(lse_in[k] - top)
    lse = top + jnp.log(total)

    sum_here = whole_sum(unmasked * lse)
    mean_here = sum_here / jnp.maximum(count, 1.0)
    deviation = lse - mean_here
    squares = whole_sum(unmasked * deviation * deviation)
    slot = lax.broadcasted_iota(jnp.int32, stats.shape, 1)
    stats[...] = jnp.where(
        slot == 0, count, jnp.where(slot == 1, sum_here, jnp.where(slot == 2, squares, 0.0))
    )

    def st_copy(k):
        return pltpu.make_async_remote_copy(
            src_ref=stats, dst_ref=st_any.at[k], send_sem=st_send.at[k],
            recv_sem=st_recv.at[k], device_id=seat_of(k), device_id_type=MESH,
        )

    each_peer(lambda k: st_copy(k).start())
    lse_in[0] = lse
    keep_lse = pltpu.make_async_copy(lse_in.at[0], lse_any, keep_sem.at[1])
    keep_lse.start()
    keep_st = pltpu.make_async_copy(stats, st_any.at[0], keep_sem.at[2])
    keep_st.start()

    @pl.when(t > 0)
    def _():
        to_left.wait_send()

    @pl.when(t < tiles - 1)
    def _():
        to_right.wait_send()

    for k in range(1, tiles):
        tpl_copy(k).wait_send()
    for k in range(1, orients):
        if relayed and k == 2:
            @pl.when(outer)
            def _():
                relay.wait_send()

            @pl.when(jnp.logical_not(outer))
            def _():
                lse_copy(2).wait_send()
        else:
            lse_copy(k).wait_send()
    each_peer(lambda k: st_copy(k).wait())
    keep_um.wait()
    keep_lse.wait()
    keep_st.wait()


def finish(lse, unmasked, stats, out):
    table = stats[:, 0, :]
    counts, sums, sqs = table[:, 0:1], table[:, 1:2], table[:, 2:3]
    live = jnp.sum(counts, axis=0, keepdims=True)
    average = jnp.sum(sums, axis=0, keepdims=True) / live
    gap = sums / jnp.maximum(counts, 1.0) - average
    variance = jnp.sum(sqs + counts * gap * gap, axis=0, keepdims=True) / live
    out[...] = unmasked[...] * (lse[...] - average) / jnp.sqrt(variance + 1e-05)


def body(tiles, orients, micrograph, templates, orient_ids, log_weight, ice_mask):
    extent, side = micrograph.shape
    patch = templates.shape[2]
    share = side // orients
    blocks = side // patch
    everyone = tiles * orients
    anywhere = pl.BlockSpec(memory_space=pl.ANY)
    vmem = pltpu.VMEM
    dma = pltpu.SemaphoreType.DMA
    consts = [jnp.asarray(table) for table in tables(patch)]
    lse, unmasked, stats = pl.pallas_call(
        functools.partial(kernel, tiles, orients, patch // 2),
        out_shape=[
            jax.ShapeDtypeStruct((share, side), F32),
            jax.ShapeDtypeStruct((share, side), F32),
            jax.ShapeDtypeStruct((everyone, 1, 128), F32),
        ],
        in_specs=[anywhere] * (5 + len(consts)),
        out_specs=[anywhere] * 3,
        scratch_shapes=[
            vmem((extent, side), F32),
            vmem(orient_ids.shape, jnp.int32),
            vmem((1, log_weight.shape[0]), F32),
            vmem(ice_mask.shape, jnp.int32),
            *[vmem(table.shape, BF16) for table in consts],
            vmem((2, extent // 2, patch), F32),
            vmem((2, extent // 2, patch), F32),
            vmem((tiles, patch + 8, patch), F32),
            vmem((blocks + 1, extent, patch), F32),
            vmem((blocks, blocks, 4 * patch, patch), F32),
            vmem((tiles, 4 * patch, patch), F32),
            vmem((tiles, blocks, blocks, patch, patch), F32),
            vmem((orients, share, side), F32),
            vmem((orients, share, side), F32),
            vmem((share, side), F32),
            vmem((1, 128), F32),
            vmem((share, side), F32),
            dma((5 + len(consts),)),
            pltpu.SemaphoreType.REGULAR,
            dma((3,)),
            dma((2,)),
            dma((2,)), dma((2,)),
            dma((tiles,)), dma((tiles,)),
            dma((orients,)), dma((orients,)),
            dma((everyone,)), dma((everyone,)),
        ],
        compiler_params=pltpu.CompilerParams(
            collective_id=0, has_side_effects=True, vmem_limit_bytes=56 * 1024 * 1024
        ),
    )(micrograph, templates, orient_ids, log_weight.reshape(1, -1), ice_mask, *consts)
    here = pl.BlockSpec(memory_space=pltpu.VMEM)
    return pl.pallas_call(
        finish,
        out_shape=jax.ShapeDtypeStruct((share, side), F32),
        in_specs=[here] * 3,
        out_specs=here,
        cost_estimate=pl.CostEstimate(flops=4 * share * side, bytes_accessed=12 * share * side, transcendentals=0),
    )(lse, unmasked, stats)


def solution(mesh):
    return jax.shard_map(
        functools.partial(body, mesh.shape["tile"], mesh.shape["orient"]),
        mesh=mesh,
        in_specs=(
            P("group", "tile"),
            P("orient", "tile", None, None),
            P("orient", "tile"),
            P(),
            P("group", "tile"),
        ),
        out_specs=P(("group", "orient"), "tile"),
        check_vma=False,
    )
```

```python
import functools
import math

import jax
import jax.numpy as jnp
import numpy as np
from jax import lax
from jax.experimental import pallas as pl
from jax.experimental.pallas import tpu as pltpu
from jax.sharding import PartitionSpec as P

MBLK = 16
F32 = jnp.float32
BF16 = jnp.bfloat16
MESH = pl.DeviceIdType.MESH


def halves(table, axis=0):
    table = table.astype(np.float32)
    high = table.astype(jnp.bfloat16)
    low = (table - high.astype(np.float32)).astype(jnp.bfloat16)
    return np.concatenate([high, low], axis=axis)


def tables(patch):
    length = 2 * patch
    n = np.arange(length)[:, None]
    k = np.arange(patch)[None, :]
    theta = 2 * math.pi * ((n * (2 * k + 1)) % (2 * length)) / (2 * length)
    tx = np.concatenate([np.cos(theta), -np.sin(theta)], axis=1)
    back = theta[:patch].T
    ix = np.concatenate([np.cos(back), -np.sin(back)], axis=0) * (2.0 / length)
    m = np.arange(length)
    phi = 2 * math.pi * ((m[:, None] * m[None, :]) % length) / length
    c, s = np.cos(phi), np.sin(phi)
    ty = np.block([[c, s], [-s, c]])
    cp, sp = c[:, :patch], s[:, :patch]
    tt = np.block([[cp, sp], [-sp, cp]])
    ci, si = c[:patch], s[:patch]
    iy = np.block([[ci, -si], [si, ci]]) / length
    return halves(tx), halves(ix, 1), halves(ty), halves(tt), halves(iy)


def split(value):
    high = value.astype(BF16)
    low = (value - high.astype(F32)).astype(BF16)
    return high, low


def dot(a, b):
    return jnp.dot(a, b, preferred_element_type=F32)


def left_table(table, high, low):
    rows = table.shape[0] // 2
    both = dot(table[...], high)
    return both[:rows] + both[rows:] + dot(table[:rows, :], low)


def right_table(value, table):
    depth = table.shape[0] // 2
    high, low = split(value)
    return dot(jnp.concatenate([high, high], axis=1), table[...]) + dot(low, table[:depth, :])


def right_wide(value, table):
    width = table.shape[1] // 2
    high, low = split(value)
    both = dot(high, table[...])
    return both[:, :width] + both[:, width:] + dot(low, table[:, :width])


def kernel(
    tiles, orients, guard,
    mic_any, tpl_any, ids_any, logw_any, mask_any, tx_any, ix_any, ty_any, tt_any, iy_any,
    lse_any, um_any, st_any,
    mic, ids, logw, mask, tx, ix, ty, tt, iy, pack, halo,
    stack, ext, rows_spec, img, spec, scores, lse_out, lse_in, relay_in, stats, um,
    load_sem, ready, keep_sem, relay_sem,
    halo_send, halo_recv, tpl_send, tpl_recv, lse_send, lse_recv, st_send, st_recv,
):
    t = lax.axis_index("tile")
    o = lax.axis_index("orient")
    everyone = tiles * orients
    extent, side = mic.shape
    patch = tpl_any.shape[2]
    length = 2 * patch
    blocks = side // patch
    share = lse_any.shape[0]
    unrolled = everyone <= 16

    def partner(k):
        if tiles & (tiles - 1):
            return lax.rem(t + k, tiles)
        bit, peer = 1, 0
        while bit < tiles:
            peer = peer + lax.rem(t // bit + k // bit, 2) * bit
            bit *= 2
        return peer

    def seat_of(k):
        return {"tile": partner(k // orients), "orient": lax.rem(o + k % orients, orients)}

    def each_peer(body):
        if unrolled:
            for k in range(everyone - 1, 0, -1):
                body(k)
        else:
            def step(k, carry):
                body(k)
                return carry

            lax.fori_loop(1, everyone, step, 0)

    barrier = pltpu.get_barrier_semaphore()

    def announce(semaphore, first, last):
        def step(place, carry):
            for k in range(tiles):
                pl.semaphore_signal(
                    semaphore, inc=1, device_id={"tile": partner(k), "orient": place},
                    device_id_type=MESH,
                )
            return carry

        lax.fori_loop(first, last, step, 0)

    for k in range(1, tiles):
        pl.semaphore_signal(barrier, inc=1, device_id={"tile": partner(k)}, device_id_type=MESH)
    announce(barrier, o + 1, orients)

    sources = (
        ("tpl", tpl_any.at[0, 0], stack.at[0, pl.ds(0, patch)]),
        ("mic", mic_any, mic),
        ("ids", ids_any, ids),
        ("logw", logw_any, logw),
        ("tx", tx_any, tx),
        ("tt", tt_any, tt),
        ("ty", ty_any, ty),
        ("iy", iy_any, iy),
        ("ix", ix_any, ix),
        ("mask", mask_any, mask),
    )
    loads = {
        name: pltpu.make_async_copy(source, target, load_sem.at[index])
        for index, (name, source, target) in enumerate(sources)
    }
    for name in ("tpl", "mic", "ids", "logw", "tx", "tt"):
        loads[name].start()

    loads["ids"].wait()
    loads["logw"].wait()
    known = lax.broadcasted_iota(jnp.int32, (1, logw.shape[1]), 1) == ids[...]
    weight_here = jnp.sum(jnp.where(known, logw[...], 0.0), axis=1, keepdims=True)
    stack[0, patch:, :] = jnp.broadcast_to(weight_here, (stack.shape[1] - patch, patch))

    loads["mic"].wait()
    middle = extent // 2
    lane_half = lax.broadcasted_iota(jnp.int32, (middle, patch), 1) < guard
    outer, inner = mic[:, side - patch:], mic[:, :patch]
    pack[1] = jnp.where(lane_half, pltpu.roll(outer[:middle], guard, 1), outer[middle:])
    pack[0] = jnp.where(lane_half, inner[:middle], pltpu.roll(inner[middle:], guard, 1))
    loads["tpl"].wait()

    pl.semaphore_wait(barrier, tiles - 1 + tiles * o)

    def halo_copy(place, peer):
        return pltpu.make_async_remote_copy(
            src_ref=pack.at[place], dst_ref=halo.at[1 - place], send_sem=halo_send.at[place],
            recv_sem=halo_recv.at[1 - place], device_id={"tile": peer}, device_id_type=MESH,
        )

    to_left = halo_copy(0, lax.rem(t + tiles - 1, tiles))
    to_right = halo_copy(1, lax.rem(t + 1, tiles))

    def tpl_copy(k):
        return pltpu.make_async_remote_copy(
            src_ref=stack.at[0], dst_ref=stack.at[k], send_sem=tpl_send.at[k],
            recv_sem=tpl_recv.at[k], device_id={"tile": partner(k)}, device_id_type=MESH,
        )

    @pl.when(t > 0)
    def _():
        to_left.start()

    @pl.when(t < tiles - 1)
    def _():
        to_right.start()

    for k in range(1, tiles):
        tpl_copy(k).start()

    for name in ("ty", "iy", "ix", "mask"):
        loads[name].start()

    loads["tx"].wait()
    loads["tt"].wait()

    def spectra(first, many):
        value = stack[pl.ds(first, many), :patch, :].reshape(many * patch, patch)
        high, low = split(value)
        top = tx[:patch, :]
        half = dot(jnp.concatenate([high, low], axis=1), jnp.concatenate([top, top], axis=0))
        half = half + dot(high, tx[length:length + patch, :])
        high, low = split(half)

        def stacked(part):
            return jnp.concatenate(
                [
                    jnp.concatenate(
                        [part[j * patch:(j + 1) * patch, :patch], part[j * patch:(j + 1) * patch, patch:]],
                        axis=0,
                    )
                    for j in range(many)
                ],
                axis=1,
            )

        whole = left_table(tt, stacked(high), stacked(low))
        for j in range(many):
            spec[first + j] = whole[:, j * patch:(j + 1) * patch]

    spectra(0, 1)

    rolled = [pltpu.roll(mic[:, b * patch:(b + 1) * patch], guard, 1) for b in range(blocks)]
    lane = lax.broadcasted_iota(jnp.int32, (extent, patch), 1)
    ext[0] = rolled[0]
    for b in range(1, blocks):
        ext[b] = jnp.where(lane < guard, rolled[b - 1], rolled[b])
    ext[blocks] = rolled[blocks - 1]

    def receive(place):
        present = (t > 0) if place == 0 else (t < tiles - 1)

        @pl.when(present)
        def _():
            halo_copy(1 - place, t).wait_recv()

        @pl.when(jnp.logical_not(present))
        def _():
            halo[place] = jnp.zeros(halo.shape[1:], F32)

        got = halo[place]
        turned = pltpu.roll(got, guard, 1)
        near = lax.broadcasted_iota(jnp.int32, (middle, patch), 1) < guard
        edge = 0 if place == 0 else blocks
        if place == 0:
            ext[edge, :middle] = jnp.where(near, got, ext[edge, :middle])
            ext[edge, middle:] = jnp.where(near, turned, ext[edge, middle:])
        else:
            ext[edge, :middle] = jnp.where(near, ext[edge, :middle], turned)
            ext[edge, middle:] = jnp.where(near, ext[edge, middle:], got)

    def image_x(b):
        half = right_table(jnp.concatenate([ext[b], ext[b + 1]], axis=1), tx)
        for part, value in enumerate(split(half)):
            rows_spec[part, b, 0] = value[:, :patch]
            rows_spec[part, b, 1] = value[:, patch:]

    def image_y(a):
        rows = pl.ds(pl.multiple_of(a * patch, patch), length)

        def stacked(part):
            return jnp.concatenate(
                [
                    jnp.concatenate([rows_spec[part, b, 0, rows, :], rows_spec[part, b, 1, rows, :]], axis=0)
                    for b in range(blocks)
                ],
                axis=1,
            )

        whole = left_table(ty, stacked(0), stacked(1))
        for b in range(blocks):
            img[b] = whole[:, b * patch:(b + 1) * patch]

    def correlate(items):
        highs, lows = [], []
        for k, a, b in items:
            sr, si = spec[k, :length], spec[k, length:]
            ir, ii = img[b, :length], img[b, length:]
            cross = jnp.concatenate([ir * sr + ii * si, ii * sr - ir * si], axis=0)
            high, low = split(cross)
            highs.append(high)
            lows.append(low)
        mid = left_table(iy, jnp.concatenate(highs, axis=1), jnp.concatenate(lows, axis=1))
        pieces = jnp.concatenate(
            [
                jnp.concatenate(
                    [mid[:patch, i * patch:(i + 1) * patch], mid[patch:, i * patch:(i + 1) * patch]],
                    axis=1,
                )
                for i in range(len(items))
            ],
            axis=0,
        )
        final = right_wide(pieces, ix)
        for i, (k, a, b) in enumerate(items):
            scores[k, a, b] = final[i * patch:(i + 1) * patch] + stack[k, patch:, :][:1, :1]

    tpl_copy(1).wait_recv()
    spectra(1, 1)
    loads["ty"].wait()
    loads["ix"].wait()
    loads["iy"].wait()
    odd = lax.rem(t, 2)

    def column(i, carry):
        place = lax.rem(i + 1 + odd, 2)

        @pl.when(i == 1)
        def _():
            announce(ready, 0, o)

        @pl.when(place == 0)
        def _():
            receive(0)

        @pl.when(place == 1)
        def _():
            receive(1)

        image_x(place)
        return carry

    lax.fori_loop(0, 2, column, 0)

    def pairs(body):
        if tiles == 4:
            body(2)
        elif tiles > 4:
            def step(p, carry):
                body(2 * p)
                return carry

            lax.fori_loop(1, tiles // 2, step, 0)

    def own_lse(a, place):
        rows = pl.ds(pl.multiple_of(place * share, share), share)
        parts = []
        for b in range(blocks):
            top = scores[0, a, b, rows, :]
            for k in range(1, tiles):
                top = jnp.maximum(top, scores[k, a, b, rows, :])
            total = jnp.exp(scores[0, a, b, rows, :] - top)
            for k in range(1, tiles):
                total = total + jnp.exp(scores[k, a, b, rows, :] - top)
            parts.append(top + jnp.log(total))
        return jnp.concatenate(parts, axis=1)

    def lse_copy(k):
        return pltpu.make_async_remote_copy(
            src_ref=lse_out.at[k], dst_ref=lse_in.at[k], send_sem=lse_send.at[k],
            recv_sem=lse_recv.at[k], device_id={"orient": lax.rem(o + k, orients)},
            device_id_type=MESH,
        )

    relayed = orients == 4
    outer = lax.rem(o, 3) == 0
    held = 2 * o - 1
    part = share // 2

    def relay(h):
        rows = pl.ds(h * part, part)
        return pltpu.make_async_remote_copy(
            src_ref=lse_out.at[2, rows], dst_ref=relay_in.at[rows], send_sem=relay_sem.at[0, h],
            recv_sem=relay_sem.at[1, h], device_id={"orient": o + 1 - 2 * lax.rem(o, 2)},
            device_id_type=MESH,
        )

    def held_copy(h):
        rows = pl.ds(h * part, part)
        return pltpu.make_async_remote_copy(
            src_ref=lse_out.at[held, rows], dst_ref=lse_in.at[held, rows], send_sem=lse_send.at[held],
            recv_sem=lse_recv.at[held], device_id={"orient": lax.rem(o + held, orients)},
            device_id_type=MESH,
        )

    owners = patch // share
    home, seat = o // owners, lax.rem(o, owners)

    def far_spectra():
        for k in range(2, tiles):
            tpl_copy(k).wait_recv()
        pairs(lambda k: spectra(k, 2))

        @pl.when(o < orients - 1)
        def _():
            pl.semaphore_wait(ready, tiles * (orients - 1 - o))

    def cell(j, carry):
        first = lax.rem(j, tiles // 2) * 2
        a = lax.rem(home + 1 + j // (tiles // 2), blocks)

        @pl.when(first == 0)
        def _():
            image_y(a)

        @pl.when(j == 1)
        def _():
            far_spectra()

        correlate([(first + q, a, b) for q in range(2) for b in range(blocks)])

        @pl.when(first == tiles - 2)
        def _():
            far = jnp.where(a == home, 0, owners - 1)

            def send(gap, inner):
                place = lax.rem(seat + gap + far, owners)
                ahead = lax.rem(a * owners + place - o + orients, orients)
                lse_out[ahead] = own_lse(a, place)

                direct = ahead > 0
                if relayed:
                    direct = direct & jnp.where(outer, ahead != 2, ahead != held)

                    @pl.when(outer & (ahead == 2))
                    def _():
                        relay(0).start()
                        relay(1).start()

                @pl.when(direct)
                def _():
                    lse_copy(ahead).start()

                return inner

            lax.fori_loop(1, owners + 1, send, 0)

        return carry

    lax.fori_loop(0, blocks * (tiles // 2), cell, 0)

    if relayed:
        @pl.when(jnp.logical_not(outer))
        def _():
            for h in range(2):
                relay(h).wait_recv()
                rows = pl.ds(h * part, part)
                ours, theirs = lse_out[held, rows, :], relay_in[rows, :]
                most = jnp.maximum(ours, theirs)
                lse_out[held, rows, :] = most + jnp.log(jnp.exp(ours - most) + jnp.exp(theirs - most))
                held_copy(h).start()
            lse_in[2] = jnp.full(lse_in.shape[1:], -1e30, F32)

    loads["mask"].wait()
    mask_rows, mask_cols = mask.shape
    row_id = lax.broadcasted_iota(jnp.int32, (share, mask_rows), 0) + o * share
    pick = lax.broadcasted_iota(jnp.int32, (share, mask_rows), 1)
    low_edge = pick * MBLK
    rows_of = jnp.where((row_id >= low_edge) & (row_id < low_edge + MBLK), 1.0, 0.0).astype(F32)
    col_id = lax.broadcasted_iota(jnp.int32, (mask_cols, side), 1)
    col_edge = lax.broadcasted_iota(jnp.int32, (mask_cols, side), 0) * MBLK
    cols_of = jnp.where((col_id >= col_edge) & (col_id < col_edge + MBLK), 1.0, 0.0).astype(F32)
    unmasked = 1.0 - dot(dot(rows_of, mask[...].astype(F32)), cols_of)

    def whole_sum(value):
        return jnp.sum(jnp.sum(value, axis=0, keepdims=True), axis=1, keepdims=True)

    count = whole_sum(unmasked)
    um[...] = unmasked
    keep_um = pltpu.make_async_copy(um, um_any, keep_sem.at[0])
    keep_um.start()

    mine = lse_out[0]
    for k in range(1, orients):
        if relayed and k == 2:
            @pl.when(outer)
            def _():
                lse_copy(2).wait_recv()
        else:
            lse_copy(k).wait_recv()
    top = mine
    for k in range(1, orients):
        top = jnp.maximum(top, lse_in[k])
    total = jnp.exp(mine - top)
    for k in range(1, orients):
        total = total + jnp.exp(lse_in[k] - top)
    lse = top + jnp.log(total)

    sum_here = whole_sum(unmasked * lse)
    mean_here = sum_here / jnp.maximum(count, 1.0)
    deviation = lse - mean_here
    squares = whole_sum(unmasked * deviation * deviation)
    slot = lax.broadcasted_iota(jnp.int32, stats.shape, 1)
    stats[...] = jnp.where(
        slot == 0, count, jnp.where(slot == 1, sum_here, jnp.where(slot == 2, squares, 0.0))
    )

    def st_copy(k):
        return pltpu.make_async_remote_copy(
            src_ref=stats, dst_ref=st_any.at[k], send_sem=st_send.at[k],
            recv_sem=st_recv.at[k], device_id=seat_of(k), device_id_type=MESH,
        )

    each_peer(lambda k: st_copy(k).start())
    lse_in[0] = lse
    keep_lse = pltpu.make_async_copy(lse_in.at[0], lse_any, keep_sem.at[1])
    keep_lse.start()
    keep_st = pltpu.make_async_copy(stats, st_any.at[0], keep_sem.at[2])
    keep_st.start()

    @pl.when(t > 0)
    def _():
        to_left.wait_send()

    @pl.when(t < tiles - 1)
    def _():
        to_right.wait_send()

    for k in range(1, tiles):
        tpl_copy(k).wait_send()
    for k in range(1, orients):
        if relayed and k == 2:
            @pl.when(outer)
            def _():
                relay(0).wait_send()
                relay(1).wait_send()

            @pl.when(jnp.logical_not(outer))
            def _():
                lse_copy(2).wait_send()
        else:
            lse_copy(k).wait_send()
    each_peer(lambda k: st_copy(k).wait())
    keep_um.wait()
    keep_lse.wait()
    keep_st.wait()


def finish(lse, unmasked, stats, out):
    table = stats[:, 0, :]
    counts, sums, sqs = table[:, 0:1], table[:, 1:2], table[:, 2:3]
    live = jnp.sum(counts, axis=0, keepdims=True)
    average = jnp.sum(sums, axis=0, keepdims=True) / live
    gap = sums / jnp.maximum(counts, 1.0) - average
    variance = jnp.sum(sqs + counts * gap * gap, axis=0, keepdims=True) / live
    out[...] = unmasked[...] * (lse[...] - average) / jnp.sqrt(variance + 1e-05)


def body(tiles, orients, micrograph, templates, orient_ids, log_weight, ice_mask):
    extent, side = micrograph.shape
    patch = templates.shape[2]
    share = side // orients
    blocks = side // patch
    everyone = tiles * orients
    anywhere = pl.BlockSpec(memory_space=pl.ANY)
    vmem = pltpu.VMEM
    dma = pltpu.SemaphoreType.DMA
    consts = [jnp.asarray(table) for table in tables(patch)]
    lse, unmasked, stats = pl.pallas_call(
        functools.partial(kernel, tiles, orients, patch // 2),
        out_shape=[
            jax.ShapeDtypeStruct((share, side), F32),
            jax.ShapeDtypeStruct((share, side), F32),
            jax.ShapeDtypeStruct((everyone, 1, 128), F32),
        ],
        in_specs=[anywhere] * (5 + len(consts)),
        out_specs=[anywhere] * 3,
        scratch_shapes=[
            vmem((extent, side), F32),
            vmem(orient_ids.shape, jnp.int32),
            vmem((1, log_weight.shape[0]), F32),
            vmem(ice_mask.shape, jnp.int32),
            *[vmem(table.shape, BF16) for table in consts],
            vmem((2, extent // 2, patch), F32),
            vmem((2, extent // 2, patch), F32),
            vmem((tiles, patch + 8, patch), F32),
            vmem((blocks + 1, extent, patch), F32),
            vmem((2, blocks, 2, extent, patch), BF16),
            vmem((blocks, 4 * patch, patch), F32),
            vmem((tiles, 4 * patch, patch), F32),
            vmem((tiles, blocks, blocks, patch, patch), F32),
            vmem((orients, share, side), F32),
            vmem((orients, share, side), F32),
            vmem((share, side), F32),
            vmem((1, 128), F32),
            vmem((share, side), F32),
            dma((5 + len(consts),)),
            pltpu.SemaphoreType.REGULAR,
            dma((3,)),
            dma((2, 2)),
            dma((2,)), dma((2,)),
            dma((tiles,)), dma((tiles,)),
            dma((orients,)), dma((orients,)),
            dma((everyone,)), dma((everyone,)),
        ],
        compiler_params=pltpu.CompilerParams(
            collective_id=0, has_side_effects=True, vmem_limit_bytes=56 * 1024 * 1024
        ),
    )(micrograph, templates, orient_ids, log_weight.reshape(1, -1), ice_mask, *consts)
    here = pl.BlockSpec(memory_space=pltpu.VMEM)
    return pl.pallas_call(
        finish,
        out_shape=jax.ShapeDtypeStruct((share, side), F32),
        in_specs=[here] * 3,
        out_specs=here,
        cost_estimate=pl.CostEstimate(flops=4 * share * side, bytes_accessed=12 * share * side, transcendentals=0),
    )(lse, unmasked, stats)


def solution(mesh):
    return jax.shard_map(
        functools.partial(body, mesh.shape["tile"], mesh.shape["orient"]),
        mesh=mesh,
        in_specs=(
            P("group", "tile"),
            P("orient", "tile", None, None),
            P("orient", "tile"),
            P(),
            P("group", "tile"),
        ),
        out_specs=P(("group", "orient"), "tile"),
        check_vma=False,
    )
```

```python
import functools
import math

import jax
import jax.numpy as jnp
import numpy as np
from jax import lax
from jax.experimental import pallas as pl
from jax.experimental.pallas import tpu as pltpu
from jax.sharding import PartitionSpec as P

MBLK = 16
F32 = jnp.float32
BF16 = jnp.bfloat16
MESH = pl.DeviceIdType.MESH


def halves(table, axis=0):
    table = table.astype(np.float32)
    high = table.astype(jnp.bfloat16)
    low = (table - high.astype(np.float32)).astype(jnp.bfloat16)
    return np.concatenate([high, low], axis=axis)


def tables(patch):
    length = 2 * patch
    n = np.arange(length)[:, None]
    k = np.arange(patch)[None, :]
    theta = 2 * math.pi * ((n * (2 * k + 1)) % (2 * length)) / (2 * length)
    tx = np.concatenate([np.cos(theta), -np.sin(theta)], axis=1)
    back = theta[:patch].T
    ix = np.concatenate([np.cos(back), -np.sin(back)], axis=0) * (2.0 / length)
    m = np.arange(length)
    phi = 2 * math.pi * ((m[:, None] * m[None, :]) % length) / length
    c, s = np.cos(phi), np.sin(phi)
    ty = np.block([[c, s], [-s, c]])
    cp, sp = c[:, :patch], s[:, :patch]
    tt = np.block([[cp, sp], [-sp, cp]])
    ci, si = c[:patch], s[:patch]
    iy = np.block([[ci, -si], [si, ci]]) / length
    return halves(tx), halves(ix, 1), halves(ty), halves(tt), halves(iy)


def split(value):
    high = value.astype(BF16)
    low = (value - high.astype(F32)).astype(BF16)
    return high, low


def dot(a, b):
    return jnp.dot(a, b, preferred_element_type=F32)


def left_table(table, high, low):
    rows = table.shape[0] // 2
    both = dot(table[...], high)
    return both[:rows] + both[rows:] + dot(table[:rows, :], low)


def right_table(value, table):
    depth = table.shape[0] // 2
    high, low = split(value)
    return dot(jnp.concatenate([high, high], axis=1), table[...]) + dot(low, table[:depth, :])


def right_wide(value, table):
    width = table.shape[1] // 2
    high, low = split(value)
    both = dot(high, table[...])
    return both[:, :width] + both[:, width:] + dot(low, table[:, :width])


def kernel(
    tiles, orients, guard,
    mic_any, tpl_any, ids_any, logw_any, mask_any, tx_any, ix_any, ty_any, tt_any, iy_any,
    lse_any, um_any, st_any,
    mic, ids, logw, mask, tx, ix, ty, tt, iy, pack, halo,
    stack, ext, rows_spec, img, spec, scores, lse_out, lse_in, relay_in, stats, um,
    load_sem, ready, keep_sem, relay_sem,
    halo_send, halo_recv, tpl_send, tpl_recv, lse_send, lse_recv, st_send, st_recv,
):
    t = lax.axis_index("tile")
    o = lax.axis_index("orient")
    everyone = tiles * orients
    extent, side = mic.shape
    patch = tpl_any.shape[2]
    length = 2 * patch
    blocks = side // patch
    share = lse_any.shape[0]
    unrolled = everyone <= 16

    def partner(k):
        if tiles & (tiles - 1):
            return lax.rem(t + k, tiles)
        bit, peer = 1, 0
        while bit < tiles:
            peer = peer + lax.rem(t // bit + k // bit, 2) * bit
            bit *= 2
        return peer

    barrier = pltpu.get_barrier_semaphore()

    def announce(semaphore, first, last):
        def step(place, carry):
            for k in range(tiles):
                pl.semaphore_signal(
                    semaphore, inc=1, device_id={"tile": partner(k), "orient": place},
                    device_id_type=MESH,
                )
            return carry

        lax.fori_loop(first, last, step, 0)

    for k in range(1, tiles):
        pl.semaphore_signal(barrier, inc=1, device_id={"tile": partner(k)}, device_id_type=MESH)
    announce(barrier, o + 1, orients)

    sources = (
        ("tpl", tpl_any.at[0, 0], stack.at[0, pl.ds(0, patch)]),
        ("mic", mic_any, mic),
        ("ids", ids_any, ids),
        ("logw", logw_any, logw),
        ("tx", tx_any, tx),
        ("tt", tt_any, tt),
        ("ty", ty_any, ty),
        ("iy", iy_any, iy),
        ("ix", ix_any, ix),
        ("mask", mask_any, mask),
    )
    loads = {
        name: pltpu.make_async_copy(source, target, load_sem.at[index])
        for index, (name, source, target) in enumerate(sources)
    }
    for name in ("tpl", "mic", "ids", "logw", "tx", "tt"):
        loads[name].start()

    loads["ids"].wait()
    loads["logw"].wait()
    known = lax.broadcasted_iota(jnp.int32, (1, logw.shape[1]), 1) == ids[...]
    weight_here = jnp.sum(jnp.where(known, logw[...], 0.0), axis=1, keepdims=True)
    stack[0, patch:, :] = jnp.broadcast_to(weight_here, (stack.shape[1] - patch, patch))

    loads["mic"].wait()
    middle = extent // 2
    lane_half = lax.broadcasted_iota(jnp.int32, (middle, patch), 1) < guard
    outer, inner = mic[:, side - patch:], mic[:, :patch]
    pack[1] = jnp.where(lane_half, pltpu.roll(outer[:middle], guard, 1), outer[middle:])
    pack[0] = jnp.where(lane_half, inner[:middle], pltpu.roll(inner[middle:], guard, 1))
    loads["tpl"].wait()

    pl.semaphore_wait(barrier, tiles - 1 + tiles * o)

    def halo_copy(place, peer):
        return pltpu.make_async_remote_copy(
            src_ref=pack.at[place], dst_ref=halo.at[1 - place], send_sem=halo_send.at[place],
            recv_sem=halo_recv.at[1 - place], device_id={"tile": peer}, device_id_type=MESH,
        )

    to_left = halo_copy(0, lax.rem(t + tiles - 1, tiles))
    to_right = halo_copy(1, lax.rem(t + 1, tiles))

    def tpl_copy(k):
        return pltpu.make_async_remote_copy(
            src_ref=stack.at[0], dst_ref=stack.at[k], send_sem=tpl_send.at[k],
            recv_sem=tpl_recv.at[k], device_id={"tile": partner(k)}, device_id_type=MESH,
        )

    @pl.when(t > 0)
    def _():
        to_left.start()

    @pl.when(t < tiles - 1)
    def _():
        to_right.start()

    for k in range(1, tiles):
        tpl_copy(k).start()

    for name in ("ty", "iy", "ix", "mask"):
        loads[name].start()

    loads["tx"].wait()
    loads["tt"].wait()

    def spectra(first, many):
        value = stack[pl.ds(first, many), :patch, :].reshape(many * patch, patch)
        high, low = split(value)
        top = tx[:patch, :]
        half = dot(jnp.concatenate([high, low], axis=1), jnp.concatenate([top, top], axis=0))
        half = half + dot(high, tx[length:length + patch, :])
        high, low = split(half)

        def stacked(part):
            return jnp.concatenate(
                [
                    jnp.concatenate(
                        [part[j * patch:(j + 1) * patch, :patch], part[j * patch:(j + 1) * patch, patch:]],
                        axis=0,
                    )
                    for j in range(many)
                ],
                axis=1,
            )

        whole = left_table(tt, stacked(high), stacked(low))
        for j in range(many):
            spec[first + j] = whole[:, j * patch:(j + 1) * patch]

    spectra(0, 1)

    rolled = [pltpu.roll(mic[:, b * patch:(b + 1) * patch], guard, 1) for b in range(blocks)]
    lane = lax.broadcasted_iota(jnp.int32, (extent, patch), 1)
    ext[0] = rolled[0]
    for b in range(1, blocks):
        ext[b] = jnp.where(lane < guard, rolled[b - 1], rolled[b])
    ext[blocks] = rolled[blocks - 1]

    def receive(place):
        present = (t > 0) if place == 0 else (t < tiles - 1)

        @pl.when(present)
        def _():
            halo_copy(1 - place, t).wait_recv()

        @pl.when(jnp.logical_not(present))
        def _():
            halo[place] = jnp.zeros(halo.shape[1:], F32)

        got = halo[place]
        turned = pltpu.roll(got, guard, 1)
        near = lax.broadcasted_iota(jnp.int32, (middle, patch), 1) < guard
        edge = 0 if place == 0 else blocks
        if place == 0:
            ext[edge, :middle] = jnp.where(near, got, ext[edge, :middle])
            ext[edge, middle:] = jnp.where(near, turned, ext[edge, middle:])
        else:
            ext[edge, :middle] = jnp.where(near, ext[edge, :middle], turned)
            ext[edge, middle:] = jnp.where(near, ext[edge, middle:], got)

    def image_x(b):
        half = right_table(jnp.concatenate([ext[b], ext[b + 1]], axis=1), tx)
        for part, value in enumerate(split(half)):
            rows_spec[part, b, 0] = value[:, :patch]
            rows_spec[part, b, 1] = value[:, patch:]

    def image_y(a):
        rows = pl.ds(pl.multiple_of(a * patch, patch), length)

        def stacked(part):
            return jnp.concatenate(
                [
                    jnp.concatenate([rows_spec[part, b, 0, rows, :], rows_spec[part, b, 1, rows, :]], axis=0)
                    for b in range(blocks)
                ],
                axis=1,
            )

        whole = left_table(ty, stacked(0), stacked(1))
        for b in range(blocks):
            img[b] = whole[:, b * patch:(b + 1) * patch]

    def correlate(items):
        highs, lows = [], []
        for k, a, b in items:
            sr, si = spec[k, :length], spec[k, length:]
            ir, ii = img[b, :length], img[b, length:]
            cross = jnp.concatenate([ir * sr + ii * si, ii * sr - ir * si], axis=0)
            high, low = split(cross)
            highs.append(high)
            lows.append(low)
        mid = left_table(iy, jnp.concatenate(highs, axis=1), jnp.concatenate(lows, axis=1))
        pieces = jnp.concatenate(
            [
                jnp.concatenate(
                    [mid[:patch, i * patch:(i + 1) * patch], mid[patch:, i * patch:(i + 1) * patch]],
                    axis=1,
                )
                for i in range(len(items))
            ],
            axis=0,
        )
        final = right_wide(pieces, ix)
        for i, (k, a, b) in enumerate(items):
            scores[k, a, b] = final[i * patch:(i + 1) * patch] + stack[k, patch:, :][:1, :1]

    tpl_copy(1).wait_recv()
    spectra(1, 1)
    loads["ty"].wait()
    loads["ix"].wait()
    loads["iy"].wait()
    odd = lax.rem(t, 2)

    def column(i, carry):
        place = lax.rem(i + 1 + odd, 2)

        @pl.when(i == 1)
        def _():
            announce(ready, 0, o)

        @pl.when(place == 0)
        def _():
            receive(0)

        @pl.when(place == 1)
        def _():
            receive(1)

        image_x(place)
        return carry

    lax.fori_loop(0, 2, column, 0)

    def pairs(body):
        if tiles == 4:
            body(2)
        elif tiles > 4:
            def step(p, carry):
                body(2 * p)
                return carry

            lax.fori_loop(1, tiles // 2, step, 0)

    def own_lse(a, place):
        rows = pl.ds(pl.multiple_of(place * share, share), share)
        parts = []
        for b in range(blocks):
            top = scores[0, a, b, rows, :]
            for k in range(1, tiles):
                top = jnp.maximum(top, scores[k, a, b, rows, :])
            total = jnp.exp(scores[0, a, b, rows, :] - top)
            for k in range(1, tiles):
                total = total + jnp.exp(scores[k, a, b, rows, :] - top)
            parts.append(top + jnp.log(total))
        return jnp.concatenate(parts, axis=1)

    def lse_copy(k):
        return pltpu.make_async_remote_copy(
            src_ref=lse_out.at[k], dst_ref=lse_in.at[k], send_sem=lse_send.at[k],
            recv_sem=lse_recv.at[k], device_id={"orient": lax.rem(o + k, orients)},
            device_id_type=MESH,
        )

    relayed = orients == 4
    outer = lax.rem(o, 3) == 0
    held = 2 * o - 1
    part = share // 2

    def relay(h):
        rows = pl.ds(h * part, part)
        return pltpu.make_async_remote_copy(
            src_ref=lse_out.at[2, rows], dst_ref=relay_in.at[rows], send_sem=relay_sem.at[0, h],
            recv_sem=relay_sem.at[1, h], device_id={"orient": o + 1 - 2 * lax.rem(o, 2)},
            device_id_type=MESH,
        )

    def held_copy(h):
        rows = pl.ds(h * part, part)
        return pltpu.make_async_remote_copy(
            src_ref=lse_out.at[held, rows], dst_ref=lse_in.at[held, rows], send_sem=lse_send.at[held],
            recv_sem=lse_recv.at[held], device_id={"orient": lax.rem(o + held, orients)},
            device_id_type=MESH,
        )

    owners = patch // share
    home, seat = o // owners, lax.rem(o, owners)

    def far_spectra():
        for k in range(2, tiles):
            tpl_copy(k).wait_recv()
        pairs(lambda k: spectra(k, 2))

        @pl.when(o < orients - 1)
        def _():
            pl.semaphore_wait(ready, tiles * (orients - 1 - o))

    def cell(j, carry):
        first = lax.rem(j, tiles // 2) * 2
        a = lax.rem(home + 1 + j // (tiles // 2), blocks)

        @pl.when(first == 0)
        def _():
            image_y(a)

        @pl.when(j == 1)
        def _():
            far_spectra()

        correlate([(first + q, a, b) for q in range(2) for b in range(blocks)])

        @pl.when(first == tiles - 2)
        def _():
            far = jnp.where(a == home, 0, owners - 1)

            def send(gap, inner):
                place = lax.rem(seat + gap + far, owners)
                ahead = lax.rem(a * owners + place - o + orients, orients)
                lse_out[ahead] = own_lse(a, place)

                direct = ahead > 0
                if relayed:
                    direct = direct & jnp.where(outer, ahead != 2, ahead != held)

                    @pl.when(outer & (ahead == 2))
                    def _():
                        relay(0).start()
                        relay(1).start()

                @pl.when(direct)
                def _():
                    lse_copy(ahead).start()

                return inner

            lax.fori_loop(1, owners + 1, send, 0)

        return carry

    lax.fori_loop(0, blocks * (tiles // 2), cell, 0)

    if relayed:
        @pl.when(jnp.logical_not(outer))
        def _():
            for h in range(2):
                relay(h).wait_recv()
                rows = pl.ds(h * part, part)
                ours, theirs = lse_out[held, rows, :], relay_in[rows, :]
                most = jnp.maximum(ours, theirs)
                lse_out[held, rows, :] = most + jnp.log(jnp.exp(ours - most) + jnp.exp(theirs - most))
                held_copy(h).start()
            lse_in[2] = jnp.full(lse_in.shape[1:], -1e30, F32)

    loads["mask"].wait()
    mask_rows, mask_cols = mask.shape
    row_id = lax.broadcasted_iota(jnp.int32, (share, mask_rows), 0) + o * share
    pick = lax.broadcasted_iota(jnp.int32, (share, mask_rows), 1)
    low_edge = pick * MBLK
    rows_of = jnp.where((row_id >= low_edge) & (row_id < low_edge + MBLK), 1.0, 0.0).astype(F32)
    col_id = lax.broadcasted_iota(jnp.int32, (mask_cols, side), 1)
    col_edge = lax.broadcasted_iota(jnp.int32, (mask_cols, side), 0) * MBLK
    cols_of = jnp.where((col_id >= col_edge) & (col_id < col_edge + MBLK), 1.0, 0.0).astype(F32)
    unmasked = 1.0 - dot(dot(rows_of, mask[...].astype(F32)), cols_of)

    def whole_sum(value):
        return jnp.sum(jnp.sum(value, axis=0, keepdims=True), axis=1, keepdims=True)

    count = whole_sum(unmasked)
    um[...] = unmasked
    keep_um = pltpu.make_async_copy(um, um_any, keep_sem.at[0])
    keep_um.start()

    mine = lse_out[0]
    for k in range(1, orients):
        if relayed and k == 2:
            @pl.when(outer)
            def _():
                lse_copy(2).wait_recv()
        else:
            lse_copy(k).wait_recv()
    top = mine
    for k in range(1, orients):
        top = jnp.maximum(top, lse_in[k])
    total = jnp.exp(mine - top)
    for k in range(1, orients):
        total = total + jnp.exp(lse_in[k] - top)
    lse = top + jnp.log(total)

    sum_here = whole_sum(unmasked * lse)
    mean_here = sum_here / jnp.maximum(count, 1.0)
    deviation = lse - mean_here
    squares = whole_sum(unmasked * deviation * deviation)
    slot = lax.broadcasted_iota(jnp.int32, stats.shape, 1)
    stats[...] = jnp.where(
        slot == 0, count, jnp.where(slot == 1, sum_here, jnp.where(slot == 2, squares, 0.0))
    )

    me = t * orients + o

    def st_copy(place, slot):
        return pltpu.make_async_remote_copy(
            src_ref=stats, dst_ref=st_any.at[slot], send_sem=st_send.at[place],
            recv_sem=st_recv.at[slot],
            device_id={"tile": lax.rem(place, tiles), "orient": place // tiles},
            device_id_type=MESH,
        )

    def each_other(body, skip):
        def step(place, carry):
            @pl.when(place != skip)
            def _():
                body(place)

            return carry

        if unrolled:
            for place in range(everyone):
                step(place, 0)
        else:
            lax.fori_loop(0, everyone, step, 0)

    there = o * tiles + t
    each_other(lambda place: st_copy(place, me).start(), there)
    lse_in[0] = lse
    keep_lse = pltpu.make_async_copy(lse_in.at[0], lse_any, keep_sem.at[1])
    keep_lse.start()
    keep_st = pltpu.make_async_copy(stats, st_any.at[me], keep_sem.at[2])
    keep_st.start()

    @pl.when(t > 0)
    def _():
        to_left.wait_send()

    @pl.when(t < tiles - 1)
    def _():
        to_right.wait_send()

    for k in range(1, tiles):
        tpl_copy(k).wait_send()
    for k in range(1, orients):
        if relayed and k == 2:
            @pl.when(outer)
            def _():
                relay(0).wait_send()
                relay(1).wait_send()

            @pl.when(jnp.logical_not(outer))
            def _():
                lse_copy(2).wait_send()
        else:
            lse_copy(k).wait_send()
    each_other(lambda place: st_copy(place, me).wait_send(), there)
    each_other(lambda slot: st_copy(0, slot).wait_recv(), me)
    keep_um.wait()
    keep_lse.wait()
    keep_st.wait()


def finish(lse, unmasked, stats, out):
    table = stats[:, 0, :]
    counts, sums, sqs = table[:, 0:1], table[:, 1:2], table[:, 2:3]
    live = jnp.sum(counts, axis=0, keepdims=True)
    average = jnp.sum(sums, axis=0, keepdims=True) / live
    gap = sums / jnp.maximum(counts, 1.0) - average
    variance = jnp.sum(sqs + counts * gap * gap, axis=0, keepdims=True) / live
    out[...] = unmasked[...] * (lse[...] - average) / jnp.sqrt(variance + 1e-05)


def body(tiles, orients, micrograph, templates, orient_ids, log_weight, ice_mask):
    extent, side = micrograph.shape
    patch = templates.shape[2]
    share = side // orients
    blocks = side // patch
    everyone = tiles * orients
    anywhere = pl.BlockSpec(memory_space=pl.ANY)
    vmem = pltpu.VMEM
    dma = pltpu.SemaphoreType.DMA
    consts = [jnp.asarray(table) for table in tables(patch)]
    lse, unmasked, stats = pl.pallas_call(
        functools.partial(kernel, tiles, orients, patch // 2),
        out_shape=[
            jax.ShapeDtypeStruct((share, side), F32),
            jax.ShapeDtypeStruct((share, side), F32),
            jax.ShapeDtypeStruct((everyone, 1, 128), F32),
        ],
        in_specs=[anywhere] * (5 + len(consts)),
        out_specs=[anywhere] * 3,
        scratch_shapes=[
            vmem((extent, side), F32),
            vmem(orient_ids.shape, jnp.int32),
            vmem((1, log_weight.shape[0]), F32),
            vmem(ice_mask.shape, jnp.int32),
            *[vmem(table.shape, BF16) for table in consts],
            vmem((2, extent // 2, patch), F32),
            vmem((2, extent // 2, patch), F32),
            vmem((tiles, patch + 8, patch), F32),
            vmem((blocks + 1, extent, patch), F32),
            vmem((2, blocks, 2, extent, patch), BF16),
            vmem((blocks, 4 * patch, patch), F32),
            vmem((tiles, 4 * patch, patch), F32),
            vmem((tiles, blocks, blocks, patch, patch), F32),
            vmem((orients, share, side), F32),
            vmem((orients, share, side), F32),
            vmem((share, side), F32),
            vmem((1, 128), F32),
            vmem((share, side), F32),
            dma((5 + len(consts),)),
            pltpu.SemaphoreType.REGULAR,
            dma((3,)),
            dma((2, 2)),
            dma((2,)), dma((2,)),
            dma((tiles,)), dma((tiles,)),
            dma((orients,)), dma((orients,)),
            dma((everyone,)), dma((everyone,)),
        ],
        compiler_params=pltpu.CompilerParams(
            collective_id=0, has_side_effects=True, vmem_limit_bytes=56 * 1024 * 1024
        ),
    )(micrograph, templates, orient_ids, log_weight.reshape(1, -1), ice_mask, *consts)
    here = pl.BlockSpec(memory_space=pltpu.VMEM)
    return pl.pallas_call(
        finish,
        out_shape=jax.ShapeDtypeStruct((share, side), F32),
        in_specs=[here] * 3,
        out_specs=here,
        cost_estimate=pl.CostEstimate(flops=4 * share * side, bytes_accessed=12 * share * side, transcendentals=0),
    )(lse, unmasked, stats)


def solution(mesh):
    return jax.shard_map(
        functools.partial(body, mesh.shape["tile"], mesh.shape["orient"]),
        mesh=mesh,
        in_specs=(
            P("group", "tile"),
            P("orient", "tile", None, None),
            P("orient", "tile"),
            P(),
            P("group", "tile"),
        ),
        out_specs=P(("group", "orient"), "tile"),
        check_vma=False,
    )
```

```python
import functools
import math

import jax
import jax.numpy as jnp
import numpy as np
from jax import lax
from jax.experimental import pallas as pl
from jax.experimental.pallas import tpu as pltpu
from jax.sharding import PartitionSpec as P

MBLK = 16
F32 = jnp.float32
BF16 = jnp.bfloat16
MESH = pl.DeviceIdType.MESH


def halves(table, axis=0):
    table = table.astype(np.float32)
    high = table.astype(jnp.bfloat16)
    low = (table - high.astype(np.float32)).astype(jnp.bfloat16)
    return np.concatenate([high, low], axis=axis)


def tables(patch):
    length = 2 * patch
    n = np.arange(length)[:, None]
    k = np.arange(patch)[None, :]
    theta = 2 * math.pi * ((n * (2 * k + 1)) % (2 * length)) / (2 * length)
    tx = np.concatenate([np.cos(theta), -np.sin(theta)], axis=1)
    back = theta[:patch].T
    ix = np.concatenate([np.cos(back), -np.sin(back)], axis=0) * (2.0 / length)
    m = np.arange(length)
    phi = 2 * math.pi * ((m[:, None] * m[None, :]) % length) / length
    c, s = np.cos(phi), np.sin(phi)
    ty = np.block([[c, s], [-s, c]])
    cp, sp = c[:, :patch], s[:, :patch]
    tt = np.block([[cp, sp], [-sp, cp]])
    ci, si = c[:patch], s[:patch]
    iy = np.block([[ci, -si], [si, ci]]) / length
    return halves(tx), halves(ix, 1), halves(ty), halves(tt), halves(iy)


def split(value):
    high = value.astype(BF16)
    low = (value - high.astype(F32)).astype(BF16)
    return high, low


def dot(a, b):
    return jnp.dot(a, b, preferred_element_type=F32)


def left_table(table, high, low):
    rows = table.shape[0] // 2
    both = dot(table[...], high)
    return both[:rows] + both[rows:] + dot(table[:rows, :], low)


def right_table(value, table):
    depth = table.shape[0] // 2
    high, low = split(value)
    return dot(jnp.concatenate([high, high], axis=1), table[...]) + dot(low, table[:depth, :])


def right_wide(value, table):
    width = table.shape[1] // 2
    high, low = split(value)
    both = dot(high, table[...])
    return both[:, :width] + both[:, width:] + dot(low, table[:, :width])


def kernel(
    tiles, orients, guard,
    mic_any, tpl_any, ids_any, logw_any, mask_any, tx_any, ix_any, ty_any, tt_any, iy_any,
    lse_any, um_any, st_any,
    mic, ids, logw, mask, tx, ix, ty, tt, iy, pack, halo,
    stack, ext, rows_spec, img, spec, scores, lse_out, lse_in, relay_in, stats, um,
    load_sem, ready, keep_sem, relay_sem,
    halo_send, halo_recv, tpl_send, tpl_recv, lse_send, lse_recv, st_send, st_recv,
):
    t = lax.axis_index("tile")
    o = lax.axis_index("orient")
    everyone = tiles * orients
    extent, side = mic.shape
    patch = tpl_any.shape[2]
    length = 2 * patch
    blocks = side // patch
    share = lse_any.shape[0]
    unrolled = everyone <= 16

    def partner(k):
        if tiles & (tiles - 1):
            return lax.rem(t + k, tiles)
        bit, peer = 1, 0
        while bit < tiles:
            peer = peer + lax.rem(t // bit + k // bit, 2) * bit
            bit *= 2
        return peer

    barrier = pltpu.get_barrier_semaphore()

    def announce(semaphore, first, last):
        def step(place, carry):
            for k in range(tiles):
                pl.semaphore_signal(
                    semaphore, inc=1, device_id={"tile": partner(k), "orient": place},
                    device_id_type=MESH,
                )
            return carry

        lax.fori_loop(first, last, step, 0)

    for k in range(1, tiles):
        pl.semaphore_signal(barrier, inc=1, device_id={"tile": partner(k)}, device_id_type=MESH)
    announce(barrier, o + 1, orients)

    sources = (
        ("tpl", tpl_any.at[0, 0], stack.at[0, pl.ds(0, patch)]),
        ("mic", mic_any, mic),
        ("ids", ids_any, ids),
        ("logw", logw_any, logw),
        ("tx", tx_any, tx),
        ("tt", tt_any, tt),
        ("ty", ty_any, ty),
        ("iy", iy_any, iy),
        ("ix", ix_any, ix),
        ("mask", mask_any, mask),
    )
    loads = {
        name: pltpu.make_async_copy(source, target, load_sem.at[index])
        for index, (name, source, target) in enumerate(sources)
    }
    for name in ("tpl", "mic", "ids", "logw", "tx", "tt"):
        loads[name].start()

    loads["ids"].wait()
    loads["logw"].wait()
    known = lax.broadcasted_iota(jnp.int32, (1, logw.shape[1]), 1) == ids[...]
    weight_here = jnp.sum(jnp.where(known, logw[...], 0.0), axis=1, keepdims=True)
    stack[0, patch:, :] = jnp.broadcast_to(weight_here, (stack.shape[1] - patch, patch))

    loads["mic"].wait()
    middle = extent // 2
    lane_half = lax.broadcasted_iota(jnp.int32, (middle, patch), 1) < guard
    outer, inner = mic[:, side - patch:], mic[:, :patch]
    pack[1] = jnp.where(lane_half, pltpu.roll(outer[:middle], guard, 1), outer[middle:])
    pack[0] = jnp.where(lane_half, inner[:middle], pltpu.roll(inner[middle:], guard, 1))
    loads["tpl"].wait()

    pl.semaphore_wait(barrier, tiles - 1 + tiles * o)

    def halo_copy(place, peer):
        return pltpu.make_async_remote_copy(
            src_ref=pack.at[place], dst_ref=halo.at[1 - place], send_sem=halo_send.at[place],
            recv_sem=halo_recv.at[1 - place], device_id={"tile": peer}, device_id_type=MESH,
        )

    to_left = halo_copy(0, lax.rem(t + tiles - 1, tiles))
    to_right = halo_copy(1, lax.rem(t + 1, tiles))

    def tpl_copy(k):
        return pltpu.make_async_remote_copy(
            src_ref=stack.at[0], dst_ref=stack.at[k], send_sem=tpl_send.at[k],
            recv_sem=tpl_recv.at[k], device_id={"tile": partner(k)}, device_id_type=MESH,
        )

    @pl.when(t > 0)
    def _():
        to_left.start()

    @pl.when(t < tiles - 1)
    def _():
        to_right.start()

    for k in range(1, min(3, tiles)):
        tpl_copy(k).start()

    for name in ("ty", "iy", "ix", "mask"):
        loads[name].start()

    loads["tx"].wait()
    loads["tt"].wait()

    def spectra(first, many):
        value = stack[pl.ds(first, many), :patch, :].reshape(many * patch, patch)
        high, low = split(value)
        top = tx[:patch, :]
        half = dot(jnp.concatenate([high, low], axis=1), jnp.concatenate([top, top], axis=0))
        half = half + dot(high, tx[length:length + patch, :])
        high, low = split(half)

        def stacked(part):
            return jnp.concatenate(
                [
                    jnp.concatenate(
                        [part[j * patch:(j + 1) * patch, :patch], part[j * patch:(j + 1) * patch, patch:]],
                        axis=0,
                    )
                    for j in range(many)
                ],
                axis=1,
            )

        whole = left_table(tt, stacked(high), stacked(low))
        for j in range(many):
            spec[first + j] = whole[:, j * patch:(j + 1) * patch]

    spectra(0, 1)

    for k in range(3, tiles):
        tpl_copy(k).start()


    rolled = [pltpu.roll(mic[:, b * patch:(b + 1) * patch], guard, 1) for b in range(blocks)]
    lane = lax.broadcasted_iota(jnp.int32, (extent, patch), 1)
    ext[0] = rolled[0]
    for b in range(1, blocks):
        ext[b] = jnp.where(lane < guard, rolled[b - 1], rolled[b])
    ext[blocks] = rolled[blocks - 1]

    def receive(place):
        present = (t > 0) if place == 0 else (t < tiles - 1)

        @pl.when(present)
        def _():
            halo_copy(1 - place, t).wait_recv()

        @pl.when(jnp.logical_not(present))
        def _():
            halo[place] = jnp.zeros(halo.shape[1:], F32)

        got = halo[place]
        turned = pltpu.roll(got, guard, 1)
        near = lax.broadcasted_iota(jnp.int32, (middle, patch), 1) < guard
        edge = 0 if place == 0 else blocks
        if place == 0:
            ext[edge, :middle] = jnp.where(near, got, ext[edge, :middle])
            ext[edge, middle:] = jnp.where(near, turned, ext[edge, middle:])
        else:
            ext[edge, :middle] = jnp.where(near, ext[edge, :middle], turned)
            ext[edge, middle:] = jnp.where(near, ext[edge, middle:], got)

    def image_x(b):
        half = right_table(jnp.concatenate([ext[b], ext[b + 1]], axis=1), tx)
        for part, value in enumerate(split(half)):
            rows_spec[part, b, 0] = value[:, :patch]
            rows_spec[part, b, 1] = value[:, patch:]

    def image_y(a):
        rows = pl.ds(pl.multiple_of(a * patch, patch), length)

        def stacked(part):
            return jnp.concatenate(
                [
                    jnp.concatenate([rows_spec[part, b, 0, rows, :], rows_spec[part, b, 1, rows, :]], axis=0)
                    for b in range(blocks)
                ],
                axis=1,
            )

        whole = left_table(ty, stacked(0), stacked(1))
        for b in range(blocks):
            img[b] = whole[:, b * patch:(b + 1) * patch]

    def correlate(items):
        highs, lows = [], []
        for k, a, b in items:
            sr, si = spec[k, :length], spec[k, length:]
            ir, ii = img[b, :length], img[b, length:]
            cross = jnp.concatenate([ir * sr + ii * si, ii * sr - ir * si], axis=0)
            high, low = split(cross)
            highs.append(high)
            lows.append(low)
        mid = left_table(iy, jnp.concatenate(highs, axis=1), jnp.concatenate(lows, axis=1))
        pieces = jnp.concatenate(
            [
                jnp.concatenate(
                    [mid[:patch, i * patch:(i + 1) * patch], mid[patch:, i * patch:(i + 1) * patch]],
                    axis=1,
                )
                for i in range(len(items))
            ],
            axis=0,
        )
        final = right_wide(pieces, ix)
        for i, (k, a, b) in enumerate(items):
            scores[k, a, b] = final[i * patch:(i + 1) * patch] + stack[k, patch:, :][:1, :1]

    tpl_copy(1).wait_recv()
    spectra(1, 1)
    loads["ty"].wait()
    loads["ix"].wait()
    loads["iy"].wait()
    odd = lax.rem(t, 2)

    def column(i, carry):
        place = lax.rem(i + 1 + odd, 2)

        @pl.when(i == 1)
        def _():
            announce(ready, 0, o)

        @pl.when(place == 0)
        def _():
            receive(0)

        @pl.when(place == 1)
        def _():
            receive(1)

        image_x(place)
        return carry

    lax.fori_loop(0, 2, column, 0)

    def pairs(body):
        if tiles == 4:
            body(2)
        elif tiles > 4:
            def step(p, carry):
                body(2 * p)
                return carry

            lax.fori_loop(1, tiles // 2, step, 0)

    def own_lse(a, place):
        rows = pl.ds(pl.multiple_of(place * share, share), share)
        parts = []
        for b in range(blocks):
            top = scores[0, a, b, rows, :]
            for k in range(1, tiles):
                top = jnp.maximum(top, scores[k, a, b, rows, :])
            total = jnp.exp(scores[0, a, b, rows, :] - top)
            for k in range(1, tiles):
                total = total + jnp.exp(scores[k, a, b, rows, :] - top)
            parts.append(top + jnp.log(total))
        return jnp.concatenate(parts, axis=1)

    def lse_copy(k):
        return pltpu.make_async_remote_copy(
            src_ref=lse_out.at[k], dst_ref=lse_in.at[k], send_sem=lse_send.at[k],
            recv_sem=lse_recv.at[k], device_id={"orient": lax.rem(o + k, orients)},
            device_id_type=MESH,
        )

    relayed = orients == 4
    outer = lax.rem(o, 3) == 0
    held = 2 * o - 1
    part = share // 2

    def relay(h):
        rows = pl.ds(h * part, part)
        return pltpu.make_async_remote_copy(
            src_ref=lse_out.at[2, rows], dst_ref=relay_in.at[rows], send_sem=relay_sem.at[0, h],
            recv_sem=relay_sem.at[1, h], device_id={"orient": o + 1 - 2 * lax.rem(o, 2)},
            device_id_type=MESH,
        )

    def held_copy(h):
        rows = pl.ds(h * part, part)
        return pltpu.make_async_remote_copy(
            src_ref=lse_out.at[held, rows], dst_ref=lse_in.at[held, rows], send_sem=lse_send.at[held],
            recv_sem=lse_recv.at[held], device_id={"orient": lax.rem(o + held, orients)},
            device_id_type=MESH,
        )

    owners = patch // share
    home, seat = o // owners, lax.rem(o, owners)

    def far_spectra():
        for k in range(2, tiles):
            tpl_copy(k).wait_recv()
        pairs(lambda k: spectra(k, 2))

        @pl.when(o < orients - 1)
        def _():
            pl.semaphore_wait(ready, tiles * (orients - 1 - o))

    def cell(j, carry):
        first = lax.rem(j, tiles // 2) * 2
        a = lax.rem(home + 1 + j // (tiles // 2), blocks)

        @pl.when(first == 0)
        def _():
            image_y(a)

        @pl.when(j == 1)
        def _():
            far_spectra()

        correlate([(first + q, a, b) for q in range(2) for b in range(blocks)])

        @pl.when(first == tiles - 2)
        def _():
            far = jnp.where(a == home, 0, owners - 1)

            def send(gap, inner):
                place = lax.rem(seat + gap + far, owners)
                ahead = lax.rem(a * owners + place - o + orients, orients)
                lse_out[ahead] = own_lse(a, place)

                direct = ahead > 0
                if relayed:
                    direct = direct & jnp.where(outer, ahead != 2, ahead != held)

                    @pl.when(outer & (ahead == 2))
                    def _():
                        relay(0).start()
                        relay(1).start()

                @pl.when(direct)
                def _():
                    lse_copy(ahead).start()

                return inner

            lax.fori_loop(1, owners + 1, send, 0)

        return carry

    lax.fori_loop(0, blocks * (tiles // 2), cell, 0)

    if relayed:
        @pl.when(jnp.logical_not(outer))
        def _():
            for h in range(2):
                relay(h).wait_recv()
                rows = pl.ds(h * part, part)
                ours, theirs = lse_out[held, rows, :], relay_in[rows, :]
                most = jnp.maximum(ours, theirs)
                lse_out[held, rows, :] = most + jnp.log(jnp.exp(ours - most) + jnp.exp(theirs - most))
                held_copy(h).start()
            lse_in[2] = jnp.full(lse_in.shape[1:], -1e30, F32)

    loads["mask"].wait()
    mask_rows, mask_cols = mask.shape
    row_id = lax.broadcasted_iota(jnp.int32, (share, mask_rows), 0) + o * share
    pick = lax.broadcasted_iota(jnp.int32, (share, mask_rows), 1)
    low_edge = pick * MBLK
    rows_of = jnp.where((row_id >= low_edge) & (row_id < low_edge + MBLK), 1.0, 0.0).astype(F32)
    col_id = lax.broadcasted_iota(jnp.int32, (mask_cols, side), 1)
    col_edge = lax.broadcasted_iota(jnp.int32, (mask_cols, side), 0) * MBLK
    cols_of = jnp.where((col_id >= col_edge) & (col_id < col_edge + MBLK), 1.0, 0.0).astype(F32)
    unmasked = 1.0 - dot(dot(rows_of, mask[...].astype(F32)), cols_of)

    def whole_sum(value):
        return jnp.sum(jnp.sum(value, axis=0, keepdims=True), axis=1, keepdims=True)

    count = whole_sum(unmasked)
    um[...] = unmasked
    keep_um = pltpu.make_async_copy(um, um_any, keep_sem.at[0])
    keep_um.start()

    mine = lse_out[0]
    for k in range(1, orients):
        if relayed and k == 2:
            @pl.when(outer)
            def _():
                lse_copy(2).wait_recv()
        else:
            lse_copy(k).wait_recv()
    top = mine
    for k in range(1, orients):
        top = jnp.maximum(top, lse_in[k])
    total = jnp.exp(mine - top)
    for k in range(1, orients):
        total = total + jnp.exp(lse_in[k] - top)
    lse = top + jnp.log(total)

    sum_here = whole_sum(unmasked * lse)
    mean_here = sum_here / jnp.maximum(count, 1.0)
    deviation = lse - mean_here
    squares = whole_sum(unmasked * deviation * deviation)
    slot = lax.broadcasted_iota(jnp.int32, stats.shape, 1)
    stats[...] = jnp.where(
        slot == 0, count, jnp.where(slot == 1, sum_here, jnp.where(slot == 2, squares, 0.0))
    )

    me = t * orients + o

    def st_copy(place, slot):
        return pltpu.make_async_remote_copy(
            src_ref=stats, dst_ref=st_any.at[slot], send_sem=st_send.at[place],
            recv_sem=st_recv.at[slot],
            device_id={"tile": lax.rem(place, tiles), "orient": place // tiles},
            device_id_type=MESH,
        )

    def each_other(body, skip):
        def step(place, carry):
            @pl.when(place != skip)
            def _():
                body(place)

            return carry

        if unrolled:
            for place in range(everyone):
                step(place, 0)
        else:
            lax.fori_loop(0, everyone, step, 0)

    there = o * tiles + t
    each_other(lambda place: st_copy(place, me).start(), there)
    lse_in[0] = lse
    keep_lse = pltpu.make_async_copy(lse_in.at[0], lse_any, keep_sem.at[1])
    keep_lse.start()
    keep_st = pltpu.make_async_copy(stats, st_any.at[me], keep_sem.at[2])
    keep_st.start()

    @pl.when(t > 0)
    def _():
        to_left.wait_send()

    @pl.when(t < tiles - 1)
    def _():
        to_right.wait_send()

    for k in range(1, tiles):
        tpl_copy(k).wait_send()
    for k in range(1, orients):
        if relayed and k == 2:
            @pl.when(outer)
            def _():
                relay(0).wait_send()
                relay(1).wait_send()

            @pl.when(jnp.logical_not(outer))
            def _():
                lse_copy(2).wait_send()
        else:
            lse_copy(k).wait_send()
    each_other(lambda place: st_copy(place, me).wait_send(), there)
    each_other(lambda slot: st_copy(0, slot).wait_recv(), me)
    keep_um.wait()
    keep_lse.wait()
    keep_st.wait()


def finish(lse, unmasked, stats, out):
    table = stats[:, 0, :]
    counts, sums, sqs = table[:, 0:1], table[:, 1:2], table[:, 2:3]
    live = jnp.sum(counts, axis=0, keepdims=True)
    average = jnp.sum(sums, axis=0, keepdims=True) / live
    gap = sums / jnp.maximum(counts, 1.0) - average
    variance = jnp.sum(sqs + counts * gap * gap, axis=0, keepdims=True) / live
    out[...] = unmasked[...] * (lse[...] - average) / jnp.sqrt(variance + 1e-05)


def body(tiles, orients, micrograph, templates, orient_ids, log_weight, ice_mask):
    extent, side = micrograph.shape
    patch = templates.shape[2]
    share = side // orients
    blocks = side // patch
    everyone = tiles * orients
    anywhere = pl.BlockSpec(memory_space=pl.ANY)
    vmem = pltpu.VMEM
    dma = pltpu.SemaphoreType.DMA
    consts = [jnp.asarray(table) for table in tables(patch)]
    lse, unmasked, stats = pl.pallas_call(
        functools.partial(kernel, tiles, orients, patch // 2),
        out_shape=[
            jax.ShapeDtypeStruct((share, side), F32),
            jax.ShapeDtypeStruct((share, side), F32),
            jax.ShapeDtypeStruct((everyone, 1, 128), F32),
        ],
        in_specs=[anywhere] * (5 + len(consts)),
        out_specs=[anywhere] * 3,
        scratch_shapes=[
            vmem((extent, side), F32),
            vmem(orient_ids.shape, jnp.int32),
            vmem((1, log_weight.shape[0]), F32),
            vmem(ice_mask.shape, jnp.int32),
            *[vmem(table.shape, BF16) for table in consts],
            vmem((2, extent // 2, patch), F32),
            vmem((2, extent // 2, patch), F32),
            vmem((tiles, patch + 8, patch), F32),
            vmem((blocks + 1, extent, patch), F32),
            vmem((2, blocks, 2, extent, patch), BF16),
            vmem((blocks, 4 * patch, patch), F32),
            vmem((tiles, 4 * patch, patch), F32),
            vmem((tiles, blocks, blocks, patch, patch), F32),
            vmem((orients, share, side), F32),
            vmem((orients, share, side), F32),
            vmem((share, side), F32),
            vmem((1, 128), F32),
            vmem((share, side), F32),
            dma((5 + len(consts),)),
            pltpu.SemaphoreType.REGULAR,
            dma((3,)),
            dma((2, 2)),
            dma((2,)), dma((2,)),
            dma((tiles,)), dma((tiles,)),
            dma((orients,)), dma((orients,)),
            dma((everyone,)), dma((everyone,)),
        ],
        compiler_params=pltpu.CompilerParams(
            collective_id=0, has_side_effects=True, vmem_limit_bytes=56 * 1024 * 1024
        ),
    )(micrograph, templates, orient_ids, log_weight.reshape(1, -1), ice_mask, *consts)
    here = pl.BlockSpec(memory_space=pltpu.VMEM)
    return pl.pallas_call(
        finish,
        out_shape=jax.ShapeDtypeStruct((share, side), F32),
        in_specs=[here] * 3,
        out_specs=here,
        cost_estimate=pl.CostEstimate(flops=4 * share * side, bytes_accessed=12 * share * side, transcendentals=0),
    )(lse, unmasked, stats)


def solution(mesh):
    return jax.shard_map(
        functools.partial(body, mesh.shape["tile"], mesh.shape["orient"]),
        mesh=mesh,
        in_specs=(
            P("group", "tile"),
            P("orient", "tile", None, None),
            P("orient", "tile"),
            P(),
            P("group", "tile"),
        ),
        out_specs=P(("group", "orient"), "tile"),
        check_vma=False,
    )
```

```python
import functools
import math

import jax
import jax.numpy as jnp
import numpy as np
from jax import lax
from jax.experimental import pallas as pl
from jax.experimental.pallas import tpu as pltpu
from jax.sharding import PartitionSpec as P

MBLK = 16
F32 = jnp.float32
BF16 = jnp.bfloat16
MESH = pl.DeviceIdType.MESH


def halves(table, axis=0):
    table = table.astype(np.float32)
    high = table.astype(jnp.bfloat16)
    low = (table - high.astype(np.float32)).astype(jnp.bfloat16)
    return np.concatenate([high, low], axis=axis)


def tables(patch):
    length = 2 * patch
    n = np.arange(length)[:, None]
    k = np.arange(patch)[None, :]
    theta = 2 * math.pi * ((n * (2 * k + 1)) % (2 * length)) / (2 * length)
    tx = np.concatenate([np.cos(theta), -np.sin(theta)], axis=1)
    back = theta[:patch].T
    ix = np.concatenate([np.cos(back), -np.sin(back)], axis=0) * (2.0 / length)
    m = np.arange(length)
    phi = 2 * math.pi * ((m[:, None] * m[None, :]) % length) / length
    c, s = np.cos(phi), np.sin(phi)
    ty = np.block([[c, s], [-s, c]])
    cp, sp = c[:, :patch], s[:, :patch]
    tt = np.block([[cp, sp], [-sp, cp]])
    ci, si = c[:patch], s[:patch]
    iy = np.block([[ci, -si], [si, ci]]) / length
    return halves(tx), halves(ix, 1), halves(ty), halves(tt), halves(iy)


def split(value):
    high = value.astype(BF16)
    low = (value - high.astype(F32)).astype(BF16)
    return high, low


def dot(a, b):
    return jnp.dot(a, b, preferred_element_type=F32)


def left_table(table, high, low):
    rows = table.shape[0] // 2
    both = dot(table[...], high)
    return both[:rows] + both[rows:] + dot(table[:rows, :], low)


def right_table(value, table):
    depth = table.shape[0] // 2
    high, low = split(value)
    return dot(jnp.concatenate([high, high], axis=1), table[...]) + dot(low, table[:depth, :])


def right_wide(value, table):
    width = table.shape[1] // 2
    high, low = split(value)
    both = dot(high, table[...])
    return both[:, :width] + both[:, width:] + dot(low, table[:, :width])


def kernel(
    tiles, orients, guard,
    mic_any, tpl_any, ids_any, logw_any, mask_any, tx_any, ix_any, ty_any, tt_any, iy_any,
    lse_any, um_any, st_any,
    mic, ids, logw, mask, tx, ix, ty, tt, iy, pack, halo,
    stack, ext, rows_spec, img, spec, scores, lse_out, lse_in, relay_in, stats, um,
    load_sem, ready, keep_sem, relay_sem,
    halo_send, halo_recv, tpl_send, tpl_recv, lse_send, lse_recv, st_send, st_recv,
):
    t = lax.axis_index("tile")
    o = lax.axis_index("orient")
    everyone = tiles * orients
    extent, side = mic.shape
    patch = tpl_any.shape[2]
    length = 2 * patch
    blocks = side // patch
    share = lse_any.shape[0]
    unrolled = everyone <= 16

    def partner(k):
        if tiles & (tiles - 1):
            return lax.rem(t + k, tiles)
        bit, peer = 1, 0
        while bit < tiles:
            peer = peer + lax.rem(t // bit + k // bit, 2) * bit
            bit *= 2
        return peer

    barrier = pltpu.get_barrier_semaphore()

    def announce(semaphore, first, last):
        def step(place, carry):
            for k in range(tiles):
                pl.semaphore_signal(
                    semaphore, inc=1, device_id={"tile": partner(k), "orient": place},
                    device_id_type=MESH,
                )
            return carry

        lax.fori_loop(first, last, step, 0)

    for k in range(1, tiles):
        pl.semaphore_signal(barrier, inc=1, device_id={"tile": partner(k)}, device_id_type=MESH)
    announce(barrier, o + 1, orients)

    sources = (
        ("tpl", tpl_any.at[0, 0], stack.at[0, pl.ds(0, patch)]),
        ("mic", mic_any, mic),
        ("ids", ids_any, ids),
        ("logw", logw_any, logw),
        ("tx", tx_any, tx),
        ("tt", tt_any, tt),
        ("ty", ty_any, ty),
        ("iy", iy_any, iy),
        ("ix", ix_any, ix),
        ("mask", mask_any, mask),
    )
    loads = {
        name: pltpu.make_async_copy(source, target, load_sem.at[index])
        for index, (name, source, target) in enumerate(sources)
    }
    for name in ("tpl", "mic", "ids", "logw", "tx", "tt"):
        loads[name].start()

    loads["ids"].wait()
    loads["logw"].wait()
    known = lax.broadcasted_iota(jnp.int32, (1, logw.shape[1]), 1) == ids[...]
    weight_here = jnp.sum(jnp.where(known, logw[...], 0.0), axis=1, keepdims=True)
    stack[0, patch:, :] = jnp.broadcast_to(weight_here, (stack.shape[1] - patch, patch))

    loads["mic"].wait()
    middle = extent // 2
    lane_half = lax.broadcasted_iota(jnp.int32, (middle, patch), 1) < guard
    outer, inner = mic[:, side - patch:], mic[:, :patch]
    pack[1] = jnp.where(lane_half, pltpu.roll(outer[:middle], guard, 1), outer[middle:])
    pack[0] = jnp.where(lane_half, inner[:middle], pltpu.roll(inner[middle:], guard, 1))
    loads["tpl"].wait()

    pl.semaphore_wait(barrier, tiles - 1 + tiles * o)

    def halo_copy(place, peer):
        return pltpu.make_async_remote_copy(
            src_ref=pack.at[place], dst_ref=halo.at[1 - place], send_sem=halo_send.at[place],
            recv_sem=halo_recv.at[1 - place], device_id={"tile": peer}, device_id_type=MESH,
        )

    to_left = halo_copy(0, lax.rem(t + tiles - 1, tiles))
    to_right = halo_copy(1, lax.rem(t + 1, tiles))

    def tpl_copy(k):
        return pltpu.make_async_remote_copy(
            src_ref=stack.at[0], dst_ref=stack.at[k], send_sem=tpl_send.at[k],
            recv_sem=tpl_recv.at[k], device_id={"tile": partner(k)}, device_id_type=MESH,
        )

    @pl.when(t > 0)
    def _():
        to_left.start()

    @pl.when(t < tiles - 1)
    def _():
        to_right.start()

    for k in range(1, tiles):
        tpl_copy(k).start()

    for name in ("ty", "iy", "ix", "mask"):
        loads[name].start()

    loads["tx"].wait()
    loads["tt"].wait()

    def spectra(first, many):
        value = stack[pl.ds(first, many), :patch, :].reshape(many * patch, patch)
        high, low = split(value)
        top = tx[:patch, :]
        half = dot(jnp.concatenate([high, low], axis=1), jnp.concatenate([top, top], axis=0))
        half = half + dot(high, tx[length:length + patch, :])
        high, low = split(half)

        def stacked(part):
            return jnp.concatenate(
                [
                    jnp.concatenate(
                        [part[j * patch:(j + 1) * patch, :patch], part[j * patch:(j + 1) * patch, patch:]],
                        axis=0,
                    )
                    for j in range(many)
                ],
                axis=1,
            )

        whole = left_table(tt, stacked(high), stacked(low))
        for j in range(many):
            spec[first + j] = whole[:, j * patch:(j + 1) * patch]

    spectra(0, 1)

    rolled = [pltpu.roll(mic[:, b * patch:(b + 1) * patch], guard, 1) for b in range(blocks)]
    lane = lax.broadcasted_iota(jnp.int32, (extent, patch), 1)
    ext[0] = rolled[0]
    for b in range(1, blocks):
        ext[b] = jnp.where(lane < guard, rolled[b - 1], rolled[b])
    ext[blocks] = rolled[blocks - 1]

    def receive(place):
        present = (t > 0) if place == 0 else (t < tiles - 1)

        @pl.when(present)
        def _():
            halo_copy(1 - place, t).wait_recv()

        @pl.when(jnp.logical_not(present))
        def _():
            halo[place] = jnp.zeros(halo.shape[1:], F32)

        got = halo[place]
        turned = pltpu.roll(got, guard, 1)
        near = lax.broadcasted_iota(jnp.int32, (middle, patch), 1) < guard
        edge = 0 if place == 0 else blocks
        if place == 0:
            ext[edge, :middle] = jnp.where(near, got, ext[edge, :middle])
            ext[edge, middle:] = jnp.where(near, turned, ext[edge, middle:])
        else:
            ext[edge, :middle] = jnp.where(near, ext[edge, :middle], turned)
            ext[edge, middle:] = jnp.where(near, ext[edge, middle:], got)

    def image_x(b):
        half = right_table(jnp.concatenate([ext[b], ext[b + 1]], axis=1), tx)
        for part, value in enumerate(split(half)):
            rows_spec[part, b, 0] = value[:, :patch]
            rows_spec[part, b, 1] = value[:, patch:]

    def image_y(a):
        rows = pl.ds(pl.multiple_of(a * patch, patch), length)

        def stacked(part):
            return jnp.concatenate(
                [
                    jnp.concatenate([rows_spec[part, b, 0, rows, :], rows_spec[part, b, 1, rows, :]], axis=0)
                    for b in range(blocks)
                ],
                axis=1,
            )

        whole = left_table(ty, stacked(0), stacked(1))
        for b in range(blocks):
            img[b] = whole[:, b * patch:(b + 1) * patch]

    def correlate(items):
        highs, lows = [], []
        for k, a, b in items:
            sr, si = spec[k, :length], spec[k, length:]
            ir, ii = img[b, :length], img[b, length:]
            cross = jnp.concatenate([ir * sr + ii * si, ii * sr - ir * si], axis=0)
            high, low = split(cross)
            highs.append(high)
            lows.append(low)
        mid = left_table(iy, jnp.concatenate(highs, axis=1), jnp.concatenate(lows, axis=1))
        pieces = jnp.concatenate(
            [
                jnp.concatenate(
                    [mid[:patch, i * patch:(i + 1) * patch], mid[patch:, i * patch:(i + 1) * patch]],
                    axis=1,
                )
                for i in range(len(items))
            ],
            axis=0,
        )
        final = right_wide(pieces, ix)
        for i, (k, a, b) in enumerate(items):
            scores[k, a, b] = final[i * patch:(i + 1) * patch] + stack[k, patch:, :][:1, :1]

    tpl_copy(1).wait_recv()
    spectra(1, 1)
    loads["ty"].wait()
    loads["ix"].wait()
    loads["iy"].wait()
    odd = lax.rem(t, 2)

    def column(i, carry):
        place = lax.rem(i + 1 + odd, 2)

        @pl.when(i == 1)
        def _():
            announce(ready, 0, o)

        @pl.when(place == 0)
        def _():
            receive(0)

        @pl.when(place == 1)
        def _():
            receive(1)

        image_x(place)
        return carry

    lax.fori_loop(0, 2, column, 0)

    def pairs(body):
        if tiles == 4:
            body(2)
        elif tiles > 4:
            def step(p, carry):
                body(2 * p)
                return carry

            lax.fori_loop(1, tiles // 2, step, 0)

    def own_lse(a, place, h):
        rows = pl.ds(pl.multiple_of(place * share + h * part, 8), part)
        parts = []
        for b in range(blocks):
            top = scores[0, a, b, rows, :]
            for k in range(1, tiles):
                top = jnp.maximum(top, scores[k, a, b, rows, :])
            total = jnp.exp(scores[0, a, b, rows, :] - top)
            for k in range(1, tiles):
                total = total + jnp.exp(scores[k, a, b, rows, :] - top)
            parts.append(top + jnp.log(total))
        return jnp.concatenate(parts, axis=1)

    def lse_copy(k):
        return pltpu.make_async_remote_copy(
            src_ref=lse_out.at[k], dst_ref=lse_in.at[k], send_sem=lse_send.at[k],
            recv_sem=lse_recv.at[k], device_id={"orient": lax.rem(o + k, orients)},
            device_id_type=MESH,
        )

    relayed = orients == 4
    outer = lax.rem(o, 3) == 0
    held = 2 * o - 1
    part = share // 2

    def relay(h):
        rows = pl.ds(h * part, part)
        return pltpu.make_async_remote_copy(
            src_ref=lse_out.at[2, rows], dst_ref=relay_in.at[rows], send_sem=relay_sem.at[0, h],
            recv_sem=relay_sem.at[1, h], device_id={"orient": o + 1 - 2 * lax.rem(o, 2)},
            device_id_type=MESH,
        )

    def held_copy(h):
        rows = pl.ds(h * part, part)
        return pltpu.make_async_remote_copy(
            src_ref=lse_out.at[held, rows], dst_ref=lse_in.at[held, rows], send_sem=lse_send.at[held],
            recv_sem=lse_recv.at[held], device_id={"orient": lax.rem(o + held, orients)},
            device_id_type=MESH,
        )

    owners = patch // share
    home, seat = o // owners, lax.rem(o, owners)

    def far_spectra():
        for k in range(2, tiles):
            tpl_copy(k).wait_recv()
        pairs(lambda k: spectra(k, 2))

        @pl.when(o < orients - 1)
        def _():
            pl.semaphore_wait(ready, tiles * (orients - 1 - o))

    def cell(j, carry):
        first = lax.rem(j, tiles // 2) * 2
        a = lax.rem(home + 1 + j // (tiles // 2), blocks)

        @pl.when(first == 0)
        def _():
            image_y(a)

        @pl.when(j == 1)
        def _():
            far_spectra()

        correlate([(first + q, a, b) for q in range(2) for b in range(blocks)])

        @pl.when(first == tiles - 2)
        def _():
            far = jnp.where(a == home, 0, owners - 1)

            def send(gap, inner):
                place = lax.rem(seat + gap + far, owners)
                ahead = lax.rem(a * owners + place - o + orients, orients)
                for h in range(2):
                    lse_out[ahead, pl.ds(h * part, part), :] = own_lse(a, place, h)
                    if relayed:
                        @pl.when(outer & (ahead == 2))
                        def _():
                            relay(h).start()


                direct = ahead > 0
                if relayed:
                    direct = direct & jnp.where(outer, ahead != 2, ahead != held)

                @pl.when(direct)
                def _():
                    lse_copy(ahead).start()

                return inner

            lax.fori_loop(1, owners + 1, send, 0)

        return carry

    lax.fori_loop(0, blocks * (tiles // 2), cell, 0)

    if relayed:
        @pl.when(jnp.logical_not(outer))
        def _():
            for h in range(2):
                relay(h).wait_recv()
                rows = pl.ds(h * part, part)
                ours, theirs = lse_out[held, rows, :], relay_in[rows, :]
                most = jnp.maximum(ours, theirs)
                lse_out[held, rows, :] = most + jnp.log(jnp.exp(ours - most) + jnp.exp(theirs - most))
                held_copy(h).start()
            lse_in[2] = jnp.full(lse_in.shape[1:], -1e30, F32)

    loads["mask"].wait()
    mask_rows, mask_cols = mask.shape
    row_id = lax.broadcasted_iota(jnp.int32, (share, mask_rows), 0) + o * share
    pick = lax.broadcasted_iota(jnp.int32, (share, mask_rows), 1)
    low_edge = pick * MBLK
    rows_of = jnp.where((row_id >= low_edge) & (row_id < low_edge + MBLK), 1.0, 0.0).astype(F32)
    col_id = lax.broadcasted_iota(jnp.int32, (mask_cols, side), 1)
    col_edge = lax.broadcasted_iota(jnp.int32, (mask_cols, side), 0) * MBLK
    cols_of = jnp.where((col_id >= col_edge) & (col_id < col_edge + MBLK), 1.0, 0.0).astype(F32)
    unmasked = 1.0 - dot(dot(rows_of, mask[...].astype(F32)), cols_of)

    def whole_sum(value):
        return jnp.sum(jnp.sum(value, axis=0, keepdims=True), axis=1, keepdims=True)

    count = whole_sum(unmasked)
    um[...] = unmasked
    keep_um = pltpu.make_async_copy(um, um_any, keep_sem.at[0])
    keep_um.start()

    mine = lse_out[0]
    for k in range(1, orients):
        if relayed and k == 2:
            @pl.when(outer)
            def _():
                lse_copy(2).wait_recv()
        else:
            lse_copy(k).wait_recv()
    top = mine
    for k in range(1, orients):
        top = jnp.maximum(top, lse_in[k])
    total = jnp.exp(mine - top)
    for k in range(1, orients):
        total = total + jnp.exp(lse_in[k] - top)
    lse = top + jnp.log(total)

    sum_here = whole_sum(unmasked * lse)
    mean_here = sum_here / jnp.maximum(count, 1.0)
    deviation = lse - mean_here
    squares = whole_sum(unmasked * deviation * deviation)
    slot = lax.broadcasted_iota(jnp.int32, stats.shape, 1)
    stats[...] = jnp.where(
        slot == 0, count, jnp.where(slot == 1, sum_here, jnp.where(slot == 2, squares, 0.0))
    )

    me = t * orients + o

    def st_copy(place, slot):
        return pltpu.make_async_remote_copy(
            src_ref=stats, dst_ref=st_any.at[slot], send_sem=st_send.at[place],
            recv_sem=st_recv.at[slot],
            device_id={"tile": lax.rem(place, tiles), "orient": place // tiles},
            device_id_type=MESH,
        )

    def each_other(body, skip):
        def step(place, carry):
            @pl.when(place != skip)
            def _():
                body(place)

            return carry

        if unrolled:
            for place in range(everyone):
                step(place, 0)
        else:
            lax.fori_loop(0, everyone, step, 0)

    there = o * tiles + t
    each_other(lambda place: st_copy(place, me).start(), there)
    lse_in[0] = lse
    keep_lse = pltpu.make_async_copy(lse_in.at[0], lse_any, keep_sem.at[1])
    keep_lse.start()
    keep_st = pltpu.make_async_copy(stats, st_any.at[me], keep_sem.at[2])
    keep_st.start()

    @pl.when(t > 0)
    def _():
        to_left.wait_send()

    @pl.when(t < tiles - 1)
    def _():
        to_right.wait_send()

    for k in range(1, tiles):
        tpl_copy(k).wait_send()
    for k in range(1, orients):
        if relayed and k == 2:
            @pl.when(outer)
            def _():
                relay(0).wait_send()
                relay(1).wait_send()

            @pl.when(jnp.logical_not(outer))
            def _():
                lse_copy(2).wait_send()
        else:
            lse_copy(k).wait_send()
    each_other(lambda place: st_copy(place, me).wait_send(), there)
    each_other(lambda slot: st_copy(0, slot).wait_recv(), me)
    keep_um.wait()
    keep_lse.wait()
    keep_st.wait()


def finish(lse, unmasked, stats, out):
    table = stats[:, 0, :]
    counts, sums, sqs = table[:, 0:1], table[:, 1:2], table[:, 2:3]
    live = jnp.sum(counts, axis=0, keepdims=True)
    average = jnp.sum(sums, axis=0, keepdims=True) / live
    gap = sums / jnp.maximum(counts, 1.0) - average
    variance = jnp.sum(sqs + counts * gap * gap, axis=0, keepdims=True) / live
    out[...] = unmasked[...] * (lse[...] - average) / jnp.sqrt(variance + 1e-05)


def body(tiles, orients, micrograph, templates, orient_ids, log_weight, ice_mask):
    extent, side = micrograph.shape
    patch = templates.shape[2]
    share = side // orients
    blocks = side // patch
    everyone = tiles * orients
    anywhere = pl.BlockSpec(memory_space=pl.ANY)
    vmem = pltpu.VMEM
    dma = pltpu.SemaphoreType.DMA
    consts = [jnp.asarray(table) for table in tables(patch)]
    lse, unmasked, stats = pl.pallas_call(
        functools.partial(kernel, tiles, orients, patch // 2),
        out_shape=[
            jax.ShapeDtypeStruct((share, side), F32),
            jax.ShapeDtypeStruct((share, side), F32),
            jax.ShapeDtypeStruct((everyone, 1, 128), F32),
        ],
        in_specs=[anywhere] * (5 + len(consts)),
        out_specs=[anywhere] * 3,
        scratch_shapes=[
            vmem((extent, side), F32),
            vmem(orient_ids.shape, jnp.int32),
            vmem((1, log_weight.shape[0]), F32),
            vmem(ice_mask.shape, jnp.int32),
            *[vmem(table.shape, BF16) for table in consts],
            vmem((2, extent // 2, patch), F32),
            vmem((2, extent // 2, patch), F32),
            vmem((tiles, patch + 8, patch), F32),
            vmem((blocks + 1, extent, patch), F32),
            vmem((2, blocks, 2, extent, patch), BF16),
            vmem((blocks, 4 * patch, patch), F32),
            vmem((tiles, 4 * patch, patch), F32),
            vmem((tiles, blocks, blocks, patch, patch), F32),
            vmem((orients, share, side), F32),
            vmem((orients, share, side), F32),
            vmem((share, side), F32),
            vmem((1, 128), F32),
            vmem((share, side), F32),
            dma((5 + len(consts),)),
            pltpu.SemaphoreType.REGULAR,
            dma((3,)),
            dma((2, 2)),
            dma((2,)), dma((2,)),
            dma((tiles,)), dma((tiles,)),
            dma((orients,)), dma((orients,)),
            dma((everyone,)), dma((everyone,)),
        ],
        compiler_params=pltpu.CompilerParams(
            collective_id=0, has_side_effects=True, vmem_limit_bytes=56 * 1024 * 1024
        ),
    )(micrograph, templates, orient_ids, log_weight.reshape(1, -1), ice_mask, *consts)
    here = pl.BlockSpec(memory_space=pltpu.VMEM)
    return pl.pallas_call(
        finish,
        out_shape=jax.ShapeDtypeStruct((share, side), F32),
        in_specs=[here] * 3,
        out_specs=here,
        cost_estimate=pl.CostEstimate(flops=4 * share * side, bytes_accessed=12 * share * side, transcendentals=0),
    )(lse, unmasked, stats)


def solution(mesh):
    return jax.shard_map(
        functools.partial(body, mesh.shape["tile"], mesh.shape["orient"]),
        mesh=mesh,
        in_specs=(
            P("group", "tile"),
            P("orient", "tile", None, None),
            P("orient", "tile"),
            P(),
            P("group", "tile"),
        ),
        out_specs=P(("group", "orient"), "tile"),
        check_vma=False,
    )
```
